32 devices in a mesh: section: 2 (over core), dp: 16 (over z, y, x).
Axes of the slice: x: 2, y: 2, z: 4, core: 2. Of those that a mesh axis runs over, the one named last changes fastest.
Arguments:
- boundary_in: bfloat16 [2, 2, 16, 512, 1024], P('section', None, 'dp'), may hold values from -6 to 6
- segments: int32 [2, 16, 512], P(None, 'dp'), may hold values from 0 to 7, never falling along the last dimension, each value on 1 to 128 neighbouring positions
- routed: int32 [2, 16, 64], P(None, 'dp'), may hold values from 0 to 511, as said below
- gain_attn: float32 [2, 1024], P('section', 'dp'), may hold values from 0.5 to 1.5
- w_qkv: float32 [2, 1024, 3072], P('section', 'dp'), may hold values from -0.1875 to 0.1875
- w_out: float32 [2, 1024, 1024], P('section', 'dp'), may hold values from -0.75 to 0.75
- gain_mlp: float32 [2, 1024], P('section', 'dp'), may hold values from 0.5 to 1.5
- w_up: float32 [2, 1024, 4096], P('section', 'dp'), may hold values from -0.1875 to 0.1875
- b_up: float32 [2, 4096], P('section', 'dp'), may hold values from -1.8 to 1.8
- w_down: float32 [2, 4096, 1024], P('section', 'dp'), may hold values from -0.09375 to 0.09375
- b_down: float32 [2, 1024], P('section', 'dp'), may hold values from -1.8 to 1.8
- router: float32 [1024], P(('section', 'dp')), may hold values from -0.1875 to 0.1875
Outputs:
- boundary_out: bfloat16 [2, 2, 16, 512, 1024], P('section', None, 'dp')
- grad_gain_attn: float32 [2, 1024], P('section', 'dp')
- grad_w_qkv: float32 [2, 1024, 3072], P('section', 'dp')
- grad_w_out: float32 [2, 1024, 1024], P('section', 'dp')
- grad_gain_mlp: float32 [2, 1024], P('section', 'dp')
- grad_w_up: float32 [2, 1024, 4096], P('section', 'dp')
- grad_b_up: float32 [2, 4096], P('section', 'dp')
- grad_w_down: float32 [2, 4096, 1024], P('section', 'dp')
- grad_b_down: float32 [2, 1024], P('section', 'dp')
- grad_router: float32 [1024], P(('section', 'dp'))
The draws below stay inside these ranges and needn't reach their ends.
Inputs may be any that keep to these rules, and one draw needn't show every extreme that they name: `routed`: each row holds 64 distinct positions of its sequence in increasing order.
All inputs are finite; a program needn't handle non-finite values.
Results may differ from the reference program's by a relative error of at most 0.013.
The reference program's roundings to bfloat16 on the way count: a program that leaves them out, or rounds other values in their place, can miss the bound.
Values may be sent and summed in bfloat16 or wider, within the bound.
No kernel may reach another device: no remote copies, remote signals or barrier semaphores. Data moves between devices by JAX's collectives and lax.ppermute only.
A program may use at most 576 MiB of HBM per device.

```python
import math
import jax
import jax.numpy as jnp
import numpy as np
from jax import lax

D = 1024
HEADS = 16
HEAD_DIM = 64
FF = 4096
LEN = 512
MB = 2
K = 64
SEQS = 16


def draw_routed(key, part):
    row_keys = jax.random.split(key, MB * SEQS)

    def choose(single_key):
        shuffled = jax.random.permutation(single_key, LEN)
        return jnp.sort(shuffled[:K])
    return jax.vmap(choose)(row_keys).reshape(MB, SEQS, K).astype(jnp.int32)


def with_spikes(result, rng, source, target, blocks, factor):
    owner, partner = [(jnp.arange(result.shape[axis_at]) // (result.shape[axis_at] // blocks)).reshape([-1 if axis == axis_at else 1 for axis in range(result.ndim)]) for axis_at in (source, target)]
    chosen = jax.random.permutation(rng, blocks)[partner]
    strong = (owner == chosen) | (owner == (partner + blocks // 2) % blocks)
    return jnp.where(strong, factor * result, result)


def shard_levels(stream_key, dims, shards, low, largest):
    def one(axis_at, parts):
        heights = jax.random.uniform(jax.random.fold_in(jax.random.fold_in(stream_key, 6), axis_at), (parts,), jnp.float32, low / len(shards), largest / len(shards))
        return jnp.repeat(jnp.exp(heights), dims[axis_at] // parts).reshape((-1,) + (1,) * (len(dims) - axis_at - 1))

    loudness = one(*shards[0])
    for cut in shards[1:]:
        loudness = loudness * one(*cut)
    return loudness


def split_up(amount, total, bound, skew):
    portions = [(1 << 20) // math.isqrt(rank ** skew) + 1 for rank in range(2, amount + 1)]
    spare, given = total - bound - (amount - 1), [1] * (amount - 1)
    while spare > 0:
        candidates = [i for i in range(amount - 1) if given[i] < bound]
        whole, budget = sum([portions[i] for i in candidates]), spare
        for i in candidates:
            extra = min(bound - given[i], max(1, budget * portions[i] // whole), spare)
            given[i] = given[i] + extra
            spare = spare - extra
    return np.array([bound] + given)


def ragged_sizes(stream_key, number_of, total, limit, lean):
    if number_of == 2:
        one = jax.random.randint(stream_key, (), max(1, total - limit), min(limit, total - 1) + 1)
        return jnp.stack([one, total - one])
    tallies = jnp.asarray(split_up(number_of, total, limit, lean), jnp.int32)
    couples = (number_of - 1) // 2
    donor, receiver = tallies[1:1 + 2 * couples:2], tallies[2:2 + 2 * couples:2]
    slack = jnp.minimum(donor - 1, limit - receiver)
    shifted = jax.random.randint(jax.random.fold_in(stream_key, 1), (couples,), 0, 1 << 20) % (slack + 1)
    tallies = tallies.at[1:1 + 2 * couples:2].set(donor - shifted).at[2:2 + 2 * couples:2].set(receiver + shifted)
    return tallies[jax.random.permutation(jax.random.fold_in(stream_key, 2), number_of)]


def normal_values(own_key, shape, deviation, most, cuts=(), kind=jnp.bfloat16):
    level = shard_levels(own_key, shape, cuts, -0.22, 0.18) if cuts else 1.0
    values = jax.random.normal(own_key, shape, jnp.float32) * deviation * level
    return jnp.minimum(jnp.maximum(values, -most), most).astype(kind)


def gaussian_with(stream_key, extent, width, most, shards, heavy, held_as=jnp.bfloat16):
    values = width * jax.random.normal(stream_key, extent, jnp.float32)
    if shards:
        values = values * shard_levels(stream_key, extent, shards, -0.22, 0.18)
    return jnp.clip(with_spikes(values, jax.random.fold_in(stream_key, 3), *heavy), -most, most).astype(held_as)


def setup_inputs(seed: int = 0) -> dict:
    streams_of = jax.random.split(jax.random.key(seed), 13)
    boundary_in = gaussian_with(streams_of[0], (2, MB, SEQS, LEN, D), 1.0, 6.0, ((0, 2), (2, 16)), (2, 4, 16, 2.0))
    segments = jax.vmap(lambda own: jnp.searchsorted(jnp.cumsum(ragged_sizes(own, 8, LEN, LEN // 4, 2)), jnp.arange(LEN), side="right"))(jax.random.split(streams_of[1], MB * SEQS)).reshape((MB, SEQS, LEN)).astype(jnp.int32)
    routed = draw_routed(jax.random.fold_in(streams_of[12], 71), 0)
    gain_attn = jnp.clip(1.0 + 0.1 * jax.random.normal(streams_of[3], (2, D), jnp.float32), 0.5, 1.5)
    w_qkv = normal_values(streams_of[4], (2, D, 3 * D), D ** -0.5, 0.1875, ((0, 2), (1, 16)), jnp.float32)
    w_out = normal_values(streams_of[5], (2, D, D), (D // 16) ** -0.5, 0.75, ((0, 2), (1, 16)), jnp.float32)
    gain_mlp = jnp.clip(1.0 + 0.1 * jax.random.normal(streams_of[6], (2, D), jnp.float32), 0.5, 1.5)
    w_up = normal_values(streams_of[7], (2, D, FF), D ** -0.5, 0.1875, ((0, 2), (1, 16)), jnp.float32)
    b_up = normal_values(streams_of[8], (2, FF), 0.3, 1.8, ((0, 2), (1, 16)), jnp.float32)
    w_down = normal_values(streams_of[9], (2, FF, D), FF ** -0.5, 0.09375, ((0, 2), (1, 16)), jnp.float32)
    b_down = normal_values(streams_of[10], (2, D), 0.3, 1.8, ((0, 2), (1, 16)), jnp.float32)
    router = normal_values(streams_of[11], (D,), D ** -0.5, 0.1875, ((0, 32),), jnp.float32)
    return {"boundary_in": boundary_in, "segments": segments, "routed": routed, "gain_attn": gain_attn, "w_qkv": w_qkv, "w_out": w_out, "gain_mlp": gain_mlp, "w_up": w_up, "b_up": b_up, "w_down": w_down, "b_down": b_down, "router": router}


epsilon = 1e-06
masked_score = -1e+30
root_half = 0.7071067811865476
highest = lax.Precision.HIGHEST

@jax.custom_vjp
def low(v):
    return lax.optimization_barrier(v.astype(jnp.bfloat16)).astype(jnp.float32)

@jax.custom_vjp
def low_back(v):
    return v

def low_keep(v):
    return (low(v), None)

def low_pass(kept, grad):
    return (grad,)

def back_keep(v):
    return (v, None)

def back_low(kept, grad):
    return (low(grad),)
low.defvjp(low_keep, low_pass)
low_back.defvjp(back_keep, back_low)

def product(left_side, right_side):
    return jnp.dot(left_side, right_side, preferred_element_type=jnp.float32, precision=highest)

def rms_scaled(values, gain):
    return values * lax.rsqrt(lax.optimization_barrier(jnp.mean(values * values, axis=-1, keepdims=True)) + epsilon) * gain

def block(residual, segment_ids, positions, params):
    gain_attn, w_qkv, w_out, gain_mlp, w_up, b_up, w_down, b_down = params
    row_count = residual.shape[0]
    normed = low(rms_scaled(residual, gain_attn))
    qkv = low(low_back(product(normed, w_qkv)))
    queries = qkv[:, :D].reshape(row_count, HEADS, HEAD_DIM)
    key_heads = qkv[:, D:2 * D].reshape(row_count, HEADS, HEAD_DIM)
    value_heads = qkv[:, 2 * D:].reshape(row_count, HEADS, HEAD_DIM)
    scores = low_back(jnp.einsum('qhd,khd->hqk', queries, key_heads, precision=highest) * HEAD_DIM ** (-0.5))
    allowed = (segment_ids[:, None] == segment_ids[None, :]) & (positions[:, None] >= positions[None, :])
    scores = jnp.where(allowed[None], scores, masked_score)
    exponent = jnp.exp(scores - lax.optimization_barrier(jnp.max(scores, axis=-1, keepdims=True)))
    probs = low(exponent / lax.optimization_barrier(jnp.sum(exponent, axis=-1, keepdims=True)))
    attended = jnp.einsum('hqk,khd->qhd', probs, value_heads, precision=highest).reshape(row_count, D)
    attended = low(low_back(attended))
    mixed_attn = low_back(product(attended, w_out))
    hidden = residual + mixed_attn
    normed_mlp = low(rms_scaled(hidden, gain_mlp))
    up_proj = low_back(product(normed_mlp, w_up) + b_up)
    active = low(0.5 * up_proj * (1.0 + lax.erf(up_proj * root_half)))
    down_proj = low_back(product(active, w_down) + b_down)
    return (hidden, mixed_attn, down_proj)

def sequence(first_params, second_params, router_w, residual, segment_ids, picked):
    positions = jnp.arange(LEN, dtype=jnp.int32)
    hidden, mixed_attn, down_proj = block(residual, segment_ids, positions, first_params)
    passed = low(low_back(hidden + down_proj))
    chosen = jnp.take(passed, picked, axis=0)
    chosen_ids = jnp.take(segment_ids, picked, axis=0)
    router_weight = jax.nn.sigmoid(jnp.dot(chosen, router_w, precision=highest))
    unused, mixed_two, down_two = block(chosen, chosen_ids, picked, second_params)
    return passed.at[picked].add(router_weight[:, None] * (mixed_two + down_two))

def reference(boundary_in, segments, routed, gain_attn, w_qkv, w_out, gain_mlp, w_up, b_up, w_down, b_down, router):
    flat = boundary_in.astype(jnp.float32).reshape(2, MB * SEQS, LEN, D)
    inputs = flat[0]
    cotangent = flat[1]
    segment_rows = segments.reshape(MB * SEQS, LEN)
    picked_rows = routed.reshape(MB * SEQS, K)
    params = (gain_attn, w_qkv, w_out, gain_mlp, w_up, b_up, w_down, b_down)

    def forward(params_all, router_w, inputs_all):
        rounded = tuple((low(param_one) for param_one in params_all))
        first_params = tuple((param_one[0] for param_one in rounded))
        second_params = tuple((param_one[1] for param_one in rounded))
        router_low = low(router_w)

        def single(entries):
            return sequence(first_params, second_params, router_low, entries[0], entries[1], entries[2])
        return lax.map(jax.checkpoint(single), (inputs_all, segment_rows, picked_rows))
    outputs, pullback = jax.vjp(forward, params, router, inputs)
    grad_params, grad_router, grad_inputs = pullback(cotangent)
    boundary_out = jnp.stack([grad_inputs, outputs]).reshape(2, MB, SEQS, LEN, D).astype(jnp.bfloat16)
    return (boundary_out, grad_params[0], grad_params[1], grad_params[2], grad_params[3], grad_params[4], grad_params[5], grad_params[6], grad_params[7], grad_router)
```

```python
import functools

import jax
import jax.numpy as jnp
from jax import lax
from jax.experimental import pallas as pl
from jax.experimental.pallas import tpu as pltpu
from jax.sharding import Mesh
from jax.sharding import PartitionSpec as P

D = 1024
HEADS = 16
HEAD_DIM = 64
FF = 4096
HALF = D // 2
LANES = 128

epsilon = 1e-06
masked_score = -1e30
root_half = 0.7071067811865476
inverse_root_two_pi = 0.3989422804014327

f32 = jnp.float32
bf16 = jnp.bfloat16


def mm(a, b):
    return jnp.dot(a, b, preferred_element_type=f32)


def mm_rows(a, b):
    return lax.dot_general(a, b, (((0,), (0,)), ((), ())), preferred_element_type=f32)


def mm_t(a, b):
    return lax.dot_general(a, b, (((1,), (1,)), ((), ())), preferred_element_type=f32)


def gelu_value(u):
    return 0.5 * u * (1.0 + lax.erf(u * root_half))


def gelu_slope(u):
    return 0.5 * (1.0 + lax.erf(u * root_half)) + u * jnp.exp(-0.5 * u * u) * inverse_root_two_pi


def swap(v, axis):
    return lax.ppermute(v, axis, [(0, 1), (1, 0)])


def to_plane(v, j):
    return lax.ppermute(v, ("y", "x"), [(i, i ^ j) for i in range(4)])


def place_kernel(splits, me_ref, own, px, py, pd, *rest):
    outs, sems = rest[: len(splits)], rest[len(splits)]
    me = me_ref[0]
    copies = []
    for j, src in enumerate((own, px, py, pd)):
        for k, (low, high) in enumerate(splits):
            copies.append(
                pltpu.make_async_copy(
                    src.at[:, :, low:high], outs[k].at[:, me ^ j], sems.at[j * len(splits) + k]
                )
            )
    for copy in copies:
        copy.start()
    for copy in copies:
        copy.wait()


def place(me, pieces, splits):
    depth, rows, _ = pieces[0].shape
    return pl.pallas_call(
        functools.partial(place_kernel, splits),
        out_shape=[
            jax.ShapeDtypeStruct((depth, 4, rows, high - low), pieces[0].dtype)
            for low, high in splits
        ],
        in_specs=[pl.BlockSpec(memory_space=pltpu.SMEM)] + [pl.BlockSpec(memory_space=pl.ANY)] * 4,
        out_specs=[pl.BlockSpec(memory_space=pltpu.VMEM)] * len(splits),
        scratch_shapes=[pltpu.SemaphoreType.DMA((4 * len(splits),))],
        compiler_params=pltpu.CompilerParams(vmem_limit_bytes=24 << 20),
        cost_estimate=pl.CostEstimate(
            flops=0, bytes_accessed=8 * pieces[0].size * 2, transcendentals=0
        ),
    )(jnp.reshape(me, (1,)), *pieces)


def after(v, other):
    return lax.optimization_barrier((v, other))[0]


def gather_pieces(shard, diagonal_by):
    own = lax.all_gather(shard, "z", axis=0, tiled=False)
    px = swap(own, "x")
    py = swap(own, "y")
    pd = swap(px, "y") if diagonal_by == "y" else swap(py, "x")
    return own, px, py, pd


def reduce_plane(grads, me, diagonal_by):
    def part(j):
        return lax.dynamic_index_in_dim(grads, me ^ j, axis=1, keepdims=False)

    first, second = ("x", "y") if diagonal_by == "y" else ("y", "x")
    near, far = (1, 2) if diagonal_by == "y" else (2, 1)
    across = swap(part(3), second)
    joined = (part(near).astype(f32) + across.astype(f32)).astype(grads.dtype)
    from_near = swap(joined, first)
    from_far = swap(part(far), second)
    return (part(0).astype(f32) + from_near.astype(f32) + from_far.astype(f32)).astype(grads.dtype)


def reduce_z(part):
    return lax.psum_scatter(part, "z", scatter_dimension=0, tiled=False)


def masks_of(seg_col, seg_row, i, block, low):
    width = (i + 1) * block - low
    rows = i * block + lax.broadcasted_iota(jnp.int32, (block, width), 0)
    columns = low + lax.broadcasted_iota(jnp.int32, (block, width), 1)
    same = seg_col[i * block : (i + 1) * block] == seg_row[:, low : (i + 1) * block]
    return same & (rows >= columns)


def head_lanes(h):
    lane = lax.broadcasted_iota(jnp.int32, (1, LANES), 1)
    return (lane // HEAD_DIM == h).astype(bf16)


def softmax_block(q, k, allowed):
    scores = mm_t(q, k)
    scores = jnp.where(allowed, scores, masked_score)
    top = jnp.max(scores, axis=-1, keepdims=True)
    exponent = jnp.exp(scores - top)
    return exponent / jnp.sum(exponent, axis=-1, keepdims=True)


def attend_kernel(block, q_ref, k_ref, v_ref, seg_col_ref, seg_row_ref, o_ref):
    length = q_ref.shape[0]
    seg_col, seg_row = seg_col_ref[0], seg_row_ref[0]
    for i in range(length // block):
        low = max(0, i - 1) * block
        high = (i + 1) * block
        allowed = masks_of(seg_col, seg_row, i, block, low)
        k, v = k_ref[low:high], v_ref[low:high]
        q = q_ref[i * block : high] * jnp.asarray(HEAD_DIM**-0.5, bf16)
        total = None
        for h in range(2):
            lanes = head_lanes(h)
            probs = softmax_block(q * lanes, k, allowed).astype(bf16)
            term = mm(probs, v * lanes)
            total = term if total is None else total + term
        o_ref[i * block : high] = total.astype(bf16)


def attend_back_kernel(
    block, q_ref, k_ref, v_ref, seg_col_ref, seg_row_ref, g_ref, dq_ref, dk_ref, dv_ref, dk_acc, dv_acc
):
    length = q_ref.shape[0]
    seg_col, seg_row = seg_col_ref[0], seg_row_ref[0]
    scale = jnp.asarray(HEAD_DIM**-0.5, bf16)
    dk_acc[...] = jnp.zeros_like(dk_acc)
    dv_acc[...] = jnp.zeros_like(dv_acc)
    for i in range(length // block):
        low = max(0, i - 1) * block
        high = (i + 1) * block
        allowed = masks_of(seg_col, seg_row, i, block, low)
        k, v = k_ref[low:high], v_ref[low:high]
        q = q_ref[i * block : high] * scale
        g = g_ref[i * block : high]
        dq = None
        for h in range(2):
            lanes = head_lanes(h)
            qh, gh = q * lanes, g * lanes
            probs = softmax_block(qh, k, allowed)
            dp = mm_t(gh, v)
            dv_acc[low:high] += mm_rows(probs.astype(bf16), gh)
            inner = jnp.sum(dp * probs, axis=-1, keepdims=True)
            ds = (probs * (dp - inner)).astype(bf16)
            term = mm(ds, k * (lanes * scale))
            dq = term if dq is None else dq + term
            dk_acc[low:high] += mm_rows(ds, qh)
        dq_ref[i * block : high] = dq.astype(bf16)
    dk_ref[...] = dk_acc[...].astype(bf16)
    dv_ref[...] = dv_acc[...].astype(bf16)


def attention_specs(length, pairs):
    def at(base):
        return pl.BlockSpec((length, LANES), lambda s, p: (s, base + p))

    return (
        [at(0), at(pairs), at(2 * pairs)]
        + [
            pl.BlockSpec((1, length, 1), lambda s, p: (s, 0, 0)),
            pl.BlockSpec((1, 1, length), lambda s, p: (s, 0, 0)),
        ],
        at(0),
    )


def attend(qkv, seg, block):
    count, length = seg.shape
    pairs = qkv.shape[1] // (3 * LANES)
    in_specs, one = attention_specs(length, pairs)
    work = count * pairs * 2 * length * 2 * block
    return pl.pallas_call(
        functools.partial(attend_kernel, block),
        grid=(count, pairs),
        out_shape=jax.ShapeDtypeStruct((count * length, pairs * LANES), bf16),
        in_specs=in_specs,
        out_specs=one,
        cost_estimate=pl.CostEstimate(
            flops=work * 4 * LANES, bytes_accessed=qkv.size * 3, transcendentals=work
        ),
    )(qkv, qkv, qkv, seg[:, :, None], seg[:, None, :])


def attend_back(qkv, seg, grad, block):
    count, length = seg.shape
    pairs = qkv.shape[1] // (3 * LANES)
    in_specs, one = attention_specs(length, pairs)
    work = count * pairs * 2 * length * 2 * block
    like = jax.ShapeDtypeStruct((count * length, pairs * LANES), bf16)
    parts = pl.pallas_call(
        functools.partial(attend_back_kernel, block),
        grid=(count, pairs),
        out_shape=[like] * 3,
        in_specs=in_specs + [one],
        out_specs=[one] * 3,
        scratch_shapes=[pltpu.VMEM((length, LANES), f32)] * 2,
        cost_estimate=pl.CostEstimate(
            flops=work * 10 * LANES, bytes_accessed=qkv.size * 5, transcendentals=work
        ),
    )(qkv, qkv, qkv, seg[:, :, None], seg[:, None, :], grad)
    return jnp.concatenate(parts, axis=1)


def inverse_rms(v):
    return lax.rsqrt(jnp.mean(v * v, axis=-1, keepdims=True) + epsilon)


def norm_back(grad, unit, inverse, gain):
    scaled = grad * gain
    return inverse * (scaled - unit * jnp.mean(scaled * unit, axis=-1, keepdims=True))


def shards(
    boundary_in,
    segments,
    routed,
    gain_attn,
    w_qkv,
    w_out,
    gain_mlp,
    w_up,
    b_up,
    w_down,
    b_down,
    router,
):
    core = lax.axis_index("section")
    first = core == 0
    me = 2 * lax.axis_index("y") + lax.axis_index("x")
    depth = lax.axis_size("z")
    rows = w_qkv.shape[1]
    dp = 4 * depth
    units = w_up.shape[2] // dp
    half_units = units // 2
    micro, length = boundary_in.shape[1], boundary_in.shape[3]
    tokens = micro * length

    qkv_halves = w_qkv[0].astype(bf16).reshape(rows, 3, 2, HALF)
    out_halves = w_out[0].astype(bf16).reshape(rows, 2, HALF)
    up_halves = w_up[0].astype(bf16).reshape(rows, dp, 2, half_units)
    down_halves = w_down[0].astype(bf16).reshape(2, half_units, D)
    bias_halves = b_up[0].astype(bf16).reshape(2, half_units // rows, rows)
    column = lambda v: jnp.pad(v.astype(bf16), (0, rows - v.shape[0]))[:, None]
    small = jnp.concatenate(
        [column(gain_attn[0]), column(gain_mlp[0]), column(b_down[0]), column(router)], axis=1
    )
    bias_cols = half_units // rows

    def half(h):
        pick = lambda v, axis: lax.dynamic_index_in_dim(v, h, axis=axis, keepdims=False)
        extra = jnp.concatenate([small, pick(bias_halves, 0).T], axis=1)
        extra = jnp.pad(extra, ((0, 0), (0, LANES - extra.shape[1])))
        attn = jnp.concatenate(
            [pick(qkv_halves, 2).reshape(rows, 3 * HALF), pick(out_halves, 1), extra], axis=1
        )
        return attn, pick(up_halves, 2).reshape(rows, D * 2), pick(down_halves, 0)

    kept, sent = half(core), half(1 - core)
    came = tuple(swap(v, "section") for v in sent)
    shard0 = tuple(jnp.where(first, k, r) for k, r in zip(kept, came))
    shard1 = tuple(jnp.where(first, r, k) for k, r in zip(kept, came))

    mine = boundary_in[0, :, 0].reshape(tokens, D)
    other = swap(mine, "section")
    x_b = jnp.where(first, mine, other)
    cot_b = jnp.where(first, other, mine)
    seg = segments[:, 0]
    picked = routed[:, 0]
    count = picked.shape[1]
    chosen_rows = micro * count

    def attention_weights(shard, by):
        pieces = gather_pieces(shard, by)
        w_q, w_o, extra = place(
            me, pieces, ((0, 3 * HALF), (3 * HALF, 4 * HALF), (4 * HALF, 4 * HALF + LANES))
        )
        w_o = w_o.reshape(D, HALF)
        own = lax.dynamic_slice_in_dim(w_o, core * HALF, HALF, axis=0)
        recv = swap(lax.dynamic_slice_in_dim(w_o, (1 - core) * HALF, HALF, axis=0), "section")
        w_o = jnp.concatenate([jnp.where(first, own, recv), jnp.where(first, recv, own)], axis=1)
        extra = extra.reshape(D, LANES)
        choose = (
            lax.broadcasted_iota(jnp.int32, (8, LANES), 0)
            == lax.broadcasted_iota(jnp.int32, (8, LANES), 1)
        ).astype(bf16)
        vectors = mm_t(choose, extra)
        bias = vectors[4 : 4 + bias_cols].reshape(bias_cols, dp, rows)
        return w_q.reshape(D, 3 * HALF), w_o, vectors, bias, pieces[0]

    w_q0, w_o0, vec0, bias0, w_own = attention_weights(shard0[0], "y")
    pieces = gather_pieces(after(shard0[1], w_own), "x")
    (w_u0,) = place(me, pieces, ((0, D * 2),))
    w_u0 = w_u0.reshape(D, D * 2)
    pieces = gather_pieces(after(shard0[2], pieces[0]), "y")
    last = pieces[0]
    (w_d0,) = place(me, pieces, ((0, D),))
    w_d0 = w_d0.reshape(D * 2, D)
    w_q1, w_o1, vec1, bias1, last = attention_weights(after(shard1[0], last), "x")

    up1 = shard1[1].reshape(rows, depth, 4, half_units)
    pick_up = lambda j: lax.dynamic_index_in_dim(up1, me ^ j, axis=2, keepdims=False)
    relative = [pick_up(0)] + [to_plane(pick_up(j), j) for j in (1, 2, 3)]
    relative = jnp.stack([v.reshape(rows, depth * half_units) for v in relative])
    natural = jnp.concatenate(
        [lax.dynamic_slice_in_dim(relative, me ^ n, 1, axis=0) for n in range(4)], axis=0
    )
    w_u1 = lax.all_gather(after(natural, last), "z", axis=0, tiled=False).reshape(D, depth * half_units)
    w_d1 = lax.all_gather(after(shard1[2], last), "z", axis=0, tiled=False).reshape(depth * half_units, D)

    bias_up0 = bias0.transpose(1, 0, 2).reshape(1, 2 * D)
    gain_attn0, gain_mlp0, b_down0 = vec0[0:1], vec0[1:2], vec0[2:3]
    x = x_b.astype(f32)
    inv_attn0 = inverse_rms(x)
    a0 = (x * inv_attn0 * gain_attn0).astype(bf16)
    qkv0 = mm(a0, w_q0).astype(bf16)
    o0 = attend(qkv0, seg, LANES)
    z_part = mm(o0, w_o0).astype(bf16)
    h0 = x + (z_part.astype(f32) + swap(z_part, "section").astype(f32))
    inv_mlp0 = inverse_rms(h0)
    m0 = (h0 * inv_mlp0 * gain_mlp0).astype(bf16)
    u0 = mm(m0, w_u0) + bias_up0
    g0 = gelu_value(u0).astype(bf16)
    e_part = mm(g0, w_d0).astype(bf16)
    e0 = e_part.astype(f32) + swap(e_part, "section").astype(f32) + b_down0
    y0_b = (h0 + e0).astype(bf16)

    onehot = picked[:, :, None] == lax.broadcasted_iota(jnp.int32, (micro, count, length), 2)
    onehot_b = onehot.astype(bf16)
    take = lambda v: lax.dot_general(
        onehot_b,
        v.reshape(micro, length, D),
        (((2,), (1,)), ((0,), (0,))),
        preferred_element_type=f32,
    ).reshape(chosen_rows, D)
    put = lambda v: lax.dot_general(
        onehot.astype(f32),
        v.reshape(micro, count, D),
        (((1,), (1,)), ((0,), (0,))),
        precision=lax.Precision.HIGHEST,
        preferred_element_type=f32,
    ).reshape(tokens, D)
    seg1 = jnp.sum(jnp.where(onehot, seg[:, None, :], 0), axis=2)
    chosen = take(y0_b)
    grad_chosen = take(cot_b)
    router_full = jnp.concatenate(
        [v[3].reshape(dp, rows)[:, : rows // 2].reshape(1, HALF) for v in (vec0, vec1)], axis=1
    )
    weight = jax.nn.sigmoid(jnp.sum(chosen * router_full, axis=1, keepdims=True))
    gy1 = weight * grad_chosen
    de1 = gy1.astype(bf16)

    def plane_rows(v):
        rest = v.shape[0] // 2
        one = lax.dynamic_slice_in_dim(v, core * rest, rest, axis=0)
        mine_now = jnp.stack([one] + [to_plane(one, j) for j in (1, 2, 3)])
        other_now = swap(mine_now, "section")
        both = jnp.stack(
            [jnp.where(first, mine_now, other_now), jnp.where(first, other_now, mine_now)], axis=1
        )
        both = both.reshape(4, v.shape[0], v.shape[1])
        return both.reshape(4 * v.shape[0], v.shape[1])

    de_all = plane_rows(de1)
    gain_attn1, gain_mlp1, b_down1 = vec1[0:1], vec1[1:2], vec1[2:3]
    bias_mine = lax.dynamic_index_in_dim(
        bias1.reshape(bias_cols, depth, 4, rows), me, axis=2, keepdims=False
    )
    bias_up1 = bias_mine.transpose(1, 0, 2).reshape(1, depth * half_units)
    inv_attn1 = inverse_rms(chosen)
    a1 = (chosen * inv_attn1 * gain_attn1).astype(bf16)
    qkv1 = mm(a1, w_q1).astype(bf16)
    o1 = attend(qkv1, seg1, count)
    z_part = mm(o1, w_o1).astype(bf16)
    z1 = z_part.astype(f32) + swap(z_part, "section").astype(f32)
    h1 = chosen + z1
    inv_mlp1 = inverse_rms(h1)
    m1 = (h1 * inv_mlp1 * gain_mlp1).astype(bf16)
    m_all = plane_rows(m1)
    u1 = mm(m_all, w_u1) + bias_up1
    g1 = gelu_value(u1).astype(bf16)
    e_part = mm(g1, w_d1).astype(bf16)
    du1 = (mm_t(de_all, w_d1) * gelu_slope(u1)).astype(bf16)
    dm_part = mm_t(du1, w_u1).astype(bf16)
    e_part = e_part.reshape(4, chosen_rows, D)
    dm_part = dm_part.reshape(4, chosen_rows, D)
    keep = jnp.where(first, e_part, dm_part)
    recv = swap(jnp.where(first, dm_part, e_part), "section")
    summed = (keep.astype(f32) + recv.astype(f32)).astype(bf16)
    total = summed[0].astype(f32)
    for j in (1, 2, 3):
        total = total + to_plane(summed[j], j).astype(f32)
    total = total.astype(bf16)
    crossed = swap(total, "section")
    e1 = jnp.where(first, total, crossed).astype(f32) + b_down1
    dm1 = jnp.where(first, crossed, total).astype(f32)
    delta = z1 + e1
    y1_b = (y0_b.astype(f32) + put(weight * delta)).astype(bf16)

    grad_logit = jnp.sum(grad_chosen * delta, axis=1, keepdims=True) * weight * (1.0 - weight)
    grad_router = jnp.sum(grad_logit * chosen, axis=0)
    unit_mlp1 = h1 * inv_mlp1
    dh1 = norm_back(dm1, unit_mlp1, inv_mlp1, gain_mlp1)
    dz1 = (gy1 + dh1).astype(bf16)
    do1 = mm_t(dz1, w_o1).astype(bf16)
    dqkv1 = attend_back(qkv1, seg1, do1, count)
    da_part = mm_t(dqkv1, w_q1).astype(bf16)
    da1 = da_part.astype(f32) + swap(da_part, "section").astype(f32)
    unit_attn1 = chosen * inv_attn1
    dx1 = dh1 + norm_back(da1, unit_attn1, inv_attn1, gain_attn1)
    gy0_b = (cot_b.astype(f32) + put(dx1 + grad_logit * router_full)).astype(bf16)

    def extra_of(gain_a, gain_m, down_bias, up_bias, block):
        part = grad_router[block * HALF : (block + 1) * HALF].reshape(dp, rows // 2)
        part = jnp.pad(part, ((0, 0), (0, rows - rows // 2))).reshape(D)
        columns = [v[None] for v in (gain_a, gain_m, down_bias, part)]
        columns = jnp.concatenate(columns + [up_bias], axis=0)
        columns = jnp.pad(columns, ((0, LANES - columns.shape[0]), (0, 0)))
        return columns.T.astype(bf16)

    def out_by_columns(grad):
        own = lax.dynamic_slice_in_dim(grad, core * HALF, HALF, axis=1)
        recv = swap(lax.dynamic_slice_in_dim(grad, (1 - core) * HALF, HALF, axis=1), "section")
        return jnp.concatenate([jnp.where(first, own, recv), jnp.where(first, recv, own)], axis=0)

    gw_d1 = mm_rows(g1, de_all).astype(bf16).reshape(depth, half_units, D)
    gw_u1 = mm_rows(m_all, du1).astype(bf16).reshape(depth, 4, rows, depth * half_units)
    gw_o1 = out_by_columns(mm_rows(o1, dz1).astype(bf16))
    gw_q1 = mm_rows(a1, dqkv1).astype(bf16)
    gb_u1 = jnp.sum(du1.astype(f32), axis=0).reshape(depth, 1, bias_cols, rows)
    here = lax.broadcasted_iota(jnp.int32, (1, 4, 1, 1), 1) == me
    gb_u1 = jnp.where(here, gb_u1, 0.0).transpose(2, 0, 1, 3).reshape(bias_cols, D)
    extra1 = extra_of(
        jnp.sum(da1 * unit_attn1, axis=0),
        jnp.sum(dm1 * unit_mlp1, axis=0),
        jnp.sum(de1.astype(f32), axis=0),
        gb_u1,
        1,
    )
    as_shards = lambda v: v.reshape(depth, 4, v.shape[0] // dp, v.shape[1])
    r_d1 = reduce_z(gw_d1)
    r_u1 = reduce_z(gw_u1)
    attn1 = as_shards(jnp.concatenate([gw_q1, gw_o1, extra1], axis=1))
    r_a1 = reduce_z(reduce_plane(attn1, me, "x"))
    pick_up = lambda j: lax.dynamic_index_in_dim(r_u1, me ^ j, axis=0, keepdims=False)
    relative = [pick_up(0)] + [to_plane(pick_up(j), j) for j in (1, 2, 3)]
    relative = jnp.stack([v.reshape(rows, depth, half_units) for v in relative], axis=2)
    r_u1 = jnp.concatenate(
        [lax.dynamic_slice_in_dim(relative, me ^ n, 1, axis=2) for n in range(4)], axis=2
    ).reshape(rows, 2 * D)

    gw_d0 = mm_rows(g0, gy0_b).astype(bf16)
    r_d0 = reduce_z(reduce_plane(as_shards(gw_d0), me, "y"))
    du0 = (mm_t(gy0_b, w_d0) * gelu_slope(u0)).astype(bf16)
    gw_u0 = mm_rows(m0, du0).astype(bf16)
    r_u0 = reduce_z(reduce_plane(as_shards(gw_u0), me, "x"))
    dm_part = mm_t(du0, w_u0).astype(bf16)
    dm0 = dm_part.astype(f32) + swap(dm_part, "section").astype(f32)
    unit_mlp0 = h0 * inv_mlp0
    dh0 = norm_back(dm0, unit_mlp0, inv_mlp0, gain_mlp0)
    gy0 = gy0_b.astype(f32)
    dz0 = (gy0 + dh0).astype(bf16)
    do0 = mm_t(dz0, w_o0).astype(bf16)
    dqkv0 = attend_back(qkv0, seg, do0, LANES)
    da_part = mm_t(dqkv0, w_q0).astype(bf16)
    da0 = da_part.astype(f32) + swap(da_part, "section").astype(f32)
    gw_o0 = out_by_columns(mm_rows(o0, dz0).astype(bf16))
    gw_q0 = mm_rows(a0, dqkv0).astype(bf16)
    unit_attn0 = x * inv_attn0
    dx0_b = (gy0 + dh0 + norm_back(da0, unit_attn0, inv_attn0, gain_attn0)).astype(bf16)
    gb_u0 = jnp.sum(du0.astype(f32), axis=0).reshape(dp, bias_cols, rows)
    extra0 = extra_of(
        jnp.sum(da0 * unit_attn0, axis=0),
        jnp.sum(dm0 * unit_mlp0, axis=0),
        jnp.sum(gy0, axis=0),
        gb_u0.transpose(1, 0, 2).reshape(bias_cols, D),
        0,
    )
    attn0 = as_shards(jnp.concatenate([gw_q0, gw_o0, extra0], axis=1))
    r_a0 = reduce_z(reduce_plane(attn0, me, "y"))

    def joined(grad0, grad1):
        keep = jnp.where(first, grad0, grad1)
        recv = swap(jnp.where(first, grad1, grad0), "section")
        low, high = jnp.where(first, keep, recv), jnp.where(first, recv, keep)
        return keep.astype(f32), low.astype(f32), high.astype(f32)

    _, low, high = joined(r_d0, r_d1)
    out_down = jnp.concatenate([low, high], axis=0)[None]
    _, low, high = joined(r_u0, r_u1)
    cut = lambda v: v.reshape(rows, dp, half_units)
    out_up = jnp.stack([cut(low), cut(high)], axis=2).reshape(1, rows, FF)
    keep, low, high = joined(r_a0, r_a1)
    cut = lambda v: v[:, : 3 * HALF].reshape(rows, 3, HALF)
    out_qkv = jnp.stack([cut(low), cut(high)], axis=2).reshape(1, rows, 3 * D)
    cut = lambda v: v[:, 3 * HALF : 4 * HALF]
    out_out = jnp.concatenate([cut(low), cut(high)], axis=1)[None]
    small = keep[:, 4 * HALF : 4 * HALF + 8].T
    cut = lambda v: v[:, 4 * HALF + 4 : 4 * HALF + 4 + bias_cols].T
    out_b_up = jnp.stack([cut(low), cut(high)]).reshape(1, units)
    boundary_out = jnp.where(first, dx0_b, y1_b).reshape(1, micro, 1, length, D)
    return (
        boundary_out,
        small[0:1],
        out_qkv,
        out_out,
        small[1:2],
        out_up,
        out_b_up,
        out_down,
        small[2:3],
        small[3, : rows // 2],
    )


def solution(mesh):
    sections, dp = mesh.shape["section"], mesh.shape["dp"]
    grid = Mesh(mesh.devices.reshape(sections, dp // 4, 2, 2), ("section", "z", "y", "x"))
    chips = ("z", "y", "x")
    in_specs = (
        P("section", None, chips, None, None),
        P(None, chips, None),
        P(None, chips, None),
        P("section", chips),
        P("section", chips, None),
        P("section", chips, None),
        P("section", chips),
        P("section", chips, None),
        P("section", chips),
        P("section", chips, None),
        P("section", chips),
        P(("section",) + chips),
    )
    out_specs = (
        P("section", None, chips, None, None),
        P("section", chips),
        P("section", chips, None),
        P("section", chips, None),
        P("section", chips),
        P("section", chips, None),
        P("section", chips),
        P("section", chips, None),
        P("section", chips),
        P(("section",) + chips),
    )
    return jax.shard_map(shards, mesh=grid, in_specs=in_specs, out_specs=out_specs, check_vma=False)
```

```python
import functools

import jax
import jax.numpy as jnp
from jax import lax
from jax.experimental import pallas as pl
from jax.experimental.pallas import tpu as pltpu
from jax.sharding import Mesh
from jax.sharding import PartitionSpec as P

D = 1024
HEADS = 16
HEAD_DIM = 64
FF = 4096
HALF = D // 2
LANES = 128

epsilon = 1e-06
masked_score = -1e30
root_half = 0.7071067811865476
inverse_root_two_pi = 0.3989422804014327

f32 = jnp.float32
bf16 = jnp.bfloat16


def mm(a, b):
    return jnp.dot(a, b, preferred_element_type=f32)


def mm_rows(a, b):
    return lax.dot_general(a, b, (((0,), (0,)), ((), ())), preferred_element_type=f32)


def mm_t(a, b):
    return lax.dot_general(a, b, (((1,), (1,)), ((), ())), preferred_element_type=f32)


def inverse_rms(v):
    return lax.rsqrt(jnp.mean(v * v, axis=-1, keepdims=True) + epsilon)


def norm_back(grad, unit, inverse, gain):
    scaled = grad * gain
    return inverse * (scaled - unit * jnp.mean(scaled * unit, axis=-1, keepdims=True))


def swap(v, axis):
    return lax.ppermute(v, axis, [(0, 1), (1, 0)])


def to_plane(v, j):
    return lax.ppermute(v, ("y", "x"), [(i, i ^ j) for i in range(4)])


def fence(*values):
    return lax.optimization_barrier(values)


def over_z(shard):
    return lax.all_gather(shard, "z", axis=0, tiled=False)


def reduce_z(part):
    return lax.psum_scatter(part, "z", scatter_dimension=0, tiled=False)


light = pl.CostEstimate(flops=1, bytes_accessed=1, transcendentals=0)


near_memory = pl.BlockSpec(memory_space=pltpu.VMEM)
far_memory = pl.BlockSpec(memory_space=pltpu.HBM)


def place_kernel(splits, spans, plane_first, me_ref, *rest):
    pieces = rest[: len(spans)]
    outs, sems = rest[len(spans) : len(spans) + len(splits)], rest[-1]
    me = me_ref[0]
    copies = []
    for p, (src, (j, start, stop)) in enumerate(zip(pieces, spans)):
        for k, (low, high) in enumerate(splits):
            out = outs[k].at[me ^ j, start:stop] if plane_first else outs[k].at[start:stop, me ^ j]
            copies.append(
                pltpu.make_async_copy(src.at[:, :, low:high], out, sems.at[p * len(splits) + k])
            )
    for copy in copies:
        copy.start()
    for copy in copies:
        copy.wait()


def place(me, pieces, spans, splits, plane_first=False):
    depth, rows, _ = pieces[0].shape
    lead = (4, depth) if plane_first else (depth, 4)
    return pl.pallas_call(
        functools.partial(place_kernel, splits, spans, plane_first),
        out_shape=[
            jax.ShapeDtypeStruct((*lead, rows, high - low), bf16) for low, high in splits
        ],
        in_specs=[pl.BlockSpec(memory_space=pltpu.SMEM)] + [far_memory] * len(spans),
        out_specs=[near_memory] * len(splits),
        scratch_shapes=[pltpu.SemaphoreType.DMA((len(spans) * len(splits),))],
        compiler_params=pltpu.CompilerParams(vmem_limit_bytes=24 << 20),
        cost_estimate=light,
    )(jnp.reshape(me, (1,)), *pieces)


def mask_of(seg_col, seg_row, low, start, stop):
    keys = low + lax.broadcasted_iota(jnp.int32, (stop - low, stop - start), 0)
    queries = start + lax.broadcasted_iota(jnp.int32, (stop - low, stop - start), 1)
    return (seg_col[low:stop] == seg_row[:, start:stop]) & (keys <= queries)


def head_lanes(h):
    lane = lax.broadcasted_iota(jnp.int32, (1, LANES), 1)
    return (lane // HEAD_DIM == h).astype(bf16)


def softmax_down(q, k, allowed):
    scores = jnp.where(allowed, mm_t(k, q), masked_score)
    exponent = jnp.exp(scores - jnp.max(scores, axis=0, keepdims=True))
    return exponent / jnp.sum(exponent, axis=0, keepdims=True)


def attend_pair(q, k, v, masks, block):
    scale = jnp.asarray(HEAD_DIM**-0.5, bf16)
    rows = []
    for i, allowed in enumerate(masks):
        low, high = max(0, i - 1) * block, (i + 1) * block
        total = None
        for h in range(2):
            lanes = head_lanes(h)
            probs = softmax_down(q[i * block : high] * (lanes * scale), k[low:high], allowed)
            term = mm_rows(probs.astype(bf16), v[low:high] * lanes)
            total = term if total is None else total + term
        rows.append(total)
    return rows


def attend_pair_back(q, k, v, g, masks, block):
    scale = jnp.asarray(HEAD_DIM**-0.5, bf16)
    dq = []
    dk = [None] * len(masks)
    dv = [None] * len(masks)

    def add(parts, low, high, term):
        for b in range(low, high):
            piece = term[(b - low) * block : (b - low + 1) * block]
            parts[b] = piece if parts[b] is None else parts[b] + piece

    for i, allowed in enumerate(masks):
        first = max(0, i - 1)
        low, high = first * block, (i + 1) * block
        total = None
        for h in range(2):
            lanes = head_lanes(h)
            qh = q[i * block : high] * (lanes * scale)
            gh = g[i * block : high] * lanes
            probs = softmax_down(qh, k[low:high], allowed)
            dp = mm_t(v[low:high], gh)
            add(dv, first, i + 1, mm(probs.astype(bf16), gh))
            inner = jnp.sum(dp * probs, axis=0, keepdims=True)
            ds = (probs * (dp - inner)).astype(bf16)
            term = mm_rows(ds, k[low:high] * (lanes * scale))
            total = term if total is None else total + term
            add(dk, first, i + 1, mm(ds, qh))
        dq.append(total)
    return dq, dk, dv


def masks_for(seg_col, seg_row, length, block):
    return [
        mask_of(seg_col, seg_row, max(0, i - 1) * block, i * block, (i + 1) * block)
        for i in range(length // block)
    ]


def attend_kernel(block, pairs, length, qkv_ref, seg_col_ref, seg_row_ref, o_ref):
    for s in range(seg_col_ref.shape[0]):
        masks = masks_for(seg_col_ref[s], seg_row_ref[s], length, block)
        at = slice(s * length, (s + 1) * length)
        for p in range(pairs):
            cut = lambda t: qkv_ref[at, (t * pairs + p) * LANES : (t * pairs + p + 1) * LANES]
            for i, rows in enumerate(attend_pair(cut(0), cut(1), cut(2), masks, block)):
                low = s * length + i * block
                o_ref[low : low + block, p * LANES : (p + 1) * LANES] = rows.astype(bf16)


def attend_out_kernel(block, pairs, length, qkv_ref, sc_ref, sr_ref, w_ref, o_ref, z_ref):
    attend_kernel(block, pairs, length, qkv_ref, sc_ref, sr_ref, o_ref)
    z_ref[...] = mm(o_ref[...], w_ref[...]).astype(bf16)


def attend_back_out_kernel(
    block, pairs, length, qkv_ref, sc_ref, sr_ref, g_ref, w_ref, d_ref, z_ref
):
    attend_back_kernel(block, pairs, length, qkv_ref, sc_ref, sr_ref, g_ref, d_ref)
    z_ref[...] = mm_t(d_ref[...], w_ref[...]).astype(bf16)


def attend_back_kernel(block, pairs, length, qkv_ref, seg_col_ref, seg_row_ref, g_ref, d_ref):
    for s in range(seg_col_ref.shape[0]):
        masks = masks_for(seg_col_ref[s], seg_row_ref[s], length, block)
        at = slice(s * length, (s + 1) * length)
        for p in range(pairs):
            cut = lambda t: qkv_ref[at, (t * pairs + p) * LANES : (t * pairs + p + 1) * LANES]
            g = g_ref[at, p * LANES : (p + 1) * LANES]
            grads = attend_pair_back(cut(0), cut(1), cut(2), g, masks, block)
            for t, parts in enumerate(grads):
                for i, rows in enumerate(parts):
                    low, lane = s * length + i * block, (t * pairs + p) * LANES
                    d_ref[low : low + block, lane : lane + LANES] = rows.astype(bf16)


def attention_call(kernel, seg, arrays, weights, width):
    count, length = seg.shape
    pairs = arrays[0].shape[1] // (3 * LANES)
    at = lambda columns: pl.BlockSpec((length, columns), lambda s: (s, 0))
    return pl.pallas_call(
        functools.partial(kernel, LANES, pairs, length),
        grid=(count,),
        out_shape=[
            jax.ShapeDtypeStruct((count * length, width), bf16),
            jax.ShapeDtypeStruct((count * length, D), bf16),
        ],
        in_specs=[at(arrays[0].shape[1])]
        + [
            pl.BlockSpec((1, length, 1), lambda s: (s, 0, 0)),
            pl.BlockSpec((1, 1, length), lambda s: (s, 0, 0)),
        ]
        + [at(v.shape[1]) for v in arrays[1:]]
        + [pl.BlockSpec(weights.shape, lambda s: (0, 0))],
        out_specs=[at(width), at(D)],
        compiler_params=pltpu.CompilerParams(vmem_limit_bytes=40 << 20),
        cost_estimate=light,
    )(arrays[0], seg[:, :, None], seg[:, None, :], *arrays[1:], weights)


def attn_grad_kernel(relative, count, me_ref, a_ref, d_ref, *refs):
    beside, refs = refs[:count], refs[count:]
    out = refs[-1] if relative else refs[0]
    product = mm_rows(a_ref[...], d_ref[...]).astype(bf16)
    out[:, :, :, : 3 * HALF] = product.reshape(*out.shape[:3], 3 * HALF)
    low = 3 * HALF
    for ref in beside:
        out[:, :, :, low : low + ref.shape[1]] = ref[...].reshape(*out.shape[:3], ref.shape[1])
        low += ref.shape[1]
    if relative:
        for j in range(4):
            refs[j][...] = out[:, me_ref[0] ^ j]


def attn_grad(me, relative, depth, a, dqkv, *beside):
    tokens, step = a.shape[0], 256
    rows = D // (4 * depth)
    deep = step // (4 * rows)
    width = 3 * HALF + sum(v.shape[1] for v in beside)
    if relative:
        outs = [((depth, rows, width), bf16, pl.BlockSpec((deep, rows, width), lambda i: (i, 0, 0)))]
        outs = outs * 4
    else:
        block = pl.BlockSpec((deep, 4, rows, width), lambda i: (i, 0, 0, 0))
        outs = [((depth, 4, rows, width), bf16, block)]
    return tiled_call(
        functools.partial(attn_grad_kernel, relative, len(beside)),
        D // step,
        outs,
        [
            (jnp.reshape(me, (1,)), pl.BlockSpec(memory_space=pltpu.SMEM)),
            (a, pl.BlockSpec((tokens, step), lambda i: (0, i))),
            (dqkv, resident(dqkv.shape)),
        ]
        + [(v, pl.BlockSpec((step, v.shape[1]), lambda i: (i, 0))) for v in beside],
        [pltpu.VMEM((deep, 4, rows, width), bf16)] if relative else [],
    )


def whole(kernel, outs, scalars, arrays, scratch=(), anywhere=0):
    near = len(arrays) - anywhere
    return pl.pallas_call(
        kernel,
        out_shape=[jax.ShapeDtypeStruct(shape, dtype) for shape, dtype in outs],
        in_specs=[pl.BlockSpec(memory_space=pltpu.SMEM)] * len(scalars)
        + [near_memory] * near
        + [far_memory] * anywhere,
        out_specs=[near_memory] * len(outs),
        scratch_shapes=list(scratch),
        compiler_params=pltpu.CompilerParams(vmem_limit_bytes=40 << 20),
        cost_estimate=light,
    )(*[jnp.reshape(v, (1,)) for v in scalars], *arrays)


def resident(shape):
    return pl.BlockSpec(shape, lambda i: (0, 0), pipeline_mode=pl.Buffered(1))


def tiled_call(kernel, steps, outs, ins, scratch=()):
    return pl.pallas_call(
        kernel,
        grid=(steps,),
        out_shape=[jax.ShapeDtypeStruct(shape, dtype) for shape, dtype, _ in outs],
        in_specs=[spec for _, spec in ins],
        out_specs=[spec for _, _, spec in outs],
        scratch_shapes=list(scratch),
        compiler_params=pltpu.CompilerParams(vmem_limit_bytes=48 << 20),
        cost_estimate=light,
    )(*[v for v, _ in ins])


def copy_weights(spans, low, high, me, pieces, w_ref, sems):
    copies = [
        pltpu.make_async_copy(src.at[:, :, low:high], w_ref.at[start:stop, me ^ j], sems.at[p])
        for p, (src, (j, start, stop)) in enumerate(zip(pieces, spans))
    ]
    for copy in copies:
        copy.start()
    return copies


def qkv_kernel(spans, step, me_ref, x_ref, gain_ref, *rest):
    pieces = rest[: len(spans)]
    w_ref, a_ref, qkv_ref, sems = rest[len(spans) :]
    copies = copy_weights(spans, 0, 3 * HALF, me_ref[0], pieces, w_ref, sems)
    for i in range(0, x_ref.shape[0], step):
        x = x_ref[i : i + step].astype(f32)
        a_ref[i : i + step] = (x * inverse_rms(x) * gain_ref[...]).astype(bf16)
    for copy in copies:
        copy.wait()
    weights = w_ref[...].reshape(D, 3 * HALF)
    for i in range(0, x_ref.shape[0], step):
        qkv_ref[i : i + step] = mm(a_ref[i : i + step], weights).astype(bf16)


def hidden_kernel(x_ref, part_ref, recv_ref, gain_ref, h_ref, m_ref):
    h = x_ref[...].astype(f32) + (part_ref[...].astype(f32) + recv_ref[...].astype(f32))
    h_ref[...] = h
    m_ref[...] = (h * inverse_rms(h) * gain_ref[...]).astype(bf16)


def hidden_rows(x, part, recv, gain, step=256):
    tokens = x.shape[0]
    down = pl.BlockSpec((step, D), lambda i: (i, 0))
    row = pl.BlockSpec((1, D), lambda i: (0, 0))
    return tiled_call(
        hidden_kernel,
        tokens // step,
        [((tokens, D), f32, down), ((tokens, D), bf16, down)],
        [(x, down), (part, down), (recv, down), (gain, row)],
    )


def down_kernel(g_ref, w_ref, out_ref):
    out_ref[...] = mm(g_ref[...], w_ref[...]).astype(bf16)


def down_product(g, w, step=256):
    tokens, width = g.shape
    return tiled_call(
        down_kernel,
        tokens // step,
        [((tokens, D), bf16, pl.BlockSpec((step, D), lambda i: (i, 0)))],
        [(g, pl.BlockSpec((step, width), lambda i: (i, 0))), (w, resident(w.shape))],
    )[0]


def choose_kernel(
    h_ref, part_ref, recv_ref, bias_ref, cot_ref, picked_ref, router_ref, gain_ref, *outs
):
    y_ref, chosen_ref, grad_ref, weight_ref, de_ref, a_ref = outs
    e = part_ref[...].astype(f32) + recv_ref[...].astype(f32) + bias_ref[...]
    y = (h_ref[...] + e).astype(bf16)
    y_ref[...] = y
    picked = picked_ref[0]
    places = lax.broadcasted_iota(jnp.int32, (picked.shape[0], y.shape[0]), 1) == picked
    onehot = places.astype(bf16)
    chosen, grad = mm(onehot, y), mm(onehot, cot_ref[...])
    weight = jax.nn.sigmoid(jnp.sum(chosen * router_ref[...], axis=1, keepdims=True))
    chosen_ref[...] = chosen
    grad_ref[...] = grad
    weight_ref[...] = weight
    de_ref[...] = (weight * grad).astype(bf16)
    a_ref[...] = (chosen * inverse_rms(chosen) * gain_ref[...]).astype(bf16)


def choose_rows(h, part, recv, bias, cot, picked, router, gain):
    micro, count = picked.shape
    tokens = h.shape[0]
    down = pl.BlockSpec((tokens // micro, D), lambda i: (i, 0))
    row = pl.BlockSpec((1, D), lambda i: (0, 0))
    few = lambda width: pl.BlockSpec((count, width), lambda i: (i, 0))
    rows = micro * count
    return tiled_call(
        choose_kernel,
        micro,
        [
            ((tokens, D), bf16, down),
            ((rows, D), f32, few(D)),
            ((rows, D), f32, few(D)),
            ((rows, 1), f32, few(1)),
            ((rows, D), bf16, few(D)),
            ((rows, D), bf16, few(D)),
        ],
        [
            (h, down),
            (part, down),
            (recv, down),
            (bias, row),
            (cot, down),
            (picked[:, :, None], pl.BlockSpec((1, count, 1), lambda i: (i, 0, 0))),
            (router, row),
            (gain, row),
        ],
    )


def last_kernel(part_ref, recv_ref, x_ref, gain_ref, sum_ref, dx_ref, gain_g):
    da = part_ref[...].astype(f32) + recv_ref[...].astype(f32)
    x = x_ref[...].astype(f32)
    inverse = inverse_rms(x)
    unit = x * inverse
    dx_ref[...] = (sum_ref[...] + norm_back(da, unit, inverse, gain_ref[...])).astype(bf16)
    grad = jnp.sum(da * unit, axis=0, keepdims=True)

    @pl.when(pl.program_id(0) == 0)
    def _():
        gain_g[...] = grad

    @pl.when(pl.program_id(0) > 0)
    def _():
        gain_g[...] += grad


def last_rows(part, recv, x, gain, total, step=256):
    tokens = x.shape[0]
    down = pl.BlockSpec((step, D), lambda i: (i, 0))
    row = pl.BlockSpec((1, D), lambda i: (0, 0))
    return tiled_call(
        last_kernel,
        tokens // step,
        [((tokens, D), bf16, down), ((1, D), f32, row)],
        [(part, down), (recv, down), (x, down), (gain, row), (total, down)],
    )


def up_kernel(m_ref, w_ref, b_ref, g_ref, slope_ref):
    u = mm(m_ref[...], w_ref[...]) + b_ref[...]
    bell = 0.5 * (1.0 + lax.erf(u * root_half))
    g_ref[...] = (u * bell).astype(bf16)
    slope_ref[...] = (bell + u * jnp.exp(-0.5 * u * u) * inverse_root_two_pi).astype(bf16)


def up_product(m, w, bias, step=512):
    tokens, width = m.shape[0], w.shape[1]
    across = pl.BlockSpec((tokens, step), lambda i: (0, i))
    return tiled_call(
        up_kernel,
        width // step,
        [((tokens, width), bf16, across)] * 2,
        [
            (m, resident(m.shape)),
            (w, pl.BlockSpec((w.shape[0], step), lambda i: (0, i))),
            (bias, pl.BlockSpec((1, step), lambda i: (0, i))),
        ],
    )


def down_grad_kernel(me_ref, g_ref, d_ref, *outs):
    product = mm_rows(g_ref[...], d_ref[...]).astype(bf16)
    for j, out in enumerate(outs):

        @pl.when(pl.program_id(0) == j)
        def _(out=out):
            out[...] = product.reshape(out.shape)


def down_grad(me, depth, g, d):
    tokens, width = g.shape
    units = width // (4 * depth)
    return pl.pallas_call(
        down_grad_kernel,
        grid_spec=pltpu.PrefetchScalarGridSpec(
            num_scalar_prefetch=1,
            grid=(4,),
            in_specs=[
                pl.BlockSpec((tokens, width // 4), lambda j, me: (0, me[0] ^ j)),
                pl.BlockSpec(d.shape, lambda j, me: (0, 0), pipeline_mode=pl.Buffered(1)),
            ],
            out_specs=[pl.BlockSpec((depth, units, D), lambda j, me: (0, 0, 0))] * 4,
        ),
        out_shape=[jax.ShapeDtypeStruct((depth, units, D), bf16)] * 4,
        compiler_params=pltpu.CompilerParams(vmem_limit_bytes=48 << 20),
        cost_estimate=light,
    )(jnp.reshape(me, (1,)), g, d)


def mlp_back_kernel(me_ref, d_ref, wd_ref, slope_ref, m_ref, wu_ref, *refs):
    gw_refs, (dm_ref, gb_ref, acc, gw) = refs[:4], refs[4:]
    du = (mm_t(d_ref[...], wd_ref[...]) * slope_ref[...].astype(f32)).astype(bf16)
    gb_ref[...] = jnp.sum(du.astype(f32), axis=0, keepdims=True)
    gw[...] = mm_rows(m_ref[...], du).astype(bf16).reshape(gw.shape)
    for j, gw_ref in enumerate(gw_refs):
        gw_ref[...] = gw[:, me_ref[0] ^ j]
    part = mm_t(du, wu_ref[...])
    step, last = pl.program_id(0), pl.num_programs(0) - 1

    @pl.when(step == 0)
    def _():
        acc[...] = part

    @pl.when((step > 0) & (step < last))
    def _():
        acc[...] += part

    @pl.when(step == last)
    def _():
        dm_ref[...] = (acc[...] + part).astype(bf16)


def mlp_back(me, depth, d, w_down, slope, m, w_up, step=512):
    tokens, width = slope.shape
    rows = D // (4 * depth)
    across = pl.BlockSpec((tokens, step), lambda i: (0, i))
    return tiled_call(
        mlp_back_kernel,
        width // step,
        [
            *[
                ((depth, rows, width), bf16, pl.BlockSpec((depth, rows, step), lambda i: (0, 0, i)))
            ]
            * 4,
            ((tokens, D), bf16, pl.BlockSpec((tokens, D), lambda i: (0, 0))),
            ((1, width), f32, pl.BlockSpec((1, step), lambda i: (0, i))),
        ],
        [
            (jnp.reshape(me, (1,)), pl.BlockSpec(memory_space=pltpu.SMEM)),
            (d, resident(d.shape)),
            (w_down, pl.BlockSpec((step, D), lambda i: (i, 0))),
            (slope, across),
            (m, resident(m.shape)),
            (w_up, pl.BlockSpec((D, step), lambda i: (0, i))),
        ],
        [pltpu.VMEM((tokens, D), f32), pltpu.VMEM((depth, 4, rows, step), bf16)],
    )


def norm_back_kernel(
    part_ref, recv_ref, h_ref, gain_ref, gy_ref, w_ref, dz_ref, sum_ref, do_ref, gain_g, bias_g
):
    dm = part_ref[...].astype(f32) + recv_ref[...].astype(f32)
    h, gy = h_ref[...], gy_ref[...].astype(f32)
    inverse = inverse_rms(h)
    unit = h * inverse
    dh = norm_back(dm, unit, inverse, gain_ref[...])
    total = gy + dh
    dz = total.astype(bf16)
    sum_ref[...] = total
    dz_ref[...] = dz
    do_ref[...] = mm_t(dz, w_ref[...]).astype(bf16)
    grads = jnp.sum(dm * unit, axis=0, keepdims=True), jnp.sum(gy, axis=0, keepdims=True)

    @pl.when(pl.program_id(0) == 0)
    def _():
        gain_g[...], bias_g[...] = grads

    @pl.when(pl.program_id(0) > 0)
    def _():
        gain_g[...] += grads[0]
        bias_g[...] += grads[1]


def norm_back_product(part, recv, h, gain, gy, w_out, step=256):
    tokens = part.shape[0]
    down = lambda width: pl.BlockSpec((step, width), lambda i: (i, 0))
    row = pl.BlockSpec((1, D), lambda i: (0, 0))
    return tiled_call(
        norm_back_kernel,
        tokens // step,
        [
            ((tokens, D), bf16, down(D)),
            ((tokens, D), f32, down(D)),
            ((tokens, HALF), bf16, down(HALF)),
            ((1, D), f32, row),
            ((1, D), f32, row),
        ],
        [
            (part, down(D)),
            (recv, down(D)),
            (h, down(D)),
            (gain, row),
            (gy, down(D)),
            (w_out, resident(w_out.shape)),
        ],
    )


def order_rows_kernel(me_ref, *refs):
    for j, ref in enumerate(refs[:-1]):
        refs[-1][me_ref[0] ^ j] = ref[...]


def order_mlp_kernel(me_ref, u0, u1, u2, u3, d_ref, out_ref):
    rows, width = u0.shape
    units = d_ref.shape[0]
    for j, ref in enumerate((u0, u1, u2, u3)):
        start = pl.multiple_of((me_ref[0] ^ j) * rows, rows)
        out_ref[pl.ds(start, rows)] = ref[...]
    for k in range(2):
        low = 4 * rows + k * units
        out_ref[low : low + units] = d_ref[:, k * width : (k + 1) * width]


def order_columns_kernel(me_ref, *refs):
    out_ref = refs[-1]
    width = refs[0].shape[1]
    for j, ref in enumerate(refs[:-1]):
        start = pl.multiple_of((me_ref[0] ^ j) * width, width)
        out_ref[:, pl.ds(start, width)] = ref[...]


def routed_attn_kernel(count, a_ref, seg_col_ref, seg_row_ref, w_ref, qkv_ref, o_ref):
    weights = w_ref[:, :, :, : 3 * HALF].reshape(D, 3 * HALF)
    qkv_ref[...] = mm(a_ref[...], weights).astype(bf16)
    attend_kernel(count, HALF // LANES, count, qkv_ref, seg_col_ref, seg_row_ref, o_ref)


def routed_hidden_kernel(part_ref, recv_ref, chosen_ref, gain_ref, z_ref, h_ref, m_ref):
    z = part_ref[...].astype(f32) + recv_ref[...].astype(f32)
    h = chosen_ref[...] + z
    z_ref[...] = z
    h_ref[...] = h
    m_ref[...] = (h * inverse_rms(h) * gain_ref[...]).astype(bf16)


def routed_mlp_kernel(core_ref, m0, m1, m2, m3, d0, d1, d2, d3, w_ref, b_ref, *rest):
    g_ref, du_ref, keep_ref, send_ref, gb_ref, m_ref, d_ref = rest
    rows = m0.shape[0]
    for j, (m, d) in enumerate(zip((m0, m1, m2, m3), (d0, d1, d2, d3))):
        m_ref[j * rows : (j + 1) * rows] = m[...]
        d_ref[j * rows : (j + 1) * rows] = d[...]
    hidden = w_ref.shape[2]
    own_rows = D // w_ref.shape[0]
    units = (w_ref.shape[1] - own_rows) // 2
    w_up = w_ref[:, :own_rows].reshape(D, hidden)
    w_down = [
        w_ref[:, own_rows + k * units : own_rows + (k + 1) * units].reshape(hidden, hidden)
        for k in range(2)
    ]
    u = mm(m_ref[...], w_up) + b_ref[...]
    bell = 0.5 * (1.0 + lax.erf(u * root_half))
    g = (u * bell).astype(bf16)
    slope = bell + u * jnp.exp(-0.5 * u * u) * inverse_root_two_pi
    dg = mm_t(d_ref[:, :hidden], w_down[0]) + mm_t(d_ref[:, hidden:], w_down[1])
    du = (dg * slope).astype(bf16)
    g_ref[...] = g
    du_ref[...] = du
    gb_ref[...] = jnp.sum(du.astype(f32), axis=0, keepdims=True)
    e = jnp.concatenate([mm(g, w).astype(bf16) for w in w_down], axis=1).reshape(keep_ref.shape)
    dm = mm_t(du, w_up).astype(bf16).reshape(keep_ref.shape)

    @pl.when(core_ref[0] == 0)
    def _():
        keep_ref[...] = e
        send_ref[...] = dm

    @pl.when(core_ref[0] != 0)
    def _():
        keep_ref[...] = dm
        send_ref[...] = e


def routed_grads_kernel(g_ref, d_ref, m_ref, du_ref, out_ref):
    depth, all_rows, hidden = out_ref.shape
    rows = D // depth
    units = (all_rows - rows) // 2
    up = mm_rows(m_ref[...], du_ref[...]).astype(bf16)
    out_ref[:, :rows] = up.reshape(depth, rows, hidden)
    for k in range(2):
        down = mm_rows(g_ref[...], d_ref[:, k * hidden : (k + 1) * hidden]).astype(bf16)
        low = rows + k * units
        out_ref[:, low : low + units] = down.reshape(depth, units, hidden)


def routed_back_kernel(count, core_ref, *refs):
    ins, outs = refs[:13], refs[13:]
    total, crossed, bias, z_ref, chosen_g, weight_ref, h_ref, gain, wo_ref, wq_ref = ins[:10]
    qkv_ref, seg_col_ref, seg_row_ref = ins[10:]
    delta_ref, logit_ref, dh_ref, dz_ref, gain_g, dqkv_ref, da_ref, do_scr = outs
    first = core_ref[0] == 0
    a, b = total[...].astype(f32), crossed[...].astype(f32)
    e = jnp.where(first, a, b) + bias[...]
    dm = jnp.where(first, b, a)
    delta = z_ref[...] + e
    delta_ref[...] = delta
    weight, grad = weight_ref[...], chosen_g[...]
    logit_ref[...] = jnp.sum(grad * delta, axis=1, keepdims=True) * weight * (1.0 - weight)
    h = h_ref[...]
    inverse = inverse_rms(h)
    unit = h * inverse
    gain_g[...] = jnp.sum(dm * unit, axis=0, keepdims=True)
    dh = norm_back(dm, unit, inverse, gain[...])
    dh_ref[...] = dh
    dz = (weight * grad + dh).astype(bf16)
    dz_ref[...] = dz
    do_scr[...] = mm_t(dz, wo_ref[...]).astype(bf16)
    attend_back_kernel(
        count, HALF // LANES, count, qkv_ref, seg_col_ref, seg_row_ref, do_scr, dqkv_ref
    )
    weights = wq_ref[:, :, :, : 3 * HALF].reshape(D, 3 * HALF)
    da_ref[...] = mm_t(dqkv_ref[...], weights).astype(bf16)


def put_rows(base, rows, picked, length):
    places = lax.broadcasted_iota(jnp.int32, (length, picked.shape[1]), 0) == picked
    onehot = places.astype(bf16)
    high = rows.astype(bf16)
    low = (rows - high.astype(f32)).astype(bf16)
    return base.astype(f32) + (mm(onehot, high) + mm(onehot, low))


def routed_out_kernel(
    part_ref, recv_ref, chosen_ref, gain, dh_ref, logit_ref, router, picked_ref, cot_ref, *outs
):
    gy_ref, gain_g, router_g = outs
    da = part_ref[...].astype(f32) + recv_ref[...].astype(f32)
    chosen, logit = chosen_ref[...], logit_ref[...]
    inverse = inverse_rms(chosen)
    unit = chosen * inverse
    gain_g[...] = jnp.sum(da * unit, axis=0, keepdims=True)
    router_g[...] = jnp.sum(logit * chosen, axis=0, keepdims=True)
    rows = dh_ref[...] + norm_back(da, unit, inverse, gain[...]) + logit * router[...]
    micro, count = picked_ref.shape[0], picked_ref.shape[2]
    length = cot_ref.shape[0] // micro
    for s in range(micro):
        at = slice(s * length, (s + 1) * length)
        cut = rows[s * count : (s + 1) * count]
        gy_ref[at] = put_rows(cot_ref[at], cut, picked_ref[s], length).astype(bf16)


def routed_sum_kernel(y_ref, delta_ref, weight_ref, picked_ref, out_ref):
    rows = weight_ref[...] * delta_ref[...]
    micro, count = picked_ref.shape[0], picked_ref.shape[2]
    length = y_ref.shape[0] // micro
    for s in range(micro):
        at = slice(s * length, (s + 1) * length)
        cut = rows[s * count : (s + 1) * count]
        out_ref[at] = put_rows(y_ref[at], cut, picked_ref[s], length).astype(bf16)


def finish_kernel(core_ref, keep_ref, recv_ref, qkv_ref, out_ref):
    keep, recv = keep_ref[...].astype(f32), recv_ref[:, : 4 * HALF].astype(f32)
    first = core_ref[0] == 0
    low, high = jnp.where(first, keep, recv), jnp.where(first, recv, keep)
    for t in range(3):
        qkv_ref[:, t * D : t * D + HALF] = low[:, t * HALF : (t + 1) * HALF]
        qkv_ref[:, t * D + HALF : (t + 1) * D] = high[:, t * HALF : (t + 1) * HALF]
    out_ref[:, :HALF] = low[:, 3 * HALF : 4 * HALF]
    out_ref[:, HALF:] = high[:, 3 * HALF : 4 * HALF]


def shards(
    boundary_in,
    segments,
    routed,
    gain_attn,
    w_qkv,
    w_out,
    gain_mlp,
    w_up,
    b_up,
    w_down,
    b_down,
    router,
):
    core = lax.axis_index("section")
    first = core == 0
    me = 2 * lax.axis_index("y") + lax.axis_index("x")
    depth = lax.axis_size("z")
    rows = w_qkv.shape[1]
    dp = 4 * depth
    units = w_up.shape[2] // dp
    half_units = units // 2
    micro, length = boundary_in.shape[1], boundary_in.shape[3]
    tokens = micro * length

    qkv_halves = w_qkv[0].astype(bf16).reshape(rows, 3, 2, HALF)
    out_halves = w_out[0].astype(bf16).reshape(rows, 2, HALF)
    up_halves = w_up[0].astype(bf16).reshape(rows, depth, 4, 2, half_units)
    down_halves = w_down[0].astype(bf16).reshape(2, half_units, D)
    bias_cols = half_units // rows
    bias_halves = b_up[0].astype(bf16).reshape(2, bias_cols, rows)
    column = lambda v: jnp.pad(v.astype(bf16), (0, rows - v.shape[0]))[:, None]
    small = jnp.concatenate(
        [column(gain_attn[0]), column(gain_mlp[0]), column(b_down[0]), column(router)], axis=1
    )

    def half(h):
        pick = lambda v, axis: lax.dynamic_index_in_dim(v, h, axis=axis, keepdims=False)
        strip = jnp.concatenate([small, pick(bias_halves, 0).T], axis=1)
        strip = jnp.pad(strip, ((0, 0), (0, 8 - strip.shape[1])))
        none = jnp.zeros_like(strip)
        strip = jnp.concatenate(
            [jnp.where(first, strip, none), jnp.where(first, none, strip)], axis=1
        )
        strip = jnp.pad(strip, ((0, 0), (0, LANES - 16)))
        attn = jnp.concatenate(
            [pick(qkv_halves, 2).reshape(rows, 3 * HALF), pick(out_halves, 1), strip], axis=1
        )
        up = pick(up_halves, 3).transpose(0, 2, 1, 3).reshape(rows, D * 2)
        return attn, up, pick(down_halves, 0)

    kept, sent = half(core), half(1 - core)
    came = tuple(swap(v, "section") for v in sent)
    width = 4 * HALF
    shard0 = [jnp.where(first, k, r) for k, r in zip(kept, came)]
    shard1 = [jnp.where(first, r, k) for k, r in zip(kept, came)]
    strip = kept[0][:, width:] + came[0][:, width:]
    shard0[0] = jnp.concatenate([shard0[0][:, :width], strip], axis=1)
    shard1[0] = shard1[0][:, :width]

    mine = boundary_in[0, :, 0].reshape(tokens, D)
    other = swap(mine, "section")
    x_b = jnp.where(first, mine, other)
    cot_b = jnp.where(first, other, mine)
    seg = segments[:, 0]
    picked = routed[:, 0]
    count = picked.shape[1]
    chosen_rows = micro * count

    def whole_out(w_o):
        w_o = w_o.reshape(D, HALF)
        own = lax.dynamic_slice_in_dim(w_o, core * HALF, HALF, axis=0)
        recv = swap(lax.dynamic_slice_in_dim(w_o, (1 - core) * HALF, HALF, axis=0), "section")
        return jnp.concatenate([jnp.where(first, own, recv), jnp.where(first, recv, own)], axis=1)

    halfway = depth // 2

    own_q = over_z(shard0[0])
    rest = [shard1[0]] + [to_plane(shard1[0], j) for j in (1, 2, 3)]
    (rest,) = whole(order_rows_kernel, [((4, rows, width), bf16)], [me], rest)
    hidden = depth * half_units
    pick_up = lambda j: lax.dynamic_slice_in_dim(shard1[1], (me ^ j) * hidden, hidden, axis=1)
    mlp = [pick_up(0)] + [to_plane(pick_up(j), j) for j in (1, 2, 3)]
    mlp_rows = 4 * rows + 2 * half_units
    (mlp,) = whole(order_mlp_kernel, [((mlp_rows, hidden), bf16)], [me], [*mlp, shard1[2]])
    onehot = picked[:, :, None] == lax.broadcasted_iota(jnp.int32, (micro, count, length), 2)
    seg1 = jnp.sum(jnp.where(onehot, seg[:, None, :], 0), axis=2)
    seg1_col, seg1_row = seg1[:, :, None], seg1[:, None, :]
    own_q, rest, mlp, shard_u = fence(own_q, rest, mlp, shard0[1])

    px_q, py_q = swap(own_q, "x"), swap(own_q, "y")
    own_u = over_z(shard_u)
    own_q, px_q, py_q, own_u, shard_d, x_b, cot_b, seg1_col, seg1_row = fence(
        own_q, px_q, py_q, own_u, shard0[2], x_b, cot_b, seg1_col, seg1_row
    )
    pd_q, px_u = swap(px_q, "y"), swap(own_u, "x")
    own_d = over_z(shard_d)
    own_q, px_q, py_q, pd_q, own_u, px_u, own_d, rest = fence(
        own_q, px_q, py_q, pd_q, own_u, px_u, own_d, rest
    )
    py_u = swap(own_u, "y")
    px_d, py_d = swap(own_d, "x"), swap(own_d, "y")
    w_r1 = over_z(rest)

    spans_all = [(j, 0, depth) for j in range(4)]
    w_o0, strip = place(
        me, [own_q, px_q, py_q, pd_q], spans_all, ((3 * HALF, width), (width, width + LANES))
    )
    w_o0 = whole_out(w_o0)
    choose = (
        lax.broadcasted_iota(jnp.int32, (16, LANES), 0)
        == lax.broadcasted_iota(jnp.int32, (16, LANES), 1)
    ).astype(bf16)
    vectors = mm_t(choose, strip.reshape(D, LANES))
    gain_attn0, gain_mlp0, b_down0 = vectors[0:1], vectors[1:2], vectors[2:3]
    gain_attn1, gain_mlp1, b_down1 = vectors[8:9], vectors[9:10], vectors[10:11]
    router_full = jnp.concatenate(
        [vectors[b].reshape(dp, rows)[:, : rows // 2].reshape(1, HALF) for b in (3, 11)], axis=1
    )
    biases = lambda b: (
        vectors[b : b + bias_cols].reshape(bias_cols, depth, 4, rows).transpose(2, 1, 0, 3)
    )
    bias_up0 = biases(4).reshape(1, 2 * D)
    bias_up1 = lax.dynamic_index_in_dim(biases(12), me, axis=0, keepdims=False)
    bias_up1 = bias_up1.reshape(1, hidden)
    w_q0, a0, qkv0 = whole(
        functools.partial(qkv_kernel, spans_all, 256),
        [
            ((depth, 4, rows, 3 * HALF), bf16),
            ((tokens, D), bf16),
            ((tokens, 3 * HALF), bf16),
        ],
        [me],
        [x_b, gain_attn0, own_q, px_q, py_q, pd_q],
        [pltpu.SemaphoreType.DMA((4,))],
        anywhere=4,
    )
    w_q0 = w_q0.reshape(D, 3 * HALF)
    o0, z_part = attention_call(attend_out_kernel, seg, [qkv0], w_o0, HALF)
    o0, z_part, own_u, px_u, py_u, px_d = fence(o0, z_part, own_u, px_u, py_u, px_d)

    pd_u = swap(py_u, "x")
    pd_d0 = swap(px_d[:halfway], "y")
    h0, m0 = hidden_rows(x_b, z_part, swap(z_part, "section"), gain_mlp0)
    m0, pd_u, py_d = fence(m0, pd_u, py_d)

    pd_d1 = swap(py_d[halfway:], "x")
    (w_u0,) = place(me, [own_u, px_u, py_u, pd_u], spans_all, ((0, D * 2),))
    w_u0 = w_u0.reshape(D, D * 2)
    g0, slope0 = up_product(m0, w_u0, bias_up0)
    g0, pd_d0, pd_d1, mlp, w_r1 = fence(g0, pd_d0, pd_d1, mlp, w_r1)

    w_m1 = over_z(mlp)
    spans_cut = spans_all[:3] + [(3, 0, halfway), (3, halfway, depth)]
    (w_d0,) = place(
        me, [own_d, px_d, py_d, pd_d0, pd_d1], spans_cut, ((0, D),), plane_first=True
    )
    w_d0 = w_d0.reshape(D * 2, D)
    e_part = down_product(g0, w_d0)
    w_o1 = whole_out(w_r1[..., 3 * HALF :])

    y0_b, chosen, grad_chosen, weight, de1, a1 = choose_rows(
        h0, e_part, swap(e_part, "section"), b_down0, cot_b, picked, router_full, gain_attn1
    )
    de_all = [de1] + [to_plane(de1, j) for j in (1, 2, 3)]
    qkv1, o1 = whole(
        functools.partial(routed_attn_kernel, count),
        [((chosen_rows, 3 * HALF), bf16), ((chosen_rows, HALF), bf16)],
        [],
        [a1, seg1_col, seg1_row, w_r1],
    )
    de_all, o1, w_o1 = fence(de_all, o1, w_o1)
    z_part = mm(o1, w_o1).astype(bf16)
    z1, h1, m1 = whole(
        routed_hidden_kernel,
        [((chosen_rows, D), f32)] * 2 + [((chosen_rows, D), bf16)],
        [],
        [z_part, swap(z_part, "section"), chosen, gain_mlp1],
    )
    m_all = [m1] + [to_plane(m1, j) for j in (1, 2, 3)]
    g1, du1, keep, send, gb_u1, m_rows, de_rows = whole(
        routed_mlp_kernel,
        [((4 * chosen_rows, hidden), bf16)] * 2
        + [((4, chosen_rows, D), bf16)] * 2
        + [((1, hidden), f32)]
        + [((4 * chosen_rows, D), bf16)] * 2,
        [core],
        [*m_all, *de_all, w_m1, bias_up1],
    )
    plus = lambda *terms: sum(t.astype(f32) for t in terms).astype(bf16)
    summed = plus(keep, swap(send, "section"))
    (gw_m1,) = whole(
        routed_grads_kernel,
        [((depth, mlp_rows, hidden), bf16)],
        [],
        [g1, de_rows, m_rows, du1],
    )
    total = plus(summed[0], *[to_plane(summed[j], j) for j in (1, 2, 3)])
    crossed = swap(total, "section")
    total, crossed, gw_m1 = fence(total, crossed, gw_m1)

    r_m1 = reduce_z(gw_m1)
    delta, grad_logit, dh1, dz1, gg_mlp1, dqkv1, da_part = whole(
        functools.partial(routed_back_kernel, count),
        [
            ((chosen_rows, D), f32),
            ((chosen_rows, 1), f32),
            ((chosen_rows, D), f32),
            ((chosen_rows, D), bf16),
            ((1, D), f32),
            ((chosen_rows, 3 * HALF), bf16),
            ((chosen_rows, D), bf16),
        ],
        [core],
        [
            total,
            crossed,
            b_down1,
            z1,
            grad_chosen,
            weight,
            h1,
            gain_mlp1,
            w_o1,
            w_r1,
            qkv1,
            seg1_col,
            seg1_row,
        ],
        [pltpu.VMEM((chosen_rows, HALF), bf16)],
    )

    def out_by_columns(grad):
        own = lax.dynamic_slice_in_dim(grad, core * HALF, HALF, axis=1)
        recv = swap(lax.dynamic_slice_in_dim(grad, (1 - core) * HALF, HALF, axis=1), "section")
        return jnp.concatenate([jnp.where(first, own, recv), jnp.where(first, recv, own)], axis=0)

    gw_o1 = out_by_columns(mm_rows(o1, dz1).astype(bf16))
    gy0_b, gg_attn1, grad_router = whole(
        routed_out_kernel,
        [((tokens, D), bf16), ((1, D), f32), ((1, D), f32)],
        [],
        [
            da_part,
            swap(da_part, "section"),
            chosen,
            gain_attn1,
            dh1,
            grad_logit,
            router_full,
            picked[:, None, :],
            cot_b,
        ],
    )
    (attn1,) = attn_grad(me, False, depth, a1, dqkv1, gw_o1)
    gw_d0 = down_grad(me, depth, g0, gy0_b)
    gw_d0, attn1, gy0_b, r_m1 = fence(gw_d0, attn1, gy0_b, r_m1)

    r_a1 = reduce_z(attn1)
    diag_d = swap(gw_d0[3], "x")
    *gw_u0, dm_part, gb_u0 = mlp_back(me, depth, gy0_b, w_d0, slope0, m0, w_u0)
    gw_u0, dm_part, gw_d0, diag_d = fence(gw_u0, dm_part, gw_d0, diag_d)

    far_d, diag_u = swap(gw_d0[1], "x"), swap(gw_u0[3], "y")
    sum_d = plus(gw_d0[2], diag_d)
    dz0, gy_dh0, do0, gg_mlp0, g_down0 = norm_back_product(
        dm_part, swap(dm_part, "section"), h0, gain_mlp0, gy0_b, w_o0
    )
    dqkv0, da_part = attention_call(attend_back_out_kernel, seg, [qkv0, do0], w_q0, 3 * HALF)
    gw_o0 = out_by_columns(mm_rows(o0, dz0).astype(bf16))
    far_d, diag_u, sum_d, dqkv0, da_part, gw_o0 = fence(far_d, diag_u, sum_d, dqkv0, da_part, gw_o0)

    near_u, near_d = swap(plus(gw_u0[1], diag_u), "x"), swap(sum_d, "y")
    dx0_b, gg_attn0 = last_rows(da_part, swap(da_part, "section"), x_b, gain_attn0, gy_dh0)
    here = lax.broadcasted_iota(jnp.int32, (depth, 4, bias_cols, rows), 1) == me
    gb_u1 = gb_u1.reshape(depth, 1, bias_cols, rows)
    gb_u1 = jnp.where(here, gb_u1, 0.0).transpose(2, 0, 1, 3).reshape(bias_cols, D)
    gb_u0 = gb_u0.reshape(4, depth, bias_cols, rows).transpose(2, 1, 0, 3).reshape(bias_cols, D)
    router_rows = jnp.pad(
        grad_router.reshape(2, dp, rows // 2), ((0, 0), (0, 0), (0, rows - rows // 2))
    ).reshape(2, D)
    g_down1 = jnp.sum(de1.astype(f32), axis=0, keepdims=True)
    blank = jnp.zeros((4 - bias_cols, D), f32)
    strip = jnp.concatenate(
        [gg_attn0, gg_mlp0, g_down0, router_rows[0:1], gb_u0, blank]
        + [gg_attn1, gg_mlp1, g_down1, router_rows[1:2], gb_u1, blank]
    )
    strip = jnp.pad(strip, ((0, LANES - 16), (0, 0))).T.astype(bf16)
    attn0 = attn_grad(me, True, depth, a0, dqkv0, gw_o0, strip)
    attn0, near_u, near_d, far_d, r_a1 = fence(attn0, near_u, near_d, far_d, r_a1)

    diag_q, far_u = swap(attn0[3], "x"), swap(gw_u0[2], "y")
    r_d0 = reduce_z(plus(gw_d0[0], near_d, far_d))
    (y1_b,) = whole(
        routed_sum_kernel,
        [((tokens, D), bf16)],
        [],
        [y0_b, delta, weight, picked[:, None, :]],
    )
    boundary_out = jnp.where(first, dx0_b, y1_b).reshape(1, micro, 1, length, D)
    boundary_out, diag_q, far_u, r_a1, r_m1 = fence(boundary_out, diag_q, far_u, r_a1, r_m1)

    far_q, near_q = swap(attn0[1], "x"), swap(plus(attn0[2], diag_q), "y")
    r_u0 = reduce_z(plus(gw_u0[0], near_u, far_u))
    part = lambda v, j: lax.dynamic_index_in_dim(v, me ^ j, axis=0, keepdims=False)
    r_a1 = plus(part(r_a1, 0), *[to_plane(part(r_a1, j), j) for j in (1, 2, 3)])
    up = r_m1[: 4 * rows].reshape(4, rows, hidden)
    up = [part(up, 0)] + [to_plane(part(up, j), j) for j in (1, 2, 3)]
    (r_u1,) = whole(order_columns_kernel, [((rows, 2 * D), bf16)], [me], up)
    low = 4 * rows + half_units
    r_d1 = jnp.concatenate([r_m1[4 * rows : low], r_m1[low:]], axis=1)
    far_q, near_q, r_a1, r_u1, r_d1, r_d0 = fence(far_q, near_q, r_a1, r_u1, r_d1, r_d0)
    r_a0 = reduce_z(plus(attn0[0], near_q, far_q))

    def joined(grad0, grad1):
        keep = jnp.where(first, grad0, grad1)
        recv = swap(jnp.where(first, grad1, grad0), "section")
        return jnp.where(first, keep, recv).astype(f32), jnp.where(first, recv, keep).astype(f32)

    low, high = joined(r_d0, r_d1)
    out_down = jnp.concatenate([low, high], axis=0)[None]
    low, high = joined(r_u0, r_u1)
    cut = lambda v: v.reshape(rows, 4, depth, half_units).transpose(0, 2, 1, 3)
    out_up = jnp.stack([cut(low), cut(high)], axis=3).reshape(1, rows, FF)
    r_a0, out_up, out_down, boundary_out = fence(r_a0, out_up, out_down, boundary_out)
    strip = r_a0[:, width:]
    strip_mine = jnp.where(first, strip[:, :8], strip[:, 8:16])
    strip_other = jnp.where(first, strip[:, 8:16], strip[:, :8])
    keep = jnp.where(first, r_a0[:, :width], r_a1)
    send = jnp.where(first, r_a1, r_a0[:, :width])
    pad = lambda v: jnp.pad(v, ((0, 0), (0, LANES - 8)))
    recv = swap(jnp.concatenate([send, pad(strip_other)], axis=1), "section")
    out_qkv, out_out = whole(
        finish_kernel,
        [((rows, 3 * D), f32), ((rows, D), f32)],
        [core],
        [keep, recv],
    )
    small = strip_mine.astype(f32).T
    bias_half = small[4 : 4 + bias_cols]
    bias_other = recv[:, width + 4 : width + 4 + bias_cols].astype(f32).T
    out_b_up = jnp.concatenate(
        [jnp.where(first, bias_half, bias_other), jnp.where(first, bias_other, bias_half)]
    ).reshape(1, units)
    return (
        boundary_out,
        small[0:1],
        out_qkv[None],
        out_out[None],
        small[1:2],
        out_up,
        out_b_up,
        out_down,
        small[2:3],
        small[3, : rows // 2],
    )


def solution(mesh):
    sections, dp = mesh.shape["section"], mesh.shape["dp"]
    grid = Mesh(mesh.devices.reshape(sections, dp // 4, 2, 2), ("section", "z", "y", "x"))
    chips = ("z", "y", "x")
    in_specs = (
        P("section", None, chips, None, None),
        P(None, chips, None),
        P(None, chips, None),
        P("section", chips),
        P("section", chips, None),
        P("section", chips, None),
        P("section", chips),
        P("section", chips, None),
        P("section", chips),
        P("section", chips, None),
        P("section", chips),
        P(("section",) + chips),
    )
    out_specs = (
        P("section", None, chips, None, None),
        P("section", chips),
        P("section", chips, None),
        P("section", chips, None),
        P("section", chips),
        P("section", chips, None),
        P("section", chips),
        P("section", chips, None),
        P("section", chips),
        P(("section",) + chips),
    )
    return jax.shard_map(shards, mesh=grid, in_specs=in_specs, out_specs=out_specs, check_vma=False)
```

```python
import functools

import jax
import jax.numpy as jnp
from jax import lax
from jax.experimental import pallas as pl
from jax.experimental.pallas import tpu as pltpu
from jax.sharding import Mesh
from jax.sharding import PartitionSpec as P

D = 1024
HEADS = 16
HEAD_DIM = 64
FF = 4096
HALF = D // 2
LANES = 128

epsilon = 1e-06
masked_score = -1e30
root_half = 0.7071067811865476
inverse_root_two_pi = 0.3989422804014327

f32 = jnp.float32
bf16 = jnp.bfloat16


def mm(a, b):
    return jnp.dot(a, b, preferred_element_type=f32)


def mm_rows(a, b):
    return lax.dot_general(a, b, (((0,), (0,)), ((), ())), preferred_element_type=f32)


def mm_t(a, b):
    return lax.dot_general(a, b, (((1,), (1,)), ((), ())), preferred_element_type=f32)


def inverse_rms(v):
    return lax.rsqrt(jnp.mean(v * v, axis=-1, keepdims=True) + epsilon)


def norm_back(grad, unit, inverse, gain):
    scaled = grad * gain
    return inverse * (scaled - unit * jnp.mean(scaled * unit, axis=-1, keepdims=True))


def swap(v, axis):
    return lax.ppermute(v, axis, [(0, 1), (1, 0)])


def to_plane(v, j):
    return lax.ppermute(v, ("y", "x"), [(i, i ^ j) for i in range(4)])


def fence(*values):
    return lax.optimization_barrier(values)


def over_z(shard):
    return lax.all_gather(shard, "z", axis=0, tiled=False)


def reduce_z(part):
    return lax.psum_scatter(part, "z", scatter_dimension=0, tiled=False)


mark = ((8, LANES), f32)
light = pl.CostEstimate(flops=1, bytes_accessed=1, transcendentals=0)


near_memory = pl.BlockSpec(memory_space=pltpu.VMEM)
far_memory = pl.BlockSpec(memory_space=pltpu.HBM)


def place_kernel(splits, spans, plane_first, me_ref, *rest):
    pieces = rest[: len(spans)]
    outs, sems = rest[len(spans) : len(spans) + len(splits)], rest[-1]
    me = me_ref[0]
    copies = []
    for p, (src, (j, start, stop)) in enumerate(zip(pieces, spans)):
        for k, (low, high) in enumerate(splits):
            out = outs[k].at[me ^ j, start:stop] if plane_first else outs[k].at[start:stop, me ^ j]
            copies.append(
                pltpu.make_async_copy(src.at[:, :, low:high], out, sems.at[p * len(splits) + k])
            )
    for copy in copies:
        copy.start()
    for copy in copies:
        copy.wait()


def place(me, pieces, spans, splits, plane_first=False):
    depth, rows, _ = pieces[0].shape
    lead = (4, depth) if plane_first else (depth, 4)
    return pl.pallas_call(
        functools.partial(place_kernel, splits, spans, plane_first),
        out_shape=[
            jax.ShapeDtypeStruct((*lead, rows, high - low), bf16) for low, high in splits
        ],
        in_specs=[pl.BlockSpec(memory_space=pltpu.SMEM)] + [far_memory] * len(spans),
        out_specs=[near_memory] * len(splits),
        scratch_shapes=[pltpu.SemaphoreType.DMA((len(spans) * len(splits),))],
        compiler_params=pltpu.CompilerParams(vmem_limit_bytes=16 << 20),
        cost_estimate=light,
    )(jnp.reshape(me, (1,)), *pieces)


def mask_of(seg_col, seg_row, low, start, stop):
    keys = low + lax.broadcasted_iota(jnp.int32, (stop - low, stop - start), 0)
    queries = start + lax.broadcasted_iota(jnp.int32, (stop - low, stop - start), 1)
    allowed = (seg_col[low:stop] == seg_row[:, start:stop]) & (keys <= queries)
    return allowed.astype(jnp.int32)


def both_heads(v):
    lane = lax.broadcasted_iota(jnp.int32, (1, LANES), 1)
    upper = (lane >= HEAD_DIM).astype(bf16)
    return jnp.concatenate([v * (1 - upper), v * upper], axis=0)


def merged_heads(v):
    half = v.shape[0] // 2
    lane = lax.broadcasted_iota(jnp.int32, (1, LANES), 1)
    return jnp.where(lane < HEAD_DIM, v[:half], v[half:])


def softmax_down(q, k, allowed):
    scores = jnp.where(allowed != 0, mm_t(k, q), masked_score)
    exponent = jnp.exp(scores - jnp.max(scores, axis=0, keepdims=True))
    return exponent / jnp.sum(exponent, axis=0, keepdims=True)


def attend_pair(q, k, v, masks, block):
    scale = jnp.asarray(HEAD_DIM**-0.5, bf16)
    rows = []
    for i, allowed in enumerate(masks):
        low, high = max(0, i - 1) * block, (i + 1) * block
        probs = softmax_down(both_heads(q[i * block : high] * scale), k[low:high], allowed)
        rows.append(merged_heads(mm_rows(probs.astype(bf16), v[low:high])))
    return rows


def attend_pair_back(q, k, v, g, masks, block):
    scale = jnp.asarray(HEAD_DIM**-0.5, bf16)
    dq = []
    dk = [None] * len(masks)
    dv = [None] * len(masks)

    def add(parts, low, high, term):
        for b in range(low, high):
            piece = term[(b - low) * block : (b - low + 1) * block]
            parts[b] = piece if parts[b] is None else parts[b] + piece

    for i, allowed in enumerate(masks):
        first = max(0, i - 1)
        low, high = first * block, (i + 1) * block
        qh, gh = both_heads(q[i * block : high] * scale), both_heads(g[i * block : high])
        probs = softmax_down(qh, k[low:high], allowed)
        dp = mm_t(v[low:high], gh)
        add(dv, first, i + 1, mm(probs.astype(bf16), gh))
        inner = jnp.sum(dp * probs, axis=0, keepdims=True)
        ds = (probs * (dp - inner)).astype(bf16)
        dq.append(merged_heads(mm_rows(ds, k[low:high] * scale)))
        add(dk, first, i + 1, mm(ds, qh))
    return dq, dk, dv


def masks_for(seg_col, seg_row, length, block):
    masks = [
        mask_of(seg_col, seg_row, max(0, i - 1) * block, i * block, (i + 1) * block)
        for i in range(length // block)
    ]
    return [jnp.concatenate([m, m], axis=1) for m in masks]


def attend_kernel(block, pairs, length, qkv_ref, seg_col_ref, seg_row_ref, o_ref):
    for s in range(seg_col_ref.shape[0]):
        masks = masks_for(seg_col_ref[s], seg_row_ref[s], length, block)
        at = slice(s * length, (s + 1) * length)
        for p in range(pairs):
            cut = lambda t: qkv_ref[at, (t * pairs + p) * LANES : (t * pairs + p + 1) * LANES]
            for i, rows in enumerate(attend_pair(cut(0), cut(1), cut(2), masks, block)):
                low = s * length + i * block
                o_ref[low : low + block, p * LANES : (p + 1) * LANES] = rows.astype(bf16)


def attend_out_kernel(block, pairs, length, qkv_ref, sc_ref, sr_ref, w_ref, o_ref, z_ref):
    attend_kernel(block, pairs, length, qkv_ref, sc_ref, sr_ref, o_ref)
    z_ref[...] = mm(o_ref[...], w_ref[...]).astype(bf16)


def attend_back_out_kernel(
    block, pairs, length, qkv_ref, sc_ref, sr_ref, g_ref, x_ref, w_ref, d_ref, z_ref, gain_g
):
    attend_back_kernel(block, pairs, length, qkv_ref, sc_ref, sr_ref, g_ref, d_ref)
    da = mm_t(d_ref[...], w_ref[...])
    z_ref[...] = da.astype(bf16)
    x = x_ref[...].astype(f32)
    grad = jnp.sum(da * (x * inverse_rms(x)), axis=0, keepdims=True)

    @pl.when(pl.program_id(0) == 0)
    def _():
        gain_g[...] = grad

    @pl.when(pl.program_id(0) > 0)
    def _():
        gain_g[...] += grad


def attend_back_kernel(block, pairs, length, qkv_ref, seg_col_ref, seg_row_ref, g_ref, d_ref):
    for s in range(seg_col_ref.shape[0]):
        masks = masks_for(seg_col_ref[s], seg_row_ref[s], length, block)
        at = slice(s * length, (s + 1) * length)
        for p in range(pairs):
            cut = lambda t: qkv_ref[at, (t * pairs + p) * LANES : (t * pairs + p + 1) * LANES]
            g = g_ref[at, p * LANES : (p + 1) * LANES]
            grads = attend_pair_back(cut(0), cut(1), cut(2), g, masks, block)
            for t, parts in enumerate(grads):
                for i, rows in enumerate(parts):
                    low, lane = s * length + i * block, (t * pairs + p) * LANES
                    d_ref[low : low + block, lane : lane + LANES] = rows.astype(bf16)


def attention_call(kernel, seg, arrays, weights, width, sums=0):
    count, length = seg.shape
    pairs = arrays[0].shape[1] // (3 * LANES)
    at = lambda columns: pl.BlockSpec((length, columns), lambda s: (s, 0))
    return pl.pallas_call(
        functools.partial(kernel, LANES, pairs, length),
        grid=(count,),
        out_shape=[
            jax.ShapeDtypeStruct((count * length, width), bf16),
            jax.ShapeDtypeStruct((count * length, D), bf16),
        ]
        + [jax.ShapeDtypeStruct((1, D), f32)] * sums,
        in_specs=[at(arrays[0].shape[1])]
        + [
            pl.BlockSpec((1, length, 1), lambda s: (s, 0, 0)),
            pl.BlockSpec((1, 1, length), lambda s: (s, 0, 0)),
        ]
        + [at(v.shape[1]) for v in arrays[1:]]
        + [pl.BlockSpec(weights.shape, lambda s: (0, 0))],
        out_specs=[at(width), at(D)] + [pl.BlockSpec((1, D), lambda s: (0, 0))] * sums,
        compiler_params=pltpu.CompilerParams(vmem_limit_bytes=16 << 20),
        cost_estimate=light,
    )(arrays[0], seg[:, :, None], seg[:, None, :], *arrays[1:], weights)


def attn_grad_kernel(relative, count, me_ref, a_ref, d_ref, *refs):
    beside, refs = refs[:count], refs[count:]
    out = refs[-1] if relative else refs[0]
    product = mm_rows(a_ref[...], d_ref[...]).astype(bf16)
    out[:, :, :, : 3 * HALF] = product.reshape(*out.shape[:3], 3 * HALF)
    low = 3 * HALF
    for ref in beside:
        out[:, :, :, low : low + ref.shape[1]] = ref[...].reshape(*out.shape[:3], ref.shape[1])
        low += ref.shape[1]
    for h in range(2 if relative else 0):

        @pl.when(pl.program_id(0) // 2 == h)
        def _(h=h):
            for j in range(4):
                refs[2 * j + h][...] = out[:, me_ref[0] ^ j]


def attn_grad(me, relative, depth, a, dqkv, *beside):
    tokens, step = a.shape[0], D // 4
    rows = D // (4 * depth)
    deep = step // (4 * rows)
    width = 3 * HALF + sum(v.shape[1] for v in beside)
    if relative:
        half = lambda h: pl.BlockSpec(
            (deep, rows, width), lambda i: (jnp.clip(i - 2 * h, 0, 1), 0, 0)
        )
        outs = [((depth // 2, rows, width), bf16, half(h)) for _ in range(4) for h in range(2)]
    else:
        block = pl.BlockSpec((deep, 4, rows, width), lambda i: (i, 0, 0, 0))
        outs = [((depth, 4, rows, width), bf16, block)]
    found = tiled_call(
        functools.partial(attn_grad_kernel, relative, len(beside)),
        D // step,
        outs,
        [
            (jnp.reshape(me, (1,)), pl.BlockSpec(memory_space=pltpu.SMEM)),
            (a, pl.BlockSpec((tokens, step), lambda i: (0, i))),
            (dqkv, resident(dqkv.shape)),
        ]
        + [(v, pl.BlockSpec((step, v.shape[1]), lambda i: (i, 0))) for v in beside],
        [pltpu.VMEM((deep, 4, rows, width), bf16)] if relative else [],
    )
    return pairs_of(found) if relative else found[0]


def pairs_of(arrays):
    return [tuple(arrays[2 * j : 2 * j + 2]) for j in range(len(arrays) // 2)]


def whole(kernel, outs, scalars, arrays, scratch=(), anywhere=0):
    near = len(arrays) - anywhere
    return pl.pallas_call(
        kernel,
        out_shape=[jax.ShapeDtypeStruct(shape, dtype) for shape, dtype in outs],
        in_specs=[pl.BlockSpec(memory_space=pltpu.SMEM)] * len(scalars)
        + [near_memory] * near
        + [far_memory] * anywhere,
        out_specs=[near_memory] * len(outs),
        scratch_shapes=list(scratch),
        compiler_params=pltpu.CompilerParams(vmem_limit_bytes=16 << 20),
        cost_estimate=light,
    )(*[jnp.reshape(v, (1,)) for v in scalars], *arrays)


def resident(shape):
    return pl.BlockSpec(shape, lambda i: (0, 0), pipeline_mode=pl.Buffered(1))


def tiled_call(kernel, steps, outs, ins, scratch=()):
    return pl.pallas_call(
        kernel,
        grid=(steps,),
        out_shape=[jax.ShapeDtypeStruct(shape, dtype) for shape, dtype, _ in outs],
        in_specs=[spec for _, spec in ins],
        out_specs=[spec for _, _, spec in outs],
        scratch_shapes=list(scratch),
        compiler_params=pltpu.CompilerParams(vmem_limit_bytes=20 << 20),
        cost_estimate=light,
    )(*[v for v, _ in ins])


def copy_weights(spans, low, high, me, pieces, w_ref, sems):
    copies = [
        pltpu.make_async_copy(src.at[:, :, low:high], w_ref.at[start:stop, me ^ j], sems.at[p])
        for p, (src, (j, start, stop)) in enumerate(zip(pieces, spans))
    ]
    for copy in copies:
        copy.start()
    return copies


def qkv_kernel(spans, step, me_ref, x_ref, gain_ref, *rest):
    pieces = rest[: len(spans)]
    w_ref, a_ref, qkv_ref, sems = rest[len(spans) :]
    copies = copy_weights(spans, 0, 3 * HALF, me_ref[0], pieces, w_ref, sems)
    for i in range(0, x_ref.shape[0], step):
        x = x_ref[i : i + step].astype(f32)
        a_ref[i : i + step] = (x * inverse_rms(x) * gain_ref[...]).astype(bf16)
    for copy in copies:
        copy.wait()
    weights = w_ref[...].reshape(D, 3 * HALF)
    for i in range(0, x_ref.shape[0], step):
        qkv_ref[i : i + step] = mm(a_ref[i : i + step], weights).astype(bf16)


def hidden_kernel(x_ref, part_ref, recv_ref, gain_ref, h_ref, m_ref):
    h = x_ref[...].astype(f32) + (part_ref[...].astype(f32) + recv_ref[...].astype(f32))
    h_ref[...] = h
    m_ref[...] = (h * inverse_rms(h) * gain_ref[...]).astype(bf16)


def hidden_rows(x, part, recv, gain, step=256):
    tokens = x.shape[0]
    down = pl.BlockSpec((step, D), lambda i: (i, 0))
    row = pl.BlockSpec((1, D), lambda i: (0, 0))
    return tiled_call(
        hidden_kernel,
        tokens // step,
        [((tokens, D), f32, down), ((tokens, D), bf16, down)],
        [(x, down), (part, down), (recv, down), (gain, row)],
    )


def down_kernel(g_ref, w_ref, out_ref):
    out_ref[...] = mm(g_ref[...], w_ref[...]).astype(bf16)


def down_product(g, w, step=256):
    tokens, width = g.shape
    return tiled_call(
        down_kernel,
        tokens // step,
        [((tokens, D), bf16, pl.BlockSpec((step, D), lambda i: (i, 0)))],
        [(g, pl.BlockSpec((step, width), lambda i: (i, 0))), (w, resident(w.shape))],
    )[0]


def choose_kernel(
    h_ref, part_ref, recv_ref, bias_ref, cot_ref, picked_ref, router_ref, gain_ref, *outs
):
    y_ref, chosen_ref, grad_ref, weight_ref, de_ref, a_ref = outs
    e = part_ref[...].astype(f32) + recv_ref[...].astype(f32) + bias_ref[...]
    y = (h_ref[...] + e).astype(bf16)
    y_ref[...] = y
    picked = picked_ref[0]
    places = lax.broadcasted_iota(jnp.int32, (picked.shape[0], y.shape[0]), 1) == picked
    onehot = places.astype(bf16)
    chosen, grad = mm(onehot, y), mm(onehot, cot_ref[...])
    weight = jax.nn.sigmoid(jnp.sum(chosen * router_ref[...], axis=1, keepdims=True))
    chosen_ref[...] = chosen.astype(bf16)
    grad_ref[...] = grad.astype(bf16)
    weight_ref[...] = weight
    de_ref[...] = (weight * grad).astype(bf16)
    a_ref[...] = (chosen * inverse_rms(chosen) * gain_ref[...]).astype(bf16)


def choose_rows(h, part, recv, bias, cot, picked, router, gain):
    micro, count = picked.shape
    tokens = h.shape[0]
    down = pl.BlockSpec((tokens // micro, D), lambda i: (i, 0))
    row = pl.BlockSpec((1, D), lambda i: (0, 0))
    few = lambda width: pl.BlockSpec((count, width), lambda i: (i, 0))
    rows = micro * count
    return tiled_call(
        choose_kernel,
        micro,
        [
            ((tokens, D), bf16, down),
            ((rows, D), bf16, few(D)),
            ((rows, D), bf16, few(D)),
            ((rows, 1), f32, few(1)),
            ((rows, D), bf16, few(D)),
            ((rows, D), bf16, few(D)),
        ],
        [
            (h, down),
            (part, down),
            (recv, down),
            (bias, row),
            (cot, down),
            (picked[:, :, None], pl.BlockSpec((1, count, 1), lambda i: (i, 0, 0))),
            (router, row),
            (gain, row),
        ],
    )


def last_kernel(part_ref, recv_ref, x_ref, gain_ref, sum_ref, dx_ref):
    da = part_ref[...].astype(f32) + recv_ref[...].astype(f32)
    x = x_ref[...].astype(f32)
    inverse = inverse_rms(x)
    unit = x * inverse
    dx_ref[...] = (sum_ref[...] + norm_back(da, unit, inverse, gain_ref[...])).astype(bf16)


def last_rows(part, recv, x, gain, total, step=256):
    tokens = x.shape[0]
    down = pl.BlockSpec((step, D), lambda i: (i, 0))
    row = pl.BlockSpec((1, D), lambda i: (0, 0))
    return tiled_call(
        last_kernel,
        tokens // step,
        [((tokens, D), bf16, down)],
        [(part, down), (recv, down), (x, down), (gain, row), (total, down)],
    )[0]


def up_kernel(m_ref, w_ref, b_ref, g_ref, slope_ref):
    u = mm(m_ref[...], w_ref[...]) + b_ref[...]
    bell = 0.5 * (1.0 + lax.erf(u * root_half))
    g_ref[...] = (u * bell).astype(bf16)
    slope_ref[...] = (bell + u * jnp.exp(-0.5 * u * u) * inverse_root_two_pi).astype(bf16)


def up_product(m, w, bias, step=512):
    tokens, width = m.shape[0], w.shape[1]
    across = pl.BlockSpec((tokens, step), lambda i: (0, i))
    return tiled_call(
        up_kernel,
        width // step,
        [((tokens, width), bf16, across)] * 2,
        [
            (m, resident(m.shape)),
            (w, pl.BlockSpec((w.shape[0], step), lambda i: (0, i))),
            (bias, pl.BlockSpec((1, step), lambda i: (0, i))),
        ],
    )


def down_grad_kernel(me_ref, g_ref, d_ref, *outs):
    product = mm_rows(g_ref[...], d_ref[...]).astype(bf16)
    for i, out in enumerate(outs):

        @pl.when(pl.program_id(0) == i)
        def _(out=out):
            out[...] = product.reshape(out.shape)


def down_grad(me, depth, chips, g, d):
    tokens, width = g.shape
    units = width // (4 * depth)
    return pl.pallas_call(
        down_grad_kernel,
        grid_spec=pltpu.PrefetchScalarGridSpec(
            num_scalar_prefetch=1,
            grid=(len(chips),),
            in_specs=[
                pl.BlockSpec((tokens, width // 4), lambda i, me: (0, me[0] ^ (i + chips[0]))),
                pl.BlockSpec(d.shape, lambda i, me: (0, 0), pipeline_mode=pl.Buffered(1)),
            ],
            out_specs=[pl.BlockSpec((depth, units, D), lambda i, me: (0, 0, 0))] * len(chips),
        ),
        out_shape=[jax.ShapeDtypeStruct((depth, units, D), bf16)] * len(chips),
        compiler_params=pltpu.CompilerParams(vmem_limit_bytes=20 << 20),
        cost_estimate=light,
    )(jnp.reshape(me, (1,)), g, d)


def norm_back_kernel(
    part_ref, recv_ref, h_ref, gain_ref, gy_ref, w_ref, dz_ref, sum_ref, do_ref, gain_g, bias_g
):
    dm = part_ref[...].astype(f32) + recv_ref[...].astype(f32)
    h, gy = h_ref[...], gy_ref[...].astype(f32)
    inverse = inverse_rms(h)
    unit = h * inverse
    dh = norm_back(dm, unit, inverse, gain_ref[...])
    total = gy + dh
    dz = total.astype(bf16)
    sum_ref[...] = total
    dz_ref[...] = dz
    do_ref[...] = mm_t(dz, w_ref[...]).astype(bf16)
    grads = jnp.sum(dm * unit, axis=0, keepdims=True), jnp.sum(gy, axis=0, keepdims=True)

    @pl.when(pl.program_id(0) == 0)
    def _():
        gain_g[...], bias_g[...] = grads

    @pl.when(pl.program_id(0) > 0)
    def _():
        gain_g[...] += grads[0]
        bias_g[...] += grads[1]


def norm_back_product(part, recv, h, gain, gy, w_out, step=256):
    tokens = part.shape[0]
    down = lambda width: pl.BlockSpec((step, width), lambda i: (i, 0))
    row = pl.BlockSpec((1, D), lambda i: (0, 0))
    return tiled_call(
        norm_back_kernel,
        tokens // step,
        [
            ((tokens, D), bf16, down(D)),
            ((tokens, D), f32, down(D)),
            ((tokens, HALF), bf16, down(HALF)),
            ((1, D), f32, row),
            ((1, D), f32, row),
        ],
        [
            (part, down(D)),
            (recv, down(D)),
            (h, down(D)),
            (gain, row),
            (gy, down(D)),
            (w_out, resident(w_out.shape)),
        ],
    )


def take_rows_kernel(picked_ref, *refs):
    sources, (first_out, second_out, done_ref) = refs[1:3], refs[3:]
    picked = picked_ref[0]
    length = sources[0].shape[0]
    places = lax.broadcasted_iota(jnp.int32, (picked.shape[0], length), 1) == picked
    onehot = places.astype(bf16)
    for source, out in zip(sources, (first_out, second_out)):
        out[...] = mm(onehot, source[...]).astype(bf16)
    done_ref[...] = jnp.zeros_like(done_ref)


def take_rows(picked, earlier, *sources):
    micro, count = picked.shape
    width = sources[0].shape[1]
    length = sources[0].shape[0] // micro
    few = ((micro * count, width), bf16, pl.BlockSpec((count, width), lambda i: (i, 0)))
    corner = pl.BlockSpec((1, 8, LANES), lambda i: (0, 0, 0))
    return tiled_call(
        take_rows_kernel,
        micro,
        [few, few, (*mark, pl.BlockSpec(mark[0], lambda i: (0, 0)))],
        [
            (picked[:, :, None], pl.BlockSpec((1, count, 1), lambda i: (i, 0, 0))),
            (earlier, corner),
        ]
        + [(v, pl.BlockSpec((length, width), lambda i: (i, 0))) for v in sources],
    )


def mlp_pre_kernel(d_ref, wd_ref, slope_ref, wu_ref, du_ref, dm_ref, done_ref, acc):
    du = (mm_t(d_ref[...], wd_ref[...]) * slope_ref[...].astype(f32)).astype(bf16)
    du_ref[...] = du
    part = mm_t(du, wu_ref[...])
    step, last = pl.program_id(0), pl.num_programs(0) - 1

    @pl.when(step == 0)
    def _():
        acc[...] = part

    @pl.when((step > 0) & (step < last))
    def _():
        acc[...] += part

    @pl.when(step == last)
    def _():
        dm_ref[...] = (acc[...] + part).astype(bf16)
        done_ref[...] = jnp.zeros_like(done_ref)


def mlp_pre(d, w_down, slope, w_up, step=512):
    tokens, width = slope.shape
    across = pl.BlockSpec((tokens, step), lambda i: (0, i))
    return tiled_call(
        mlp_pre_kernel,
        width // step,
        [
            ((tokens, width), bf16, across),
            ((tokens, D), bf16, pl.BlockSpec((tokens, D), lambda i: (0, 0))),
            (*mark, pl.BlockSpec(mark[0], lambda i: (0, 0))),
        ],
        [
            (d, resident(d.shape)),
            (w_down, pl.BlockSpec((step, D), lambda i: (i, 0))),
            (slope, across),
            (w_up, pl.BlockSpec((D, step), lambda i: (0, i))),
        ],
        [pltpu.VMEM((tokens, D), f32)],
    )


def down_rest_kernel(me_ref, gy_ref, g_ref, *refs):
    ins, outs = refs[:4], refs[4:]
    more = mm_rows(g_ref[...], gy_ref[...])
    for j in range(4):

        @pl.when(pl.program_id(0) == j)
        def _(j=j):
            total = (ins[j][...].astype(f32) + more.reshape(ins[j].shape)).astype(bf16)
            half = total.shape[0] // 2
            outs[2 * j][...] = total[:half]
            outs[2 * j + 1][...] = total[half:]


def down_rest(me, gy, g, pre):
    rows, width = g.shape
    fixed = lambda shape: pl.BlockSpec(
        shape, lambda i, me: (0,) * len(shape), pipeline_mode=pl.Buffered(1)
    )
    half = (pre[0].shape[0] // 2, *pre[0].shape[1:])
    found = pl.pallas_call(
        down_rest_kernel,
        grid_spec=pltpu.PrefetchScalarGridSpec(
            num_scalar_prefetch=1,
            grid=(4,),
            in_specs=[
                fixed(gy.shape),
                pl.BlockSpec((rows, width // 4), lambda i, me: (0, me[0] ^ i)),
            ]
            + [fixed(v.shape) for v in pre],
            out_specs=[pl.BlockSpec(half, lambda i, me: (0, 0, 0))] * 8,
        ),
        out_shape=[jax.ShapeDtypeStruct(half, bf16)] * 8,
        compiler_params=pltpu.CompilerParams(vmem_limit_bytes=16 << 20),
        cost_estimate=light,
    )(jnp.reshape(me, (1,)), gy, g, *pre)
    return pairs_of(found)


def up_rest_kernel(
    me_ref, picked_ref, gy_ref, wd_ref, slope_ref, du_ref, m_ref, wu_ref, dm_in, *refs
):
    outs, (dm_ref, gb_ref, du, acc, gw) = refs[:8], refs[8:]
    half = gw.shape[0] // 2
    micro, count = picked_ref.shape[0], picked_ref.shape[2]
    length = dm_in.shape[0] // micro
    rows = (mm_t(gy_ref[...], wd_ref[...]) * slope_ref[...].astype(f32)).astype(bf16)
    for s in range(micro):
        at = slice(s * length, (s + 1) * length)
        places = lax.broadcasted_iota(jnp.int32, (length, count), 0) == picked_ref[s]
        more = mm(places.astype(bf16), rows[s * count : (s + 1) * count])
        du[at] = du_ref[at] + more.astype(bf16)
    gb_ref[...] = jnp.sum(du[...].astype(f32), axis=0, keepdims=True)
    gw[...] = mm_rows(m_ref[...], du[...]).astype(bf16).reshape(gw.shape)
    for j in range(4):
        outs[2 * j][...] = gw[:half, me_ref[0] ^ j]
        outs[2 * j + 1][...] = gw[half:, me_ref[0] ^ j]
    part = mm_t(rows, wu_ref[...])

    @pl.when(pl.program_id(0) == 0)
    def _():
        acc[...] = part

    @pl.when(pl.program_id(0) > 0)
    def _():
        acc[...] += part

    @pl.when(pl.program_id(0) == pl.num_programs(0) - 1)
    def _():
        for s in range(micro):
            at = slice(s * length, (s + 1) * length)
            cut = acc[s * count : (s + 1) * count]
            dm_ref[at] = put_rows(dm_in[at], cut, picked_ref[s], length).astype(bf16)


def up_rest(me, depth, picked, gy, w_down, slope, du, m, w_up, dm, step=512):
    tokens, width = du.shape
    rows = D // (4 * depth)
    tall = lambda height: pl.BlockSpec((height, step), lambda i: (0, i))
    once = lambda v: pl.BlockSpec(v.shape, lambda i: (0,) * v.ndim, pipeline_mode=pl.Buffered(1))
    block = pl.BlockSpec((depth // 2, rows, step), lambda i: (0, 0, i))
    return tiled_call(
        up_rest_kernel,
        width // step,
        [((depth // 2, rows, width), bf16, block)] * 8
        + [
            ((tokens, D), bf16, pl.BlockSpec((tokens, D), lambda i: (0, 0))),
            ((1, width), f32, tall(1)),
        ],
        [
            (jnp.reshape(me, (1,)), pl.BlockSpec(memory_space=pltpu.SMEM)),
            (picked, once(picked)),
            (gy, once(gy)),
            (w_down, pl.BlockSpec((step, D), lambda i: (i, 0))),
            (slope, tall(gy.shape[0])),
            (du, tall(tokens)),
            (m, once(m)),
            (w_up, tall(D)),
            (dm, once(dm)),
        ],
        [
            pltpu.VMEM((tokens, step), bf16),
            pltpu.VMEM((gy.shape[0], D), f32),
            pltpu.VMEM((depth, 4, rows, step), bf16),
        ],
    )


def sum_both_kernel(*refs):
    out_ref = refs[-1]
    for h in range(2):
        down, up = refs[3 * h : 3 * h + 3], refs[6 + 3 * h : 9 + 3 * h]
        depth, rows = up[0].shape[:2]
        at = slice(h * depth, (h + 1) * depth)
        add = lambda these: sum(ref[...].astype(f32) for ref in these).astype(bf16)
        out_ref[at, :rows] = add(up)
        total = add(down)
        out_ref[at, rows:, :D] = total[:, :rows]
        out_ref[at, rows:, D:] = total[:, rows:]


def order_rows_kernel(me_ref, *refs):
    for j, ref in enumerate(refs[:-1]):
        refs[-1][me_ref[0] ^ j] = ref[...]


def halves_kernel(*refs):
    out_ref = refs[-1]
    half = refs[0].shape[0]
    for h in range(2):
        total = sum(ref[...].astype(f32) for ref in refs[3 * h : 3 * h + 3])
        out_ref[h * half : (h + 1) * half] = total.astype(bf16)


def order_mlp_kernel(me_ref, u0, u1, u2, u3, d_ref, out_ref):
    rows, width = u0.shape
    units = d_ref.shape[0]
    for j, ref in enumerate((u0, u1, u2, u3)):
        start = pl.multiple_of((me_ref[0] ^ j) * rows, rows)
        out_ref[pl.ds(start, rows)] = ref[...]
    for k in range(2):
        low = 4 * rows + k * units
        out_ref[low : low + units] = d_ref[:, k * width : (k + 1) * width]


def order_columns_kernel(me_ref, *refs):
    out_ref = refs[-1]
    width = refs[0].shape[1]
    for j, ref in enumerate(refs[:-1]):
        start = pl.multiple_of((me_ref[0] ^ j) * width, width)
        out_ref[:, pl.ds(start, width)] = ref[...]


def routed_attn_kernel(count, a_ref, seg_col_ref, seg_row_ref, w_ref, qkv_ref, o_ref):
    weights = w_ref[:, :, :, : 3 * HALF].reshape(D, 3 * HALF)
    qkv_ref[...] = mm(a_ref[...], weights).astype(bf16)
    attend_kernel(count, HALF // LANES, count, qkv_ref, seg_col_ref, seg_row_ref, o_ref)


def routed_hidden_kernel(part_ref, recv_ref, chosen_ref, gain_ref, m_ref):
    z = part_ref[...].astype(f32) + recv_ref[...].astype(f32)
    h = chosen_ref[...].astype(f32) + z
    m_ref[...] = (h * inverse_rms(h) * gain_ref[...]).astype(bf16)


def routed_mlp_kernel(core_ref, m0, m1, m2, m3, d0, d1, d2, d3, w_ref, b_ref, _, *rest):
    g_ref, du_ref, keep_ref, send_ref, gb_ref, m_ref, d_ref = rest
    rows = m0.shape[0]
    for j, (m, d) in enumerate(zip((m0, m1, m2, m3), (d0, d1, d2, d3))):
        m_ref[j * rows : (j + 1) * rows] = m[...]
        d_ref[j * rows : (j + 1) * rows] = d[...]
    hidden = w_ref.shape[2]
    own_rows = D // w_ref.shape[0]
    units = (w_ref.shape[1] - own_rows) // 2
    w_up = w_ref[:, :own_rows].reshape(D, hidden)
    w_down = [
        w_ref[:, own_rows + k * units : own_rows + (k + 1) * units].reshape(hidden, hidden)
        for k in range(2)
    ]
    u = mm(m_ref[...], w_up) + b_ref[...]
    bell = 0.5 * (1.0 + lax.erf(u * root_half))
    g = (u * bell).astype(bf16)
    slope = bell + u * jnp.exp(-0.5 * u * u) * inverse_root_two_pi
    dg = mm_t(d_ref[:, :hidden], w_down[0]) + mm_t(d_ref[:, hidden:], w_down[1])
    du = (dg * slope).astype(bf16)
    g_ref[...] = g
    du_ref[...] = du
    gb_ref[...] = jnp.sum(du.astype(f32), axis=0, keepdims=True)
    e = jnp.concatenate([mm(g, w).astype(bf16) for w in w_down], axis=1).reshape(keep_ref.shape)
    dm = mm_t(du, w_up).astype(bf16).reshape(keep_ref.shape)

    @pl.when(core_ref[0] == 0)
    def _():
        keep_ref[...] = e
        send_ref[...] = dm

    @pl.when(core_ref[0] != 0)
    def _():
        keep_ref[...] = dm
        send_ref[...] = e


def routed_grads_kernel(g_ref, d_ref, m_ref, du_ref, out_ref, done_ref):
    depth, all_rows, hidden = out_ref.shape
    rows = D // depth
    units = (all_rows - rows) // 2
    up = mm_rows(m_ref[...], du_ref[...]).astype(bf16)
    out_ref[:, :rows] = up.reshape(depth, rows, hidden)
    for k in range(2):
        down = mm_rows(g_ref[...], d_ref[:, k * hidden : (k + 1) * hidden]).astype(bf16)
        low = rows + k * units
        out_ref[:, low : low + units] = down.reshape(depth, units, hidden)
    done_ref[...] = jnp.zeros_like(done_ref)


def add_parts_kernel(a_ref, b_ref, _, *outs):
    for j, out in enumerate(outs):
        out[...] = (a_ref[j].astype(f32) + b_ref[j].astype(f32)).astype(bf16)


def add_kernel(*refs):
    refs[-1][...] = sum(ref[...].astype(f32) for ref in refs[:-2]).astype(bf16)


def routed_back_kernel(count, core_ref, *refs):
    ins, outs = refs[:14], refs[14:]
    total, crossed, bias, z_ref, z_recv, chosen_ref, chosen_g, weight_ref, gain = ins[:9]
    wo_ref, wq_ref, qkv_ref, seg_col_ref, seg_row_ref = ins[9:]
    delta_ref, logit_ref, dh_ref, dz_ref, gain_g, dqkv_ref, da_ref, do_scr = outs
    first = core_ref[0] == 0
    a, b = total[...].astype(f32), crossed[...].astype(f32)
    e = jnp.where(first, a, b) + bias[...]
    dm = jnp.where(first, b, a)
    z = z_ref[...].astype(f32) + z_recv[...].astype(f32)
    delta = z + e
    delta_ref[...] = delta
    weight, grad = weight_ref[...], chosen_g[...].astype(f32)
    logit_ref[...] = jnp.sum(grad * delta, axis=1, keepdims=True) * weight * (1.0 - weight)
    h = chosen_ref[...].astype(f32) + z
    inverse = inverse_rms(h)
    unit = h * inverse
    gain_g[...] = jnp.sum(dm * unit, axis=0, keepdims=True)
    dh = norm_back(dm, unit, inverse, gain[...])
    dh_ref[...] = dh
    dz = (weight * grad + dh).astype(bf16)
    dz_ref[...] = dz
    do_scr[...] = mm_t(dz, wo_ref[...]).astype(bf16)
    attend_back_kernel(
        count, HALF // LANES, count, qkv_ref, seg_col_ref, seg_row_ref, do_scr, dqkv_ref
    )
    weights = wq_ref[:, :, :, : 3 * HALF].reshape(D, 3 * HALF)
    da_ref[...] = mm_t(dqkv_ref[...], weights).astype(bf16)


def put_rows(base, rows, picked, length):
    places = lax.broadcasted_iota(jnp.int32, (length, picked.shape[1]), 0) == picked
    onehot = places.astype(bf16)
    high = rows.astype(bf16)
    low = (rows - high.astype(f32)).astype(bf16)
    return base.astype(f32) + (mm(onehot, high) + mm(onehot, low))


def routed_out_kernel(
    part_ref, recv_ref, chosen_ref, gain, dh_ref, logit_ref, router, picked_ref, cot_ref, *outs
):
    gy_ref, gy_rows, gain_g, router_g = outs
    own = part_ref[...].astype(f32)
    da = own + recv_ref[...].astype(f32)
    chosen, logit = chosen_ref[...].astype(f32), logit_ref[...]
    inverse = inverse_rms(chosen)
    unit = chosen * inverse
    gain_g[...] = jnp.sum(own * unit, axis=0, keepdims=True)
    router_g[...] = jnp.sum(logit * chosen, axis=0, keepdims=True)
    rows = dh_ref[...] + norm_back(da, unit, inverse, gain[...]) + logit * router[...]
    micro, count = picked_ref.shape[0], picked_ref.shape[2]
    length = cot_ref.shape[0] // micro
    for s in range(micro):
        at = slice(s * length, (s + 1) * length)
        cut = rows[s * count : (s + 1) * count]
        gy = put_rows(cot_ref[at], cut, picked_ref[s], length).astype(bf16)
        gy_ref[at] = gy
        places = lax.broadcasted_iota(jnp.int32, (length, count), 0) == picked_ref[s]
        gy_rows[s * count : (s + 1) * count] = mm_rows(places.astype(bf16), gy).astype(bf16)


def routed_sum_kernel(y_ref, delta_ref, weight_ref, picked_ref, out_ref):
    rows = weight_ref[...] * delta_ref[...]
    micro, count = picked_ref.shape[0], picked_ref.shape[2]
    length = y_ref.shape[0] // micro
    for s in range(micro):
        at = slice(s * length, (s + 1) * length)
        cut = rows[s * count : (s + 1) * count]
        out_ref[at] = put_rows(y_ref[at], cut, picked_ref[s], length).astype(bf16)


def finish_kernel(core_ref, keep_ref, recv_ref, qkv_ref, out_ref):
    keep, recv = keep_ref[...].astype(f32), recv_ref[:, : 4 * HALF].astype(f32)
    first = core_ref[0] == 0
    low, high = jnp.where(first, keep, recv), jnp.where(first, recv, keep)
    for t in range(3):
        qkv_ref[:, t * D : t * D + HALF] = low[:, t * HALF : (t + 1) * HALF]
        qkv_ref[:, t * D + HALF : (t + 1) * D] = high[:, t * HALF : (t + 1) * HALF]
    out_ref[:, :HALF] = low[:, 3 * HALF : 4 * HALF]
    out_ref[:, HALF:] = high[:, 3 * HALF : 4 * HALF]


def shards(
    boundary_in,
    segments,
    routed,
    gain_attn,
    w_qkv,
    w_out,
    gain_mlp,
    w_up,
    b_up,
    w_down,
    b_down,
    router,
):
    core = lax.axis_index("section")
    first = core == 0
    me = 2 * lax.axis_index("y") + lax.axis_index("x")
    depth = lax.axis_size("z")
    rows = w_qkv.shape[1]
    dp = 4 * depth
    units = w_up.shape[2] // dp
    half_units = units // 2
    micro, length = boundary_in.shape[1], boundary_in.shape[3]
    tokens = micro * length

    qkv_halves = w_qkv[0].astype(bf16).reshape(rows, 3, 2, HALF)
    out_halves = w_out[0].astype(bf16).reshape(rows, 2, HALF)
    up_halves = w_up[0].astype(bf16).reshape(rows, depth, 4, 2, half_units)
    down_halves = w_down[0].astype(bf16).reshape(2, half_units, D)
    bias_cols = half_units // rows
    bias_halves = b_up[0].astype(bf16).reshape(2, bias_cols, rows)
    column = lambda v: jnp.pad(v.astype(bf16), (0, rows - v.shape[0]))[:, None]
    small = jnp.concatenate(
        [column(gain_attn[0]), column(gain_mlp[0]), column(b_down[0]), column(router)], axis=1
    )

    def half(h):
        pick = lambda v, axis: lax.dynamic_index_in_dim(v, h, axis=axis, keepdims=False)
        strip = jnp.concatenate([small, pick(bias_halves, 0).T], axis=1)
        strip = jnp.pad(strip, ((0, 0), (0, 8 - strip.shape[1])))
        none = jnp.zeros_like(strip)
        strip = jnp.concatenate(
            [jnp.where(first, strip, none), jnp.where(first, none, strip)], axis=1
        )
        strip = jnp.pad(strip, ((0, 0), (0, LANES - 16)))
        attn = jnp.concatenate(
            [pick(qkv_halves, 2).reshape(rows, 3 * HALF), pick(out_halves, 1), strip], axis=1
        )
        up = pick(up_halves, 3).transpose(0, 2, 1, 3).reshape(rows, D * 2)
        return attn, up, pick(down_halves, 0)

    kept, sent = half(core), half(1 - core)
    came = tuple(swap(v, "section") for v in sent)
    width = 4 * HALF
    shard0 = [jnp.where(first, k, r) for k, r in zip(kept, came)]
    shard1 = [jnp.where(first, r, k) for k, r in zip(kept, came)]
    strip = kept[0][:, width:] + came[0][:, width:]
    shard0[0] = jnp.concatenate([shard0[0][:, :width], strip], axis=1)
    shard1[0] = shard1[0][:, :width]

    mine = boundary_in[0, :, 0].reshape(tokens, D)
    other = swap(mine, "section")
    x_b = jnp.where(first, mine, other)
    cot_b = jnp.where(first, other, mine)
    seg = segments[:, 0]
    picked = routed[:, 0]
    count = picked.shape[1]
    chosen_rows = micro * count

    def whole_out(w_o):
        w_o = w_o.reshape(D, HALF)
        own = lax.dynamic_slice_in_dim(w_o, core * HALF, HALF, axis=0)
        recv = swap(lax.dynamic_slice_in_dim(w_o, (1 - core) * HALF, HALF, axis=0), "section")
        return jnp.concatenate([jnp.where(first, own, recv), jnp.where(first, recv, own)], axis=1)

    halfway = depth // 2

    own_q = over_z(shard0[0])
    rest = [shard1[0]] + [to_plane(shard1[0], j) for j in (1, 2, 3)]
    (rest,) = whole(order_rows_kernel, [((4, rows, width), bf16)], [me], rest)
    hidden = depth * half_units
    pick_up = lambda j: lax.dynamic_slice_in_dim(shard1[1], (me ^ j) * hidden, hidden, axis=1)
    mlp = [pick_up(0)] + [to_plane(pick_up(j), j) for j in (1, 2, 3)]
    mlp_rows = 4 * rows + 2 * half_units
    (mlp,) = whole(order_mlp_kernel, [((mlp_rows, hidden), bf16)], [me], [*mlp, shard1[2]])
    onehot = picked[:, :, None] == lax.broadcasted_iota(jnp.int32, (micro, count, length), 2)
    seg1 = jnp.sum(jnp.where(onehot, seg[:, None, :], 0), axis=2)
    seg1_col, seg1_row = seg1[:, :, None], seg1[:, None, :]
    is_routed = jnp.any(onehot, axis=1).reshape(tokens, 1)
    cot_other = jnp.where(is_routed, jnp.zeros_like(cot_b), cot_b)
    own_q, rest, mlp, shard_u = fence(own_q, rest, mlp, shard0[1])

    px_q, py_q = swap(own_q, "x"), swap(own_q, "y")
    own_u = over_z(shard_u)
    own_q, px_q, py_q, own_u, shard_d, x_b, cot_b, cot_other, seg1_col, seg1_row = fence(
        own_q, px_q, py_q, own_u, shard0[2], x_b, cot_b, cot_other, seg1_col, seg1_row
    )
    pd_q, px_u = swap(px_q, "y"), swap(own_u, "x")
    own_d = over_z(shard_d)
    own_q, px_q, py_q, pd_q, own_u, px_u, own_d, rest = fence(
        own_q, px_q, py_q, pd_q, own_u, px_u, own_d, rest
    )
    py_u = swap(own_u, "y")
    px_d, py_d = swap(own_d, "x"), swap(own_d, "y")
    w_r1 = over_z(rest)

    spans_all = [(j, 0, depth) for j in range(4)]
    w_o0, strip = place(
        me, [own_q, px_q, py_q, pd_q], spans_all, ((3 * HALF, width), (width, width + LANES))
    )
    w_o0 = whole_out(w_o0)
    choose = (
        lax.broadcasted_iota(jnp.int32, (16, LANES), 0)
        == lax.broadcasted_iota(jnp.int32, (16, LANES), 1)
    ).astype(bf16)
    vectors = mm_t(choose, strip.reshape(D, LANES))
    gain_attn0, gain_mlp0, b_down0 = vectors[0:1], vectors[1:2], vectors[2:3]
    gain_attn1, gain_mlp1, b_down1 = vectors[8:9], vectors[9:10], vectors[10:11]
    router_full = jnp.concatenate(
        [vectors[b].reshape(dp, rows)[:, : rows // 2].reshape(1, HALF) for b in (3, 11)], axis=1
    )
    biases = lambda b: (
        vectors[b : b + bias_cols].reshape(bias_cols, depth, 4, rows).transpose(2, 1, 0, 3)
    )
    bias_up0 = biases(4).reshape(1, 2 * D)
    bias_up1 = lax.dynamic_index_in_dim(biases(12), me, axis=0, keepdims=False)
    bias_up1 = bias_up1.reshape(1, hidden)
    w_q0, a0, qkv0 = whole(
        functools.partial(qkv_kernel, spans_all, 256),
        [
            ((depth, 4, rows, 3 * HALF), bf16),
            ((tokens, D), bf16),
            ((tokens, 3 * HALF), bf16),
        ],
        [me],
        [x_b, gain_attn0, own_q, px_q, py_q, pd_q],
        [pltpu.SemaphoreType.DMA((4,))],
        anywhere=4,
    )
    w_q0 = w_q0.reshape(D, 3 * HALF)
    o0, z_part = attention_call(attend_out_kernel, seg, [qkv0], w_o0, HALF)
    o0, z_part, own_u, px_u, py_u, px_d, mlp = fence(o0, z_part, own_u, px_u, py_u, px_d, mlp)
    w_m1 = over_z(mlp)

    pd_u = swap(py_u, "x")
    pd_d0 = swap(px_d[:halfway], "y")
    h0, m0 = hidden_rows(x_b, z_part, swap(z_part, "section"), gain_mlp0)
    m0, pd_u, py_d, bias_up0, bias_up1, router_full = fence(
        m0, pd_u, py_d, bias_up0, bias_up1, router_full
    )

    pd_d1 = swap(py_d[halfway:], "x")
    (w_u0,) = place(me, [own_u, px_u, py_u, pd_u], spans_all, ((0, D * 2),))
    w_u0 = w_u0.reshape(D, D * 2)
    g0, slope0 = up_product(m0, w_u0, bias_up0)
    g0, pd_d0, pd_d1, w_r1 = fence(g0, pd_d0, pd_d1, w_r1)

    spans_cut = spans_all[:3] + [(3, 0, halfway), (3, halfway, depth)]
    (w_d0,) = place(
        me, [own_d, px_d, py_d, pd_d0, pd_d1], spans_cut, ((0, D),), plane_first=True
    )
    w_d0 = w_d0.reshape(D * 2, D)
    e_part = down_product(g0, w_d0)
    w_o1 = whole_out(w_r1[..., 3 * HALF :])

    y0_b, chosen, grad_chosen, weight, de1, a1 = choose_rows(
        h0, e_part, swap(e_part, "section"), b_down0, cot_b, picked, router_full, gain_attn1
    )
    de_all = [de1] + [to_plane(de1, j) for j in (1, 2, 3)]
    qkv1, o1 = whole(
        functools.partial(routed_attn_kernel, count),
        [((chosen_rows, 3 * HALF), bf16), ((chosen_rows, HALF), bf16)],
        [],
        [a1, seg1_col, seg1_row, w_r1],
    )
    z_part = mm(o1, w_o1).astype(bf16)
    z_recv = swap(z_part, "section")
    (m1,) = whole(
        routed_hidden_kernel,
        [((chosen_rows, D), bf16)],
        [],
        [z_part, z_recv, chosen, gain_mlp1],
    )
    m_all = [m1] + [to_plane(m1, j) for j in (1, 2, 3)]
    pre_du, pre_dm, pre_done = mlp_pre(cot_other, w_d0, slope0, w_u0)
    g1, du1, keep, send, gb_u1, m_rows, de_rows = whole(
        routed_mlp_kernel,
        [((4 * chosen_rows, hidden), bf16)] * 2
        + [((4, chosen_rows, D), bf16)] * 2
        + [((1, hidden), f32)]
        + [((4 * chosen_rows, D), bf16)] * 2,
        [core],
        [*m_all, *de_all, w_m1, bias_up1, pre_done],
    )
    plus = lambda *terms: sum(t.astype(f32) for t in terms).astype(bf16)
    others = swap(send, "section")
    gw_m1, grads_done = whole(
        routed_grads_kernel,
        [((depth, mlp_rows, hidden), bf16), mark],
        [],
        [g1, de_rows, m_rows, du1],
    )
    plus = lambda *terms: sum(t.astype(f32) for t in terms).astype(bf16)
    r_m1 = reduce_z(gw_m1)
    summed = whole(
        add_parts_kernel, [((chosen_rows, D), bf16)] * 4, [], [keep, others, grads_done]
    )
    terms = [summed[0]] + [to_plane(summed[j], j) for j in (1, 2, 3)]
    pre_d = down_grad(me, depth, (0, 1, 2, 3), g0, cot_other)
    g_rows, slope_rows, rows_done = take_rows(picked, pre_d[0], g0, slope0)
    (total,) = whole(add_kernel, [((chosen_rows, D), bf16)], [], [*terms, rows_done])
    crossed = swap(total, "section")

    delta, grad_logit, dh1, dz1, gg_mlp1, dqkv1, da_part = whole(
        functools.partial(routed_back_kernel, count),
        [
            ((chosen_rows, D), f32),
            ((chosen_rows, 1), f32),
            ((chosen_rows, D), f32),
            ((chosen_rows, D), bf16),
            ((1, D), f32),
            ((chosen_rows, 3 * HALF), bf16),
            ((chosen_rows, D), bf16),
        ],
        [core],
        [
            total,
            crossed,
            b_down1,
            z_part,
            z_recv,
            chosen,
            grad_chosen,
            weight,
            gain_mlp1,
            w_o1,
            w_r1,
            qkv1,
            seg1_col,
            seg1_row,
        ],
        [pltpu.VMEM((chosen_rows, HALF), bf16)],
    )

    def out_by_columns(grad):
        own = lax.dynamic_slice_in_dim(grad, core * HALF, HALF, axis=1)
        recv = swap(lax.dynamic_slice_in_dim(grad, (1 - core) * HALF, HALF, axis=1), "section")
        return jnp.concatenate([jnp.where(first, own, recv), jnp.where(first, recv, own)], axis=0)

    gw_o1 = out_by_columns(mm_rows(o1, dz1).astype(bf16))
    gy0_b, gy_rows, gg_attn1, grad_router = whole(
        routed_out_kernel,
        [((tokens, D), bf16), ((chosen_rows, D), bf16), ((1, D), f32), ((1, D), f32)],
        [],
        [
            da_part,
            swap(da_part, "section"),
            chosen,
            gain_attn1,
            dh1,
            grad_logit,
            router_full,
            picked[:, None, :],
            cot_b,
        ],
    )
    send_diagonal = lambda grads: [swap(grads[3][0], "x"), swap(grads[3][1], "y")]
    send_far = lambda grads: [swap(grads[1][0], "x"), swap(grads[2][1], "y")]
    near = lambda grads, diag: [plus(grads[2][0], diag[0]), plus(grads[1][1], diag[1])]
    send_near = lambda sums: [swap(sums[0], "y"), swap(sums[1], "x")]
    parts = lambda grads, near, far: [
        v for h in range(2) for v in (grads[0][h], near[h], far[h])
    ]

    gw_d0 = down_rest(me, gy_rows, g_rows, pre_d)
    gw_d0, gy_rows = fence(gw_d0, gy_rows)
    diag_d, far_d = send_diagonal(gw_d0), send_far(gw_d0)
    attn1 = attn_grad(me, False, depth, a1, dqkv1, gw_o1)
    *gw_u0, dm_part, gb_u0 = up_rest(
        me,
        depth,
        picked[:, None, :],
        gy_rows,
        w_d0,
        slope_rows,
        pre_du,
        m0,
        w_u0,
        pre_dm,
    )
    diag_d, far_d, gw_u0, dm_part, gy0_b, attn1 = fence(
        diag_d, far_d, pairs_of(gw_u0), dm_part, gy0_b, attn1
    )

    r_a1 = reduce_z(attn1)
    diag_u = send_diagonal(gw_u0)
    near_d = send_near(near(gw_d0, diag_d))
    dz0, gy_dh0, do0, gg_mlp0, g_down0 = norm_back_product(
        dm_part, swap(dm_part, "section"), h0, gain_mlp0, gy0_b, w_o0
    )
    gw_o0 = out_by_columns(mm_rows(o0, dz0).astype(bf16))
    dqkv0, da_part, gg_attn0 = attention_call(
        attend_back_out_kernel, seg, [qkv0, do0, x_b], w_q0, 3 * HALF, sums=1
    )
    diag_u, near_d, dqkv0, da_part, gw_o0 = fence(diag_u, near_d, dqkv0, da_part, gw_o0)

    far_u = send_far(gw_u0)
    near_u = send_near(near(gw_u0, diag_u))
    here = lax.broadcasted_iota(jnp.int32, (depth, 4, bias_cols, rows), 1) == me
    gb_u1 = gb_u1.reshape(depth, 1, bias_cols, rows)
    gb_u1 = jnp.where(here, gb_u1, 0.0).transpose(2, 0, 1, 3).reshape(bias_cols, D)
    gb_u0 = gb_u0.reshape(4, depth, bias_cols, rows).transpose(2, 1, 0, 3).reshape(bias_cols, D)
    router_rows = jnp.pad(
        grad_router.reshape(2, dp, rows // 2), ((0, 0), (0, 0), (0, rows - rows // 2))
    ).reshape(2, D)
    g_down1 = jnp.sum(de1.astype(f32), axis=0, keepdims=True)
    blank = jnp.zeros((4 - bias_cols, D), f32)
    strip = jnp.concatenate(
        [gg_attn0, gg_mlp0, g_down0, router_rows[0:1], gb_u0, blank]
        + [gg_attn1, gg_mlp1, g_down1, router_rows[1:2], gb_u1, blank]
    )
    strip = jnp.pad(strip, ((0, LANES - 16), (0, 0))).T.astype(bf16)
    attn0 = attn_grad(me, True, depth, a0, dqkv0, gw_o0, strip)
    attn0, near_u, far_u, da_part = fence(attn0, near_u, far_u, da_part)

    diag_q, far_q = send_diagonal(attn0), send_far(attn0)
    (sum_du,) = whole(
        sum_both_kernel,
        [((depth, 2 * rows, 2 * D), bf16)],
        [],
        parts(gw_d0, near_d, far_d) + parts(gw_u0, near_u, far_u),
    )
    r_du = reduce_z(sum_du)
    dx0_b = last_rows(da_part, swap(da_part, "section"), x_b, gain_attn0, gy_dh0)
    (y1_b,) = whole(
        routed_sum_kernel,
        [((tokens, D), bf16)],
        [],
        [y0_b, delta, weight, picked[:, None, :]],
    )
    boundary_out = jnp.where(first, dx0_b, y1_b).reshape(1, micro, 1, length, D)
    diag_q, r_a1, r_m1 = fence(diag_q, r_a1, r_m1)

    near_q = send_near(near(attn0, diag_q))
    far_q, boundary_out = fence(far_q, boundary_out)
    part = lambda v, j: lax.dynamic_index_in_dim(v, me ^ j, axis=0, keepdims=False)
    (sum_q,) = whole(
        halves_kernel,
        [((depth, rows, width + LANES), bf16)],
        [],
        parts(attn0, near_q, far_q),
    )
    sum_q, r_a1, r_m1, r_du = fence(sum_q, r_a1, r_m1, r_du)
    r_u0 = r_du[:rows]
    r_d0 = jnp.concatenate([r_du[rows:, :D], r_du[rows:, D:]], axis=0)
    r_a0 = reduce_z(sum_q)
    r_a1 = plus(part(r_a1, 0), *[to_plane(part(r_a1, j), j) for j in (1, 2, 3)])
    up = r_m1[: 4 * rows].reshape(4, rows, hidden)
    up = [part(up, 0)] + [to_plane(part(up, j), j) for j in (1, 2, 3)]
    (r_u1,) = whole(order_columns_kernel, [((rows, 2 * D), bf16)], [me], up)
    low = 4 * rows + half_units
    r_d1 = jnp.concatenate([r_m1[4 * rows : low], r_m1[low:]], axis=1)

    def joined(grad0, grad1):
        keep = jnp.where(first, grad0, grad1)
        recv = swap(jnp.where(first, grad1, grad0), "section")
        return jnp.where(first, keep, recv).astype(f32), jnp.where(first, recv, keep).astype(f32)

    low, high = joined(r_d0, r_d1)
    out_down = jnp.concatenate([low, high], axis=0)[None]
    low, high = joined(r_u0, r_u1)
    cut = lambda v: v.reshape(rows, 4, depth, half_units).transpose(0, 2, 1, 3)
    out_up = jnp.stack([cut(low), cut(high)], axis=3).reshape(1, rows, FF)
    r_a0, r_a1, out_up, out_down, boundary_out = fence(r_a0, r_a1, out_up, out_down, boundary_out)
    strip = r_a0[:, width:]
    strip_mine = jnp.where(first, strip[:, :8], strip[:, 8:16])
    strip_other = jnp.where(first, strip[:, 8:16], strip[:, :8])
    keep = jnp.where(first, r_a0[:, :width], r_a1)
    send = jnp.where(first, r_a1, r_a0[:, :width])
    pad = lambda v: jnp.pad(v, ((0, 0), (0, LANES - 8)))
    recv = swap(jnp.concatenate([send, pad(strip_other)], axis=1), "section")
    out_qkv, out_out = whole(
        finish_kernel,
        [((rows, 3 * D), f32), ((rows, D), f32)],
        [core],
        [keep, recv],
    )
    small = strip_mine.astype(f32).T
    gain = small[0:1] + recv[:, width : width + 1].astype(f32).T
    bias_half = small[4 : 4 + bias_cols]
    bias_other = recv[:, width + 4 : width + 4 + bias_cols].astype(f32).T
    out_b_up = jnp.concatenate(
        [jnp.where(first, bias_half, bias_other), jnp.where(first, bias_other, bias_half)]
    ).reshape(1, units)
    return (
        boundary_out,
        gain,
        out_qkv[None],
        out_out[None],
        small[1:2],
        out_up,
        out_b_up,
        out_down,
        small[2:3],
        small[3, : rows // 2],
    )


def solution(mesh):
    sections, dp = mesh.shape["section"], mesh.shape["dp"]
    grid = Mesh(mesh.devices.reshape(sections, dp // 4, 2, 2), ("section", "z", "y", "x"))
    chips = ("z", "y", "x")
    in_specs = (
        P("section", None, chips, None, None),
        P(None, chips, None),
        P(None, chips, None),
        P("section", chips),
        P("section", chips, None),
        P("section", chips, None),
        P("section", chips),
        P("section", chips, None),
        P("section", chips),
        P("section", chips, None),
        P("section", chips),
        P(("section",) + chips),
    )
    out_specs = (
        P("section", None, chips, None, None),
        P("section", chips),
        P("section", chips, None),
        P("section", chips, None),
        P("section", chips),
        P("section", chips, None),
        P("section", chips),
        P("section", chips, None),
        P("section", chips),
        P(("section",) + chips),
    )
    return jax.shard_map(shards, mesh=grid, in_specs=in_specs, out_specs=out_specs, check_vma=False)
```

```python
import functools

import jax
import jax.numpy as jnp
from jax import lax
from jax.experimental import pallas as pl
from jax.experimental.pallas import tpu as pltpu
from jax.sharding import Mesh
from jax.sharding import PartitionSpec as P

D = 1024
HEADS = 16
HEAD_DIM = 64
FF = 4096
HALF = D // 2
LANES = 128

epsilon = 1e-06
masked_score = -1e30
root_half = 0.7071067811865476
inverse_root_two_pi = 0.3989422804014327

f32 = jnp.float32
bf16 = jnp.bfloat16


def mm(a, b):
    return jnp.dot(a, b, preferred_element_type=f32)


def mm_rows(a, b):
    return lax.dot_general(a, b, (((0,), (0,)), ((), ())), preferred_element_type=f32)


def mm_t(a, b):
    return lax.dot_general(a, b, (((1,), (1,)), ((), ())), preferred_element_type=f32)


def inverse_rms(v):
    return lax.rsqrt(jnp.mean(v * v, axis=-1, keepdims=True) + epsilon)


def norm_back(grad, unit, inverse, gain):
    scaled = grad * gain
    return inverse * (scaled - unit * jnp.mean(scaled * unit, axis=-1, keepdims=True))


def swap(v, axis):
    return lax.ppermute(v, axis, [(0, 1), (1, 0)])


def to_plane(v, j):
    return lax.ppermute(v, ("y", "x"), [(i, i ^ j) for i in range(4)])


def fence(*values):
    return lax.optimization_barrier(values)


def over_z(shard):
    return lax.all_gather(shard, "z", axis=0, tiled=False)


def reduce_z(part):
    return lax.psum_scatter(part, "z", scatter_dimension=0, tiled=False)


mark = ((8, LANES), f32)
light = pl.CostEstimate(flops=1, bytes_accessed=1, transcendentals=0)


near_memory = pl.BlockSpec(memory_space=pltpu.VMEM)
far_memory = pl.BlockSpec(memory_space=pltpu.HBM)


def place_kernel(splits, spans, plane_first, me_ref, *rest):
    pieces = rest[: len(spans)]
    outs, sems = rest[len(spans) : len(spans) + len(splits)], rest[-1]
    me = me_ref[0]
    copies = []
    for p, (src, (j, start, stop)) in enumerate(zip(pieces, spans)):
        for k, (low, high) in enumerate(splits):
            out = outs[k].at[me ^ j, start:stop] if plane_first else outs[k].at[start:stop, me ^ j]
            copies.append(
                pltpu.make_async_copy(src.at[:, :, low:high], out, sems.at[p * len(splits) + k])
            )
    for copy in copies:
        copy.start()
    for copy in copies:
        copy.wait()


def place(me, pieces, spans, splits, plane_first=False):
    depth, rows, _ = pieces[0].shape
    lead = (4, depth) if plane_first else (depth, 4)
    return pl.pallas_call(
        functools.partial(place_kernel, splits, spans, plane_first),
        out_shape=[
            jax.ShapeDtypeStruct((*lead, rows, high - low), bf16) for low, high in splits
        ],
        in_specs=[pl.BlockSpec(memory_space=pltpu.SMEM)] + [far_memory] * len(spans),
        out_specs=[near_memory] * len(splits),
        scratch_shapes=[pltpu.SemaphoreType.DMA((len(spans) * len(splits),))],
        compiler_params=pltpu.CompilerParams(vmem_limit_bytes=16 << 20),
        cost_estimate=light,
    )(jnp.reshape(me, (1,)), *pieces)


def mask_of(seg_col, seg_row, low, start, stop):
    keys = low + lax.broadcasted_iota(jnp.int32, (stop - low, stop - start), 0)
    queries = start + lax.broadcasted_iota(jnp.int32, (stop - low, stop - start), 1)
    allowed = (seg_col[low:stop] == seg_row[:, start:stop]) & (keys <= queries)
    return allowed.astype(jnp.int32)


def both_heads(v):
    lane = lax.broadcasted_iota(jnp.int32, (1, LANES), 1)
    upper = (lane >= HEAD_DIM).astype(bf16)
    return jnp.concatenate([v * (1 - upper), v * upper], axis=0)


def merged_heads(v):
    half = v.shape[0] // 2
    lane = lax.broadcasted_iota(jnp.int32, (1, LANES), 1)
    return jnp.where(lane < HEAD_DIM, v[:half], v[half:])


def softmax_down(q, k, allowed):
    scores = jnp.where(allowed != 0, mm_t(k, q), masked_score)
    exponent = jnp.exp(scores - jnp.max(scores, axis=0, keepdims=True))
    return exponent / jnp.sum(exponent, axis=0, keepdims=True)


def attend_pair(q, k, v, masks, block):
    scale = jnp.asarray(HEAD_DIM**-0.5, bf16)
    rows = []
    for i, allowed in enumerate(masks):
        low, high = max(0, i - 1) * block, (i + 1) * block
        probs = softmax_down(both_heads(q[i * block : high] * scale), k[low:high], allowed)
        rows.append(merged_heads(mm_rows(probs.astype(bf16), v[low:high])))
    return rows


def attend_pair_back(q, k, v, g, masks, block):
    scale = jnp.asarray(HEAD_DIM**-0.5, bf16)
    dq = []
    dk = [None] * len(masks)
    dv = [None] * len(masks)

    def add(parts, low, high, term):
        for b in range(low, high):
            piece = term[(b - low) * block : (b - low + 1) * block]
            parts[b] = piece if parts[b] is None else parts[b] + piece

    for i, allowed in enumerate(masks):
        first = max(0, i - 1)
        low, high = first * block, (i + 1) * block
        qh, gh = both_heads(q[i * block : high] * scale), both_heads(g[i * block : high])
        probs = softmax_down(qh, k[low:high], allowed)
        dp = mm_t(v[low:high], gh)
        add(dv, first, i + 1, mm(probs.astype(bf16), gh))
        inner = jnp.sum(dp * probs, axis=0, keepdims=True)
        ds = (probs * (dp - inner)).astype(bf16)
        dq.append(merged_heads(mm_rows(ds, k[low:high] * scale)))
        add(dk, first, i + 1, mm(ds, qh))
    return dq, dk, dv


def masks_for(seg_col, seg_row, length, block):
    masks = [
        mask_of(seg_col, seg_row, max(0, i - 1) * block, i * block, (i + 1) * block)
        for i in range(length // block)
    ]
    return [jnp.concatenate([m, m], axis=1) for m in masks]


def attend_kernel(block, pairs, length, qkv_ref, seg_col_ref, seg_row_ref, o_ref):
    for s in range(seg_col_ref.shape[0]):
        masks = masks_for(seg_col_ref[s], seg_row_ref[s], length, block)
        at = slice(s * length, (s + 1) * length)
        for p in range(pairs):
            cut = lambda t: qkv_ref[at, (t * pairs + p) * LANES : (t * pairs + p + 1) * LANES]
            for i, rows in enumerate(attend_pair(cut(0), cut(1), cut(2), masks, block)):
                low = s * length + i * block
                o_ref[low : low + block, p * LANES : (p + 1) * LANES] = rows.astype(bf16)


def attend_out_kernel(block, pairs, length, qkv_ref, sc_ref, sr_ref, w_ref, o_ref, z_ref):
    attend_kernel(block, pairs, length, qkv_ref, sc_ref, sr_ref, o_ref)
    z_ref[...] = mm(o_ref[...], w_ref[...]).astype(bf16)


def attend_back_out_kernel(
    block, pairs, length, qkv_ref, sc_ref, sr_ref, g_ref, x_ref, w_ref, d_ref, z_ref, gain_g
):
    attend_back_kernel(block, pairs, length, qkv_ref, sc_ref, sr_ref, g_ref, d_ref)
    da = mm_t(d_ref[...], w_ref[...])
    z_ref[...] = da.astype(bf16)
    x = x_ref[...].astype(f32)
    grad = jnp.sum(da * (x * inverse_rms(x)), axis=0, keepdims=True)

    @pl.when(pl.program_id(0) == 0)
    def _():
        gain_g[...] = grad

    @pl.when(pl.program_id(0) > 0)
    def _():
        gain_g[...] += grad


def attend_back_kernel(block, pairs, length, qkv_ref, seg_col_ref, seg_row_ref, g_ref, d_ref):
    for s in range(seg_col_ref.shape[0]):
        masks = masks_for(seg_col_ref[s], seg_row_ref[s], length, block)
        at = slice(s * length, (s + 1) * length)
        for p in range(pairs):
            cut = lambda t: qkv_ref[at, (t * pairs + p) * LANES : (t * pairs + p + 1) * LANES]
            g = g_ref[at, p * LANES : (p + 1) * LANES]
            grads = attend_pair_back(cut(0), cut(1), cut(2), g, masks, block)
            for t, parts in enumerate(grads):
                for i, rows in enumerate(parts):
                    low, lane = s * length + i * block, (t * pairs + p) * LANES
                    d_ref[low : low + block, lane : lane + LANES] = rows.astype(bf16)


def attention_call(kernel, seg, arrays, weights, width, sums=0):
    count, length = seg.shape
    pairs = arrays[0].shape[1] // (3 * LANES)
    at = lambda columns: pl.BlockSpec((length, columns), lambda s: (s, 0))
    return pl.pallas_call(
        functools.partial(kernel, LANES, pairs, length),
        grid=(count,),
        out_shape=[
            jax.ShapeDtypeStruct((count * length, width), bf16),
            jax.ShapeDtypeStruct((count * length, D), bf16),
        ]
        + [jax.ShapeDtypeStruct((1, D), f32)] * sums,
        in_specs=[at(arrays[0].shape[1])]
        + [
            pl.BlockSpec((1, length, 1), lambda s: (s, 0, 0)),
            pl.BlockSpec((1, 1, length), lambda s: (s, 0, 0)),
        ]
        + [at(v.shape[1]) for v in arrays[1:]]
        + [pl.BlockSpec(weights.shape, lambda s: (0, 0))],
        out_specs=[at(width), at(D)] + [pl.BlockSpec((1, D), lambda s: (0, 0))] * sums,
        compiler_params=pltpu.CompilerParams(vmem_limit_bytes=16 << 20),
        cost_estimate=light,
    )(arrays[0], seg[:, :, None], seg[:, None, :], *arrays[1:], weights)


def attn_grad_kernel(relative, count, earlier, me_ref, a_ref, d_ref, *refs):
    beside, refs = refs[:count], refs[count + earlier :]
    out = refs[-1] if relative else refs[0]
    product = mm_rows(a_ref[...], d_ref[...]).astype(bf16)
    out[:, :, :, : 3 * HALF] = product.reshape(*out.shape[:3], 3 * HALF)
    low = 3 * HALF
    for ref in beside:
        out[:, :, :, low : low + ref.shape[1]] = ref[...].reshape(*out.shape[:3], ref.shape[1])
        low += ref.shape[1]
    for h in range(2 if relative else 0):

        @pl.when(pl.program_id(0) // 2 == h)
        def _(h=h):
            for j in range(4):
                refs[2 * j + h][...] = out[:, me_ref[0] ^ j]


def attn_grad(me, relative, depth, a, dqkv, *beside, earlier=()):
    tokens, step = a.shape[0], D // 4
    rows = D // (4 * depth)
    deep = step // (4 * rows)
    width = 3 * HALF + sum(v.shape[1] for v in beside)
    if relative:
        half = lambda h: pl.BlockSpec(
            (deep, rows, width), lambda i: (jnp.clip(i - 2 * h, 0, 1), 0, 0)
        )
        outs = [((depth // 2, rows, width), bf16, half(h)) for _ in range(4) for h in range(2)]
    else:
        block = pl.BlockSpec((deep, 4, rows, width), lambda i: (i, 0, 0, 0))
        outs = [((depth, 4, rows, width), bf16, block)]
    found = tiled_call(
        functools.partial(attn_grad_kernel, relative, len(beside), len(earlier)),
        D // step,
        outs,
        [
            (jnp.reshape(me, (1,)), pl.BlockSpec(memory_space=pltpu.SMEM)),
            (a, pl.BlockSpec((tokens, step), lambda i: (0, i))),
            (dqkv, resident(dqkv.shape)),
        ]
        + [(v, pl.BlockSpec((step, v.shape[1]), lambda i: (i, 0))) for v in beside]
        + [(v, pl.BlockSpec((1, *v.shape[1:]), lambda i: (0, 0, 0))) for v in earlier],
        [pltpu.VMEM((deep, 4, rows, width), bf16)] if relative else [],
    )
    return pairs_of(found) if relative else found[0]


def pairs_of(arrays):
    return [tuple(arrays[2 * j : 2 * j + 2]) for j in range(len(arrays) // 2)]


def whole(kernel, outs, scalars, arrays, scratch=(), anywhere=0):
    near = len(arrays) - anywhere
    return pl.pallas_call(
        kernel,
        out_shape=[jax.ShapeDtypeStruct(shape, dtype) for shape, dtype in outs],
        in_specs=[pl.BlockSpec(memory_space=pltpu.SMEM)] * len(scalars)
        + [near_memory] * near
        + [far_memory] * anywhere,
        out_specs=[near_memory] * len(outs),
        scratch_shapes=list(scratch),
        compiler_params=pltpu.CompilerParams(vmem_limit_bytes=16 << 20),
        cost_estimate=light,
    )(*[jnp.reshape(v, (1,)) for v in scalars], *arrays)


def resident(shape):
    return pl.BlockSpec(shape, lambda i: (0, 0), pipeline_mode=pl.Buffered(1))


def tiled_call(kernel, steps, outs, ins, scratch=(), room=56):
    return pl.pallas_call(
        kernel,
        grid=(steps,),
        out_shape=[jax.ShapeDtypeStruct(shape, dtype) for shape, dtype, _ in outs],
        in_specs=[spec for _, spec in ins],
        out_specs=[spec for _, _, spec in outs],
        scratch_shapes=list(scratch),
        compiler_params=pltpu.CompilerParams(vmem_limit_bytes=room << 20),
        cost_estimate=light,
    )(*[v for v, _ in ins])


def shard_kernel(core_ref, qkv_ref, wo_ref, keep_strip, send_strip, keep_ref, send_ref):
    for h, (first_half, second_half) in enumerate(((keep_ref, send_ref), (send_ref, keep_ref))):

        @pl.when(core_ref[0] == h)
        def _(outs=(first_half, second_half)):
            for k, out in enumerate(outs):
                for t in range(3):
                    low = t * D + k * HALF
                    cut = qkv_ref[:, low : low + HALF]
                    out[:, t * HALF : (t + 1) * HALF] = cut.astype(bf16)
                out[:, 3 * HALF : 4 * HALF] = wo_ref[:, k * HALF : (k + 1) * HALF].astype(bf16)

    keep_ref[:, 4 * HALF :] = keep_strip[...]
    send_ref[:, 4 * HALF :] = send_strip[...]


def copy_weights(spans, low, high, me, pieces, w_ref, sems):
    copies = [
        pltpu.make_async_copy(src.at[:, :, low:high], w_ref.at[start:stop, me ^ j], sems.at[p])
        for p, (src, (j, start, stop)) in enumerate(zip(pieces, spans))
    ]
    for copy in copies:
        copy.start()
    return copies


def qkv_kernel(spans, step, me_ref, x_ref, gain_ref, *rest):
    pieces = rest[: len(spans)]
    w_ref, a_ref, qkv_ref, sems = rest[len(spans) :]
    copies = copy_weights(spans, 0, 3 * HALF, me_ref[0], pieces, w_ref, sems)
    for i in range(0, x_ref.shape[0], step):
        x = x_ref[i : i + step].astype(f32)
        a_ref[i : i + step] = (x * inverse_rms(x) * gain_ref[...]).astype(bf16)
    for copy in copies:
        copy.wait()
    weights = w_ref[...].reshape(D, 3 * HALF)
    for i in range(0, x_ref.shape[0], step):
        qkv_ref[i : i + step] = mm(a_ref[i : i + step], weights).astype(bf16)


def hidden_kernel(x_ref, part_ref, recv_ref, gain_ref, h_ref, m_ref):
    h = x_ref[...].astype(f32) + (part_ref[...].astype(f32) + recv_ref[...].astype(f32))
    h_ref[...] = h
    m_ref[...] = (h * inverse_rms(h) * gain_ref[...]).astype(bf16)


def hidden_rows(x, part, recv, gain, step=256):
    tokens = x.shape[0]
    down = pl.BlockSpec((step, D), lambda i: (i, 0))
    row = pl.BlockSpec((1, D), lambda i: (0, 0))
    return tiled_call(
        hidden_kernel,
        tokens // step,
        [((tokens, D), f32, down), ((tokens, D), bf16, down)],
        [(x, down), (part, down), (recv, down), (gain, row)],
    )


def down_kernel(g_ref, w_ref, out_ref, done_ref):
    out_ref[...] = mm(g_ref[...], w_ref[...]).astype(bf16)
    done_ref[...] = jnp.zeros_like(done_ref)


def down_product(g, w, step=256):
    tokens, width = g.shape
    return tiled_call(
        down_kernel,
        tokens // step,
        [
            ((tokens, D), bf16, pl.BlockSpec((step, D), lambda i: (i, 0))),
            (*mark, pl.BlockSpec(mark[0], lambda i: (0, 0))),
        ],
        [(g, pl.BlockSpec((step, width), lambda i: (i, 0))), (w, resident(w.shape))],
        room=20,
    )


def choose_kernel(
    h_ref, part_ref, recv_ref, bias_ref, cot_ref, picked_ref, router_ref, gain_ref, *outs
):
    y_ref, chosen_ref, grad_ref, weight_ref, de_ref, a_ref = outs
    e = part_ref[...].astype(f32) + recv_ref[...].astype(f32) + bias_ref[...]
    y = (h_ref[...] + e).astype(bf16)
    y_ref[...] = y
    picked = picked_ref[0]
    places = lax.broadcasted_iota(jnp.int32, (picked.shape[0], y.shape[0]), 1) == picked
    onehot = places.astype(bf16)
    chosen, grad = mm(onehot, y), mm(onehot, cot_ref[...])
    weight = jax.nn.sigmoid(jnp.sum(chosen * router_ref[...], axis=1, keepdims=True))
    chosen_ref[...] = chosen.astype(bf16)
    grad_ref[...] = grad.astype(bf16)
    weight_ref[...] = weight
    de_ref[...] = (weight * grad).astype(bf16)
    a_ref[...] = (chosen * inverse_rms(chosen) * gain_ref[...]).astype(bf16)


def choose_rows(h, part, recv, bias, cot, picked, router, gain):
    micro, count = picked.shape
    tokens = h.shape[0]
    down = pl.BlockSpec((tokens // micro, D), lambda i: (i, 0))
    row = pl.BlockSpec((1, D), lambda i: (0, 0))
    few = lambda width: pl.BlockSpec((count, width), lambda i: (i, 0))
    rows = micro * count
    return tiled_call(
        choose_kernel,
        micro,
        [
            ((tokens, D), bf16, down),
            ((rows, D), bf16, few(D)),
            ((rows, D), bf16, few(D)),
            ((rows, 1), f32, few(1)),
            ((rows, D), bf16, few(D)),
            ((rows, D), bf16, few(D)),
        ],
        [
            (h, down),
            (part, down),
            (recv, down),
            (bias, row),
            (cot, down),
            (picked[:, :, None], pl.BlockSpec((1, count, 1), lambda i: (i, 0, 0))),
            (router, row),
            (gain, row),
        ],
    )


def last_kernel(part_ref, recv_ref, x_ref, gain_ref, sum_ref, dx_ref):
    da = part_ref[...].astype(f32) + recv_ref[...].astype(f32)
    x = x_ref[...].astype(f32)
    inverse = inverse_rms(x)
    unit = x * inverse
    dx_ref[...] = (sum_ref[...] + norm_back(da, unit, inverse, gain_ref[...])).astype(bf16)


def last_rows(part, recv, x, gain, total, step=256):
    tokens = x.shape[0]
    down = pl.BlockSpec((step, D), lambda i: (i, 0))
    row = pl.BlockSpec((1, D), lambda i: (0, 0))
    return tiled_call(
        last_kernel,
        tokens // step,
        [((tokens, D), bf16, down)],
        [(part, down), (recv, down), (x, down), (gain, row), (total, down)],
    )[0]


def up_kernel(m_ref, w_ref, b_ref, g_ref, slope_ref):
    u = mm(m_ref[...], w_ref[...]) + b_ref[...]
    bell = 0.5 * (1.0 + lax.erf(u * root_half))
    g_ref[...] = (u * bell).astype(bf16)
    slope_ref[...] = (bell + u * jnp.exp(-0.5 * u * u) * inverse_root_two_pi).astype(bf16)


def up_product(m, w, bias, step=512):
    tokens, width = m.shape[0], w.shape[1]
    across = pl.BlockSpec((tokens, step), lambda i: (0, i))
    return tiled_call(
        up_kernel,
        width // step,
        [((tokens, width), bf16, across)] * 2,
        [
            (m, resident(m.shape)),
            (w, pl.BlockSpec((w.shape[0], step), lambda i: (0, i))),
            (bias, pl.BlockSpec((1, step), lambda i: (0, i))),
        ],
    )


def down_grad_kernel(me_ref, g_ref, d_ref, *outs):
    product = mm_rows(g_ref[...], d_ref[...]).astype(bf16)
    for i, out in enumerate(outs):

        @pl.when(pl.program_id(0) == i)
        def _(out=out):
            out[...] = product.reshape(out.shape)


def down_grad(me, depth, chips, g, d):
    tokens, width = g.shape
    units = width // (4 * depth)
    return pl.pallas_call(
        down_grad_kernel,
        grid_spec=pltpu.PrefetchScalarGridSpec(
            num_scalar_prefetch=1,
            grid=(len(chips),),
            in_specs=[
                pl.BlockSpec((tokens, width // 4), lambda i, me: (0, me[0] ^ (i + chips[0]))),
                pl.BlockSpec(d.shape, lambda i, me: (0, 0), pipeline_mode=pl.Buffered(1)),
            ],
            out_specs=[pl.BlockSpec((depth, units, D), lambda i, me: (0, 0, 0))] * len(chips),
        ),
        out_shape=[jax.ShapeDtypeStruct((depth, units, D), bf16)] * len(chips),
        compiler_params=pltpu.CompilerParams(vmem_limit_bytes=56 << 20),
        cost_estimate=light,
    )(jnp.reshape(me, (1,)), g, d)


def norm_back_kernel(
    part_ref, recv_ref, h_ref, gain_ref, gy_ref, w_ref, dz_ref, sum_ref, do_ref, gain_g, bias_g
):
    dm = part_ref[...].astype(f32) + recv_ref[...].astype(f32)
    h, gy = h_ref[...], gy_ref[...].astype(f32)
    inverse = inverse_rms(h)
    unit = h * inverse
    dh = norm_back(dm, unit, inverse, gain_ref[...])
    total = gy + dh
    dz = total.astype(bf16)
    sum_ref[...] = total
    dz_ref[...] = dz
    do_ref[...] = mm_t(dz, w_ref[...]).astype(bf16)
    grads = jnp.sum(dm * unit, axis=0, keepdims=True), jnp.sum(gy, axis=0, keepdims=True)

    @pl.when(pl.program_id(0) == 0)
    def _():
        gain_g[...], bias_g[...] = grads

    @pl.when(pl.program_id(0) > 0)
    def _():
        gain_g[...] += grads[0]
        bias_g[...] += grads[1]


def norm_back_product(part, recv, h, gain, gy, w_out, step=256):
    tokens = part.shape[0]
    down = lambda width: pl.BlockSpec((step, width), lambda i: (i, 0))
    row = pl.BlockSpec((1, D), lambda i: (0, 0))
    return tiled_call(
        norm_back_kernel,
        tokens // step,
        [
            ((tokens, D), bf16, down(D)),
            ((tokens, D), f32, down(D)),
            ((tokens, HALF), bf16, down(HALF)),
            ((1, D), f32, row),
            ((1, D), f32, row),
        ],
        [
            (part, down(D)),
            (recv, down(D)),
            (h, down(D)),
            (gain, row),
            (gy, down(D)),
            (w_out, resident(w_out.shape)),
        ],
    )


def take_rows_kernel(picked_ref, *refs):
    sources, (first_out, second_out, done_ref) = refs[1:3], refs[3:]
    picked = picked_ref[0]
    length = sources[0].shape[0]
    places = lax.broadcasted_iota(jnp.int32, (picked.shape[0], length), 1) == picked
    onehot = places.astype(bf16)
    for source, out in zip(sources, (first_out, second_out)):
        out[...] = mm(onehot, source[...]).astype(bf16)
    done_ref[...] = jnp.zeros_like(done_ref)


def take_rows(picked, earlier, *sources):
    micro, count = picked.shape
    width = sources[0].shape[1]
    length = sources[0].shape[0] // micro
    few = ((micro * count, width), bf16, pl.BlockSpec((count, width), lambda i: (i, 0)))
    corner = pl.BlockSpec((1, 8, LANES), lambda i: (0, 0, 0))
    return tiled_call(
        take_rows_kernel,
        micro,
        [few, few, (*mark, pl.BlockSpec(mark[0], lambda i: (0, 0)))],
        [
            (picked[:, :, None], pl.BlockSpec((1, count, 1), lambda i: (i, 0, 0))),
            (earlier, corner),
        ]
        + [(v, pl.BlockSpec((length, width), lambda i: (i, 0))) for v in sources],
    )


def mlp_pre_kernel(d_ref, wd_ref, slope_ref, wu_ref, du_ref, dm_ref, done_ref, acc):
    du = (mm_t(d_ref[...], wd_ref[...]) * slope_ref[...].astype(f32)).astype(bf16)
    du_ref[...] = du
    part = mm_t(du, wu_ref[...])
    step, last = pl.program_id(0), pl.num_programs(0) - 1

    @pl.when(step == 0)
    def _():
        acc[...] = part

    @pl.when((step > 0) & (step < last))
    def _():
        acc[...] += part

    @pl.when(step == last)
    def _():
        dm_ref[...] = (acc[...] + part).astype(bf16)
        done_ref[...] = jnp.zeros_like(done_ref)


def mlp_pre(d, w_down, slope, w_up, step=512):
    tokens, width = slope.shape
    across = pl.BlockSpec((tokens, step), lambda i: (0, i))
    return tiled_call(
        mlp_pre_kernel,
        width // step,
        [
            ((tokens, width), bf16, across),
            ((tokens, D), bf16, pl.BlockSpec((tokens, D), lambda i: (0, 0))),
            (*mark, pl.BlockSpec(mark[0], lambda i: (0, 0))),
        ],
        [
            (d, resident(d.shape)),
            (w_down, pl.BlockSpec((step, D), lambda i: (i, 0))),
            (slope, across),
            (w_up, pl.BlockSpec((D, step), lambda i: (0, i))),
        ],
        [pltpu.VMEM((tokens, D), f32)],
        room=36,
    )


def down_rest_kernel(me_ref, gy_ref, g_ref, *refs):
    ins, outs = refs[:4], refs[4:]
    more = mm_rows(g_ref[...], gy_ref[...])
    for j in range(4):

        @pl.when(pl.program_id(0) == j)
        def _(j=j):
            total = (ins[j][...].astype(f32) + more.reshape(ins[j].shape)).astype(bf16)
            half = total.shape[0] // 2
            outs[2 * j][...] = total[:half]
            outs[2 * j + 1][...] = total[half:]


def down_rest(me, gy, g, pre):
    rows, width = g.shape
    fixed = lambda shape: pl.BlockSpec(
        shape, lambda i, me: (0,) * len(shape), pipeline_mode=pl.Buffered(1)
    )
    half = (pre[0].shape[0] // 2, *pre[0].shape[1:])
    found = pl.pallas_call(
        down_rest_kernel,
        grid_spec=pltpu.PrefetchScalarGridSpec(
            num_scalar_prefetch=1,
            grid=(4,),
            in_specs=[
                fixed(gy.shape),
                pl.BlockSpec((rows, width // 4), lambda i, me: (0, me[0] ^ i)),
            ]
            + [fixed(v.shape) for v in pre],
            out_specs=[pl.BlockSpec(half, lambda i, me: (0, 0, 0))] * 8,
        ),
        out_shape=[jax.ShapeDtypeStruct(half, bf16)] * 8,
        compiler_params=pltpu.CompilerParams(vmem_limit_bytes=16 << 20),
        cost_estimate=light,
    )(jnp.reshape(me, (1,)), gy, g, *pre)
    return pairs_of(found)


def up_rest_kernel(
    me_ref, picked_ref, gy_ref, wd_ref, slope_ref, du_ref, m_ref, wu_ref, dm_in, _, *refs
):
    outs, (dm_ref, gb_ref, du, acc, gw) = refs[:8], refs[8:]
    half = gw.shape[0] // 2
    micro, count = picked_ref.shape[0], picked_ref.shape[2]
    length = dm_in.shape[0] // micro
    rows = (mm_t(gy_ref[...], wd_ref[...]) * slope_ref[...].astype(f32)).astype(bf16)
    for s in range(micro):
        at = slice(s * length, (s + 1) * length)
        places = lax.broadcasted_iota(jnp.int32, (length, count), 0) == picked_ref[s]
        more = mm(places.astype(bf16), rows[s * count : (s + 1) * count])
        du[at] = du_ref[at] + more.astype(bf16)
    gb_ref[...] = jnp.sum(du[...].astype(f32), axis=0, keepdims=True)
    gw[...] = mm_rows(m_ref[...], du[...]).astype(bf16).reshape(gw.shape)
    for j in range(4):
        outs[2 * j][...] = gw[:half, me_ref[0] ^ j]
        outs[2 * j + 1][...] = gw[half:, me_ref[0] ^ j]
    part = mm_t(rows, wu_ref[...])

    @pl.when(pl.program_id(0) == 0)
    def _():
        acc[...] = part

    @pl.when(pl.program_id(0) > 0)
    def _():
        acc[...] += part

    @pl.when(pl.program_id(0) == pl.num_programs(0) - 1)
    def _():
        for s in range(micro):
            at = slice(s * length, (s + 1) * length)
            cut = acc[s * count : (s + 1) * count]
            dm_ref[at] = put_rows(dm_in[at], cut, picked_ref[s], length).astype(bf16)


def up_rest(me, depth, picked, gy, w_down, slope, du, m, w_up, dm, earlier, step=512):
    tokens, width = du.shape
    rows = D // (4 * depth)
    tall = lambda height: pl.BlockSpec((height, step), lambda i: (0, i))
    once = lambda v: pl.BlockSpec(v.shape, lambda i: (0,) * v.ndim, pipeline_mode=pl.Buffered(1))
    block = pl.BlockSpec((depth // 2, rows, step), lambda i: (0, 0, i))
    return tiled_call(
        up_rest_kernel,
        width // step,
        [((depth // 2, rows, width), bf16, block)] * 8
        + [
            ((tokens, D), bf16, pl.BlockSpec((tokens, D), lambda i: (0, 0))),
            ((1, width), f32, tall(1)),
        ],
        [
            (jnp.reshape(me, (1,)), pl.BlockSpec(memory_space=pltpu.SMEM)),
            (picked, once(picked)),
            (gy, once(gy)),
            (w_down, pl.BlockSpec((step, D), lambda i: (i, 0))),
            (slope, tall(gy.shape[0])),
            (du, tall(tokens)),
            (m, once(m)),
            (w_up, tall(D)),
            (dm, once(dm)),
            (earlier, pl.BlockSpec((1, 1, *earlier.shape[2:]), lambda i: (0, 0, 0, 0))),
        ],
        [
            pltpu.VMEM((tokens, step), bf16),
            pltpu.VMEM((gy.shape[0], D), f32),
            pltpu.VMEM((depth, 4, rows, step), bf16),
        ],
    )


def order_rows_kernel(me_ref, *refs):
    for j, ref in enumerate(refs[:-1]):
        refs[-1][me_ref[0] ^ j] = ref[...]


def halves_kernel(*refs):
    out_ref = refs[-1]
    half = refs[0].shape[0]
    for h in range(2):
        total = sum(ref[...].astype(f32) for ref in refs[3 * h : 3 * h + 3])
        out_ref[h * half : (h + 1) * half] = total.astype(bf16)


def order_mlp_kernel(me_ref, u0, u1, u2, u3, d_ref, out_ref):
    rows, width = u0.shape
    units = d_ref.shape[0]
    for j, ref in enumerate((u0, u1, u2, u3)):
        start = pl.multiple_of((me_ref[0] ^ j) * rows, rows)
        out_ref[pl.ds(start, rows)] = ref[...]
    for k in range(2):
        low = 4 * rows + k * units
        out_ref[low : low + units] = d_ref[:, k * width : (k + 1) * width]


def order_columns_kernel(me_ref, *refs):
    out_ref = refs[-1]
    width = refs[0].shape[1]
    for j, ref in enumerate(refs[:-1]):
        start = pl.multiple_of((me_ref[0] ^ j) * width, width)
        out_ref[:, pl.ds(start, width)] = ref[...]


def routed_attn_kernel(count, a_ref, seg_col_ref, seg_row_ref, w_ref, _, qkv_ref, o_ref):
    weights = w_ref[:, :, :, : 3 * HALF].reshape(D, 3 * HALF)
    qkv_ref[...] = mm(a_ref[...], weights).astype(bf16)
    attend_kernel(count, HALF // LANES, count, qkv_ref, seg_col_ref, seg_row_ref, o_ref)


def routed_hidden_kernel(part_ref, recv_ref, chosen_ref, gain_ref, m_ref):
    z = part_ref[...].astype(f32) + recv_ref[...].astype(f32)
    h = chosen_ref[...].astype(f32) + z
    m_ref[...] = (h * inverse_rms(h) * gain_ref[...]).astype(bf16)


def routed_mlp_kernel(core_ref, m0, m1, m2, m3, d0, d1, d2, d3, w_ref, b_ref, _, *rest):
    g_ref, du_ref, keep_ref, send_ref, gb_ref, m_ref, d_ref = rest
    rows = m0.shape[0]
    for j, (m, d) in enumerate(zip((m0, m1, m2, m3), (d0, d1, d2, d3))):
        m_ref[j * rows : (j + 1) * rows] = m[...]
        d_ref[j * rows : (j + 1) * rows] = d[...]
    hidden = w_ref.shape[2]
    own_rows = D // w_ref.shape[0]
    units = (w_ref.shape[1] - own_rows) // 2
    w_up = w_ref[:, :own_rows].reshape(D, hidden)
    w_down = [
        w_ref[:, own_rows + k * units : own_rows + (k + 1) * units].reshape(hidden, hidden)
        for k in range(2)
    ]
    u = mm(m_ref[...], w_up) + b_ref[...]
    bell = 0.5 * (1.0 + lax.erf(u * root_half))
    g = (u * bell).astype(bf16)
    slope = bell + u * jnp.exp(-0.5 * u * u) * inverse_root_two_pi
    dg = mm_t(d_ref[:, :hidden], w_down[0]) + mm_t(d_ref[:, hidden:], w_down[1])
    du = (dg * slope).astype(bf16)
    g_ref[...] = g
    du_ref[...] = du
    gb_ref[...] = jnp.sum(du.astype(f32), axis=0, keepdims=True)
    e = jnp.concatenate([mm(g, w).astype(bf16) for w in w_down], axis=1).reshape(keep_ref.shape)
    dm = mm_t(du, w_up).astype(bf16).reshape(keep_ref.shape)

    @pl.when(core_ref[0] == 0)
    def _():
        keep_ref[...] = e
        send_ref[...] = dm

    @pl.when(core_ref[0] != 0)
    def _():
        keep_ref[...] = dm
        send_ref[...] = e


def routed_grads_kernel(g_ref, d_ref, m_ref, du_ref, out_ref, done_ref):
    depth, all_rows, hidden = out_ref.shape
    rows = D // depth
    units = (all_rows - rows) // 2
    up = mm_rows(m_ref[...], du_ref[...]).astype(bf16)
    out_ref[:, :rows] = up.reshape(depth, rows, hidden)
    for k in range(2):
        down = mm_rows(g_ref[...], d_ref[:, k * hidden : (k + 1) * hidden]).astype(bf16)
        low = rows + k * units
        out_ref[:, low : low + units] = down.reshape(depth, units, hidden)
    done_ref[...] = jnp.zeros_like(done_ref)


def add_parts_kernel(a_ref, b_ref, _, *outs):
    for j, out in enumerate(outs):
        out[...] = (a_ref[j].astype(f32) + b_ref[j].astype(f32)).astype(bf16)


def add_kernel(*refs):
    refs[-1][...] = sum(ref[...].astype(f32) for ref in refs[:-2]).astype(bf16)


def routed_back_kernel(count, core_ref, *refs):
    ins, outs = refs[:14], refs[14:]
    total, crossed, bias, z_ref, z_recv, chosen_ref, chosen_g, weight_ref, gain = ins[:9]
    wo_ref, wq_ref, qkv_ref, seg_col_ref, seg_row_ref = ins[9:]
    delta_ref, logit_ref, dh_ref, dz_ref, gain_g, dqkv_ref, da_ref, do_scr = outs
    first = core_ref[0] == 0
    a, b = total[...].astype(f32), crossed[...].astype(f32)
    e = jnp.where(first, a, b) + bias[...]
    dm = jnp.where(first, b, a)
    z = z_ref[...].astype(f32) + z_recv[...].astype(f32)
    delta = z + e
    delta_ref[...] = delta
    weight, grad = weight_ref[...], chosen_g[...].astype(f32)
    logit_ref[...] = jnp.sum(grad * delta, axis=1, keepdims=True) * weight * (1.0 - weight)
    h = chosen_ref[...].astype(f32) + z
    inverse = inverse_rms(h)
    unit = h * inverse
    gain_g[...] = jnp.sum(dm * unit, axis=0, keepdims=True)
    dh = norm_back(dm, unit, inverse, gain[...])
    dh_ref[...] = dh
    dz = (weight * grad + dh).astype(bf16)
    dz_ref[...] = dz
    do_scr[...] = mm_t(dz, wo_ref[...]).astype(bf16)
    attend_back_kernel(
        count, HALF // LANES, count, qkv_ref, seg_col_ref, seg_row_ref, do_scr, dqkv_ref
    )
    weights = wq_ref[:, :, :, : 3 * HALF].reshape(D, 3 * HALF)
    da_ref[...] = mm_t(dqkv_ref[...], weights).astype(bf16)


def put_rows(base, rows, picked, length):
    places = lax.broadcasted_iota(jnp.int32, (length, picked.shape[1]), 0) == picked
    onehot = places.astype(bf16)
    high = rows.astype(bf16)
    low = (rows - high.astype(f32)).astype(bf16)
    return base.astype(f32) + (mm(onehot, high) + mm(onehot, low))


def routed_out_kernel(
    part_ref, recv_ref, chosen_ref, gain, dh_ref, logit_ref, router, picked_ref, cot_ref, *outs
):
    gy_ref, gy_rows, gain_g, router_g = outs
    own = part_ref[...].astype(f32)
    da = own + recv_ref[...].astype(f32)
    chosen, logit = chosen_ref[...].astype(f32), logit_ref[...]
    inverse = inverse_rms(chosen)
    unit = chosen * inverse
    gain_g[...] = jnp.sum(own * unit, axis=0, keepdims=True)
    router_g[...] = jnp.sum(logit * chosen, axis=0, keepdims=True)
    rows = dh_ref[...] + norm_back(da, unit, inverse, gain[...]) + logit * router[...]
    micro, count = picked_ref.shape[0], picked_ref.shape[2]
    length = cot_ref.shape[0] // micro
    for s in range(micro):
        at = slice(s * length, (s + 1) * length)
        cut = rows[s * count : (s + 1) * count]
        gy = put_rows(cot_ref[at], cut, picked_ref[s], length).astype(bf16)
        gy_ref[at] = gy
        places = lax.broadcasted_iota(jnp.int32, (length, count), 0) == picked_ref[s]
        gy_rows[s * count : (s + 1) * count] = mm_rows(places.astype(bf16), gy).astype(bf16)


def routed_sum_kernel(y_ref, delta_ref, weight_ref, picked_ref, out_ref):
    rows = weight_ref[...] * delta_ref[...]
    micro, count = picked_ref.shape[0], picked_ref.shape[2]
    length = y_ref.shape[0] // micro
    for s in range(micro):
        at = slice(s * length, (s + 1) * length)
        cut = rows[s * count : (s + 1) * count]
        out_ref[at] = put_rows(y_ref[at], cut, picked_ref[s], length).astype(bf16)


def finish_kernel(core_ref, keep_ref, recv_ref, qkv_ref, out_ref):
    keep, recv = keep_ref[...].astype(f32), recv_ref[:, : 4 * HALF].astype(f32)
    first = core_ref[0] == 0
    low, high = jnp.where(first, keep, recv), jnp.where(first, recv, keep)
    for t in range(3):
        qkv_ref[:, t * D : t * D + HALF] = low[:, t * HALF : (t + 1) * HALF]
        qkv_ref[:, t * D + HALF : (t + 1) * D] = high[:, t * HALF : (t + 1) * HALF]
    out_ref[:, :HALF] = low[:, 3 * HALF : 4 * HALF]
    out_ref[:, HALF:] = high[:, 3 * HALF : 4 * HALF]


def shards(
    boundary_in,
    segments,
    routed,
    gain_attn,
    w_qkv,
    w_out,
    gain_mlp,
    w_up,
    b_up,
    w_down,
    b_down,
    router,
):
    core = lax.axis_index("section")
    first = core == 0
    me = 2 * lax.axis_index("y") + lax.axis_index("x")
    depth = lax.axis_size("z")
    rows = w_qkv.shape[1]
    dp = 4 * depth
    units = w_up.shape[2] // dp
    half_units = units // 2
    micro, length = boundary_in.shape[1], boundary_in.shape[3]
    tokens = micro * length

    up_halves = w_up[0].astype(bf16).reshape(rows, depth, 4, 2, half_units)
    down_halves = w_down[0].astype(bf16).reshape(2, half_units, D)
    bias_cols = half_units // rows
    bias_halves = b_up[0].astype(bf16).reshape(2, bias_cols, rows)
    column = lambda v: jnp.pad(v.astype(bf16), (0, rows - v.shape[0]))[:, None]
    small = jnp.concatenate(
        [column(gain_attn[0]), column(gain_mlp[0]), column(b_down[0]), column(router)], axis=1
    )

    def half(h):
        pick = lambda v, axis: lax.dynamic_index_in_dim(v, h, axis=axis, keepdims=False)
        strip = jnp.concatenate([small, pick(bias_halves, 0).T], axis=1)
        strip = jnp.pad(strip, ((0, 0), (0, 8 - strip.shape[1])))
        none = jnp.zeros_like(strip)
        strip = jnp.concatenate(
            [jnp.where(first, strip, none), jnp.where(first, none, strip)], axis=1
        )
        strip = jnp.pad(strip, ((0, 0), (0, LANES - 16)))
        up = pick(up_halves, 3).transpose(0, 2, 1, 3).reshape(rows, D * 2)
        return strip, up, pick(down_halves, 0)

    kept, sent = list(half(core)), list(half(1 - core))
    kept[0], sent[0] = whole(
        shard_kernel,
        [((rows, 4 * HALF + LANES), bf16)] * 2,
        [core],
        [w_qkv[0], w_out[0], kept[0], sent[0]],
    )
    came = tuple(swap(v, "section") for v in sent)
    width = 4 * HALF
    shard0 = [jnp.where(first, k, r) for k, r in zip(kept, came)]
    shard1 = [jnp.where(first, r, k) for k, r in zip(kept, came)]
    strip = kept[0][:, width:] + came[0][:, width:]
    shard0[0] = jnp.concatenate([shard0[0][:, :width], strip], axis=1)
    shard1[0] = shard1[0][:, :width]

    mine = boundary_in[0, :, 0].reshape(tokens, D)
    other = swap(mine, "section")
    x_b = jnp.where(first, mine, other)
    cot_b = jnp.where(first, other, mine)
    seg = segments[:, 0]
    picked = routed[:, 0]
    count = picked.shape[1]
    chosen_rows = micro * count

    def whole_out(w_o):
        w_o = w_o.reshape(D, HALF)
        own = lax.dynamic_slice_in_dim(w_o, core * HALF, HALF, axis=0)
        recv = swap(lax.dynamic_slice_in_dim(w_o, (1 - core) * HALF, HALF, axis=0), "section")
        return jnp.concatenate([jnp.where(first, own, recv), jnp.where(first, recv, own)], axis=1)

    halfway = depth // 2

    own_q = over_z(shard0[0])
    rest = [shard1[0]] + [to_plane(shard1[0], j) for j in (1, 2, 3)]
    (rest,) = whole(order_rows_kernel, [((4, rows, width), bf16)], [me], rest)
    hidden = depth * half_units
    pick_up = lambda j: lax.dynamic_slice_in_dim(shard1[1], (me ^ j) * hidden, hidden, axis=1)
    mlp = [pick_up(0)] + [to_plane(pick_up(j), j) for j in (1, 2, 3)]
    mlp_rows = 4 * rows + 2 * half_units
    (mlp,) = whole(order_mlp_kernel, [((mlp_rows, hidden), bf16)], [me], [*mlp, shard1[2]])
    onehot = picked[:, :, None] == lax.broadcasted_iota(jnp.int32, (micro, count, length), 2)
    seg1 = jnp.sum(jnp.where(onehot, seg[:, None, :], 0), axis=2)
    seg1_col, seg1_row = seg1[:, :, None], seg1[:, None, :]
    is_routed = jnp.any(onehot, axis=1).reshape(tokens, 1)
    cot_other = jnp.where(is_routed, jnp.zeros_like(cot_b), cot_b)
    own_q, rest, mlp, shard_u = fence(own_q, rest, mlp, shard0[1])

    px_q, py_q = swap(own_q, "x"), swap(own_q, "y")
    own_u = over_z(shard_u)
    own_q, px_q, py_q, own_u, shard_d, x_b, cot_b, cot_other, seg1_col, seg1_row = fence(
        own_q, px_q, py_q, own_u, shard0[2], x_b, cot_b, cot_other, seg1_col, seg1_row
    )
    pd_q, px_u = swap(px_q, "y"), swap(own_u, "x")
    own_d = over_z(shard_d)
    own_q, px_q, py_q, pd_q, own_u, px_u, own_d, rest = fence(
        own_q, px_q, py_q, pd_q, own_u, px_u, own_d, rest
    )
    py_u = swap(own_u, "y")
    px_d, py_d = swap(own_d, "x"), swap(own_d, "y")
    w_r1 = over_z(rest)

    spans_all = [(j, 0, depth) for j in range(4)]
    w_o0, strip = place(
        me, [own_q, px_q, py_q, pd_q], spans_all, ((3 * HALF, width), (width, width + LANES))
    )
    w_o0 = whole_out(w_o0)
    choose = (
        lax.broadcasted_iota(jnp.int32, (16, LANES), 0)
        == lax.broadcasted_iota(jnp.int32, (16, LANES), 1)
    ).astype(bf16)
    vectors = mm_t(choose, strip.reshape(D, LANES))
    gain_attn0, gain_mlp0, b_down0 = vectors[0:1], vectors[1:2], vectors[2:3]
    gain_attn1, gain_mlp1, b_down1 = vectors[8:9], vectors[9:10], vectors[10:11]
    router_full = jnp.concatenate(
        [vectors[b].reshape(dp, rows)[:, : rows // 2].reshape(1, HALF) for b in (3, 11)], axis=1
    )
    biases = lambda b: (
        vectors[b : b + bias_cols].reshape(bias_cols, depth, 4, rows).transpose(2, 1, 0, 3)
    )
    bias_up0 = biases(4).reshape(1, 2 * D)
    bias_up1 = lax.dynamic_index_in_dim(biases(12), me, axis=0, keepdims=False)
    bias_up1 = bias_up1.reshape(1, hidden)
    w_q0, a0, qkv0 = whole(
        functools.partial(qkv_kernel, spans_all, 256),
        [
            ((depth, 4, rows, 3 * HALF), bf16),
            ((tokens, D), bf16),
            ((tokens, 3 * HALF), bf16),
        ],
        [me],
        [x_b, gain_attn0, own_q, px_q, py_q, pd_q],
        [pltpu.SemaphoreType.DMA((4,))],
        anywhere=4,
    )
    w_q0 = w_q0.reshape(D, 3 * HALF)
    o0, z_part = attention_call(attend_out_kernel, seg, [qkv0], w_o0, HALF)
    o0, z_part, own_u, px_u, py_u, px_d, mlp = fence(o0, z_part, own_u, px_u, py_u, px_d, mlp)
    w_m1 = over_z(mlp)

    pd_u = swap(py_u, "x")
    pd_d0 = swap(px_d[:halfway], "y")
    h0, m0 = hidden_rows(x_b, z_part, swap(z_part, "section"), gain_mlp0)
    m0, pd_u, py_d, bias_up0, bias_up1, router_full = fence(
        m0, pd_u, py_d, bias_up0, bias_up1, router_full
    )

    pd_d1 = swap(py_d[halfway:], "x")
    (w_u0,) = place(me, [own_u, px_u, py_u, pd_u], spans_all, ((0, D * 2),))
    w_u0 = w_u0.reshape(D, D * 2)
    g0, slope0 = up_product(m0, w_u0, bias_up0)
    g0, pd_d0, pd_d1 = fence(g0, pd_d0, pd_d1)

    spans_cut = spans_all[:3] + [(3, 0, halfway), (3, halfway, depth)]
    (w_d0,) = place(
        me, [own_d, px_d, py_d, pd_d0, pd_d1], spans_cut, ((0, D),), plane_first=True
    )
    w_d0 = w_d0.reshape(D * 2, D)
    e_part, down_done = down_product(g0, w_d0)
    w_r1, down_done = fence(w_r1, down_done)
    w_o1 = whole_out(w_r1[..., 3 * HALF :])

    y0_b, chosen, grad_chosen, weight, de1, a1 = choose_rows(
        h0, e_part, swap(e_part, "section"), b_down0, cot_b, picked, router_full, gain_attn1
    )
    de_all = [de1] + [to_plane(de1, j) for j in (1, 2, 3)]
    qkv1, o1 = whole(
        functools.partial(routed_attn_kernel, count),
        [((chosen_rows, 3 * HALF), bf16), ((chosen_rows, HALF), bf16)],
        [],
        [a1, seg1_col, seg1_row, w_r1, down_done],
    )
    z_part = mm(o1, w_o1).astype(bf16)
    z_recv = swap(z_part, "section")
    (m1,) = whole(
        routed_hidden_kernel,
        [((chosen_rows, D), bf16)],
        [],
        [z_part, z_recv, chosen, gain_mlp1],
    )
    m_all = [m1] + [to_plane(m1, j) for j in (1, 2, 3)]
    pre_du, pre_dm, pre_done = mlp_pre(cot_other, w_d0, slope0, w_u0)
    g1, du1, keep, send, gb_u1, m_rows, de_rows = whole(
        routed_mlp_kernel,
        [((4 * chosen_rows, hidden), bf16)] * 2
        + [((4, chosen_rows, D), bf16)] * 2
        + [((1, hidden), f32)]
        + [((4 * chosen_rows, D), bf16)] * 2,
        [core],
        [*m_all, *de_all, w_m1, bias_up1, pre_done],
    )
    plus = lambda *terms: sum(t.astype(f32) for t in terms).astype(bf16)
    others = swap(send, "section")
    gw_m1, grads_done = whole(
        routed_grads_kernel,
        [((depth, mlp_rows, hidden), bf16), mark],
        [],
        [g1, de_rows, m_rows, du1],
    )
    plus = lambda *terms: sum(t.astype(f32) for t in terms).astype(bf16)
    r_m1 = reduce_z(gw_m1)
    summed = whole(
        add_parts_kernel, [((chosen_rows, D), bf16)] * 4, [], [keep, others, grads_done]
    )
    terms = [summed[0]] + [to_plane(summed[j], j) for j in (1, 2, 3)]
    pre_d = down_grad(me, depth, (0, 1, 2, 3), g0, cot_other)
    g_rows, slope_rows, rows_done = take_rows(picked, pre_d[0], g0, slope0)
    (total,) = whole(add_kernel, [((chosen_rows, D), bf16)], [], [*terms, rows_done])
    crossed = swap(total, "section")

    delta, grad_logit, dh1, dz1, gg_mlp1, dqkv1, da_part = whole(
        functools.partial(routed_back_kernel, count),
        [
            ((chosen_rows, D), f32),
            ((chosen_rows, 1), f32),
            ((chosen_rows, D), f32),
            ((chosen_rows, D), bf16),
            ((1, D), f32),
            ((chosen_rows, 3 * HALF), bf16),
            ((chosen_rows, D), bf16),
        ],
        [core],
        [
            total,
            crossed,
            b_down1,
            z_part,
            z_recv,
            chosen,
            grad_chosen,
            weight,
            gain_mlp1,
            w_o1,
            w_r1,
            qkv1,
            seg1_col,
            seg1_row,
        ],
        [pltpu.VMEM((chosen_rows, HALF), bf16)],
    )

    def out_by_columns(grad):
        own = lax.dynamic_slice_in_dim(grad, core * HALF, HALF, axis=1)
        recv = swap(lax.dynamic_slice_in_dim(grad, (1 - core) * HALF, HALF, axis=1), "section")
        return jnp.concatenate([jnp.where(first, own, recv), jnp.where(first, recv, own)], axis=0)

    gw_o1 = out_by_columns(mm_rows(o1, dz1).astype(bf16))
    gy0_b, gy_rows, gg_attn1, grad_router = whole(
        routed_out_kernel,
        [((tokens, D), bf16), ((chosen_rows, D), bf16), ((1, D), f32), ((1, D), f32)],
        [],
        [
            da_part,
            swap(da_part, "section"),
            chosen,
            gain_attn1,
            dh1,
            grad_logit,
            router_full,
            picked[:, None, :],
            cot_b,
        ],
    )
    send_diagonal = lambda grads: [swap(grads[3][0], "x"), swap(grads[3][1], "y")]
    send_far = lambda grads: [swap(grads[1][0], "x"), swap(grads[2][1], "y")]
    near = lambda grads, diag: [plus(grads[2][0], diag[0]), plus(grads[1][1], diag[1])]
    send_near = lambda sums: [swap(sums[0], "y"), swap(sums[1], "x")]
    parts = lambda grads, near, far: [
        v for h in range(2) for v in (grads[0][h], near[h], far[h])
    ]

    gw_d0 = down_rest(me, gy_rows, g_rows, pre_d)
    gw_d0, gy_rows = fence(gw_d0, gy_rows)
    diag_d, far_d = send_diagonal(gw_d0), send_far(gw_d0)
    attn1 = attn_grad(me, False, depth, a1, dqkv1, gw_o1, earlier=[gw_d0[0][0]])
    *gw_u0, dm_part, gb_u0 = up_rest(
        me,
        depth,
        picked[:, None, :],
        gy_rows,
        w_d0,
        slope_rows,
        pre_du,
        m0,
        w_u0,
        pre_dm,
        attn1,
    )
    r_a1 = reduce_z(attn1)
    diag_d, far_d, gw_u0, dm_part, gy0_b = fence(
        diag_d, far_d, pairs_of(gw_u0), dm_part, gy0_b
    )

    diag_u = send_diagonal(gw_u0)
    near_d = send_near(near(gw_d0, diag_d))
    dz0, gy_dh0, do0, gg_mlp0, g_down0 = norm_back_product(
        dm_part, swap(dm_part, "section"), h0, gain_mlp0, gy0_b, w_o0
    )
    dqkv0, da_part, gg_attn0 = attention_call(
        attend_back_out_kernel, seg, [qkv0, do0, x_b], w_q0, 3 * HALF, sums=1
    )
    diag_u, near_d, dqkv0, da_part, dz0 = fence(diag_u, near_d, dqkv0, da_part, dz0)
    gw_o0 = out_by_columns(mm_rows(o0, dz0).astype(bf16))
    (sum_d,) = whole(
        halves_kernel,
        [((depth, half_units, D), bf16)],
        [],
        parts(gw_d0, near_d, far_d),
    )
    r_d0 = reduce_z(sum_d)

    far_u = send_far(gw_u0)
    near_u = send_near(near(gw_u0, diag_u))
    here = lax.broadcasted_iota(jnp.int32, (depth, 4, bias_cols, rows), 1) == me
    gb_u1 = gb_u1.reshape(depth, 1, bias_cols, rows)
    gb_u1 = jnp.where(here, gb_u1, 0.0).transpose(2, 0, 1, 3).reshape(bias_cols, D)
    gb_u0 = gb_u0.reshape(4, depth, bias_cols, rows).transpose(2, 1, 0, 3).reshape(bias_cols, D)
    router_rows = jnp.pad(
        grad_router.reshape(2, dp, rows // 2), ((0, 0), (0, 0), (0, rows - rows // 2))
    ).reshape(2, D)
    g_down1 = jnp.sum(de1.astype(f32), axis=0, keepdims=True)
    blank = jnp.zeros((4 - bias_cols, D), f32)
    strip = jnp.concatenate(
        [gg_attn0, gg_mlp0, g_down0, router_rows[0:1], gb_u0, blank]
        + [gg_attn1, gg_mlp1, g_down1, router_rows[1:2], gb_u1, blank]
    )
    strip = jnp.pad(strip, ((0, LANES - 16), (0, 0))).T.astype(bf16)
    attn0 = attn_grad(me, True, depth, a0, dqkv0, gw_o0, strip)
    attn0, near_u, far_u, da_part = fence(attn0, near_u, far_u, da_part)

    diag_q, far_q = send_diagonal(attn0), send_far(attn0)
    (sum_u,) = whole(
        halves_kernel,
        [((depth, rows, 2 * D), bf16)],
        [],
        parts(gw_u0, near_u, far_u),
    )
    r_u0 = reduce_z(sum_u)
    dx0_b = last_rows(da_part, swap(da_part, "section"), x_b, gain_attn0, gy_dh0)
    (y1_b,) = whole(
        routed_sum_kernel,
        [((tokens, D), bf16)],
        [],
        [y0_b, delta, weight, picked[:, None, :]],
    )
    boundary_out = jnp.where(first, dx0_b, y1_b).reshape(1, micro, 1, length, D)
    diag_q, r_a1, r_m1 = fence(diag_q, r_a1, r_m1)

    near_q = send_near(near(attn0, diag_q))
    far_q, boundary_out = fence(far_q, boundary_out)
    part = lambda v, j: lax.dynamic_index_in_dim(v, me ^ j, axis=0, keepdims=False)
    (sum_q,) = whole(
        halves_kernel,
        [((depth, rows, width + LANES), bf16)],
        [],
        parts(attn0, near_q, far_q),
    )
    sum_q, r_a1, r_m1, r_d0 = fence(sum_q, r_a1, r_m1, r_d0)
    r_a0 = reduce_z(sum_q)
    r_a1 = plus(part(r_a1, 0), *[to_plane(part(r_a1, j), j) for j in (1, 2, 3)])
    up = r_m1[: 4 * rows].reshape(4, rows, hidden)
    up = [part(up, 0)] + [to_plane(part(up, j), j) for j in (1, 2, 3)]
    (r_u1,) = whole(order_columns_kernel, [((rows, 2 * D), bf16)], [me], up)
    low = 4 * rows + half_units
    r_d1 = jnp.concatenate([r_m1[4 * rows : low], r_m1[low:]], axis=1)

    def joined(grad0, grad1):
        keep = jnp.where(first, grad0, grad1)
        recv = swap(jnp.where(first, grad1, grad0), "section")
        return jnp.where(first, keep, recv).astype(f32), jnp.where(first, recv, keep).astype(f32)

    low, high = joined(r_d0, r_d1)
    out_down = jnp.concatenate([low, high], axis=0)[None]
    low, high = joined(r_u0, r_u1)
    cut = lambda v: v.reshape(rows, 4, depth, half_units).transpose(0, 2, 1, 3)
    out_up = jnp.stack([cut(low), cut(high)], axis=3).reshape(1, rows, FF)
    r_a0, r_a1, out_up, out_down, boundary_out = fence(r_a0, r_a1, out_up, out_down, boundary_out)
    strip = r_a0[:, width:]
    strip_mine = jnp.where(first, strip[:, :8], strip[:, 8:16])
    strip_other = jnp.where(first, strip[:, 8:16], strip[:, :8])
    keep = jnp.where(first, r_a0[:, :width], r_a1)
    send = jnp.where(first, r_a1, r_a0[:, :width])
    pad = lambda v: jnp.pad(v, ((0, 0), (0, LANES - 8)))
    recv = swap(jnp.concatenate([send, pad(strip_other)], axis=1), "section")
    out_qkv, out_out = whole(
        finish_kernel,
        [((rows, 3 * D), f32), ((rows, D), f32)],
        [core],
        [keep, recv],
    )
    small = strip_mine.astype(f32).T
    gain = small[0:1] + recv[:, width : width + 1].astype(f32).T
    bias_half = small[4 : 4 + bias_cols]
    bias_other = recv[:, width + 4 : width + 4 + bias_cols].astype(f32).T
    out_b_up = jnp.concatenate(
        [jnp.where(first, bias_half, bias_other), jnp.where(first, bias_other, bias_half)]
    ).reshape(1, units)
    return (
        boundary_out,
        gain,
        out_qkv[None],
        out_out[None],
        small[1:2],
        out_up,
        out_b_up,
        out_down,
        small[2:3],
        small[3, : rows // 2],
    )


def solution(mesh):
    sections, dp = mesh.shape["section"], mesh.shape["dp"]
    grid = Mesh(mesh.devices.reshape(sections, dp // 4, 2, 2), ("section", "z", "y", "x"))
    chips = ("z", "y", "x")
    in_specs = (
        P("section", None, chips, None, None),
        P(None, chips, None),
        P(None, chips, None),
        P("section", chips),
        P("section", chips, None),
        P("section", chips, None),
        P("section", chips),
        P("section", chips, None),
        P("section", chips),
        P("section", chips, None),
        P("section", chips),
        P(("section",) + chips),
    )
    out_specs = (
        P("section", None, chips, None, None),
        P("section", chips),
        P("section", chips, None),
        P("section", chips, None),
        P("section", chips),
        P("section", chips, None),
        P("section", chips),
        P("section", chips, None),
        P("section", chips),
        P(("section",) + chips),
    )
    return jax.shard_map(shards, mesh=grid, in_specs=in_specs, out_specs=out_specs, check_vma=False)
```

```python
import functools

import jax
import jax.numpy as jnp
from jax import lax
from jax.experimental import pallas as pl
from jax.experimental.pallas import tpu as pltpu
from jax.sharding import Mesh
from jax.sharding import PartitionSpec as P

D = 1024
HEADS = 16
HEAD_DIM = 64
FF = 4096
HALF = D // 2
LANES = 128

epsilon = 1e-06
masked_score = -1e30
root_half = 0.7071067811865476
inverse_root_two_pi = 0.3989422804014327

f32 = jnp.float32
bf16 = jnp.bfloat16


def mm(a, b):
    return jnp.dot(a, b, preferred_element_type=f32)


def mm_rows(a, b):
    return lax.dot_general(a, b, (((0,), (0,)), ((), ())), preferred_element_type=f32)


def mm_t(a, b):
    return lax.dot_general(a, b, (((1,), (1,)), ((), ())), preferred_element_type=f32)


def inverse_rms(v):
    return lax.rsqrt(jnp.mean(v * v, axis=-1, keepdims=True) + epsilon)


def norm_back(grad, unit, inverse, gain):
    scaled = grad * gain
    return inverse * (scaled - unit * jnp.mean(scaled * unit, axis=-1, keepdims=True))


def swap(v, axis):
    return lax.ppermute(v, axis, [(0, 1), (1, 0)])


def to_plane(v, j):
    return lax.ppermute(v, ("y", "x"), [(i, i ^ j) for i in range(4)])


def fence(*values):
    return lax.optimization_barrier(values)


def over_z(shard):
    return lax.all_gather(shard, "z", axis=0, tiled=False)


def reduce_z(part):
    return lax.psum_scatter(part, "z", scatter_dimension=0, tiled=False)


mark = ((8, LANES), f32)
light = pl.CostEstimate(flops=1, bytes_accessed=1, transcendentals=0)


near_memory = pl.BlockSpec(memory_space=pltpu.VMEM)
far_memory = pl.BlockSpec(memory_space=pltpu.HBM)


def place_kernel(splits, spans, plane_first, me_ref, *rest):
    pieces = rest[: len(spans)]
    outs, sems = rest[len(spans) : len(spans) + len(splits)], rest[-1]
    me = me_ref[0]
    copies = []
    for p, (src, (j, start, stop)) in enumerate(zip(pieces, spans)):
        for k, (low, high) in enumerate(splits):
            out = outs[k].at[me ^ j, start:stop] if plane_first else outs[k].at[start:stop, me ^ j]
            copies.append(
                pltpu.make_async_copy(src.at[:, :, low:high], out, sems.at[p * len(splits) + k])
            )
    for copy in copies:
        copy.start()
    for copy in copies:
        copy.wait()


def place(me, pieces, spans, splits, plane_first=False):
    depth, rows, _ = pieces[0].shape
    lead = (4, depth) if plane_first else (depth, 4)
    return pl.pallas_call(
        functools.partial(place_kernel, splits, spans, plane_first),
        out_shape=[
            jax.ShapeDtypeStruct((*lead, rows, high - low), bf16) for low, high in splits
        ],
        in_specs=[pl.BlockSpec(memory_space=pltpu.SMEM)] + [far_memory] * len(spans),
        out_specs=[near_memory] * len(splits),
        scratch_shapes=[pltpu.SemaphoreType.DMA((len(spans) * len(splits),))],
        compiler_params=pltpu.CompilerParams(vmem_limit_bytes=16 << 20),
        cost_estimate=light,
    )(jnp.reshape(me, (1,)), *pieces)


def mask_of(seg_col, seg_row, low, start, stop):
    keys = low + lax.broadcasted_iota(jnp.int32, (stop - low, stop - start), 0)
    queries = start + lax.broadcasted_iota(jnp.int32, (stop - low, stop - start), 1)
    allowed = (seg_col[low:stop] == seg_row[:, start:stop]) & (keys <= queries)
    return allowed.astype(jnp.int32)


def both_heads(v):
    lane = lax.broadcasted_iota(jnp.int32, (1, LANES), 1)
    upper = (lane >= HEAD_DIM).astype(bf16)
    return jnp.concatenate([v * (1 - upper), v * upper], axis=0)


def merged_heads(v):
    half = v.shape[0] // 2
    lane = lax.broadcasted_iota(jnp.int32, (1, LANES), 1)
    return jnp.where(lane < HEAD_DIM, v[:half], v[half:])


def softmax_down(q, k, allowed):
    scores = jnp.where(allowed != 0, mm_t(k, q), masked_score)
    exponent = jnp.exp(scores - jnp.max(scores, axis=0, keepdims=True))
    return exponent / jnp.sum(exponent, axis=0, keepdims=True)


def attend_pair(q, k, v, masks, block):
    scale = jnp.asarray(HEAD_DIM**-0.5, bf16)
    rows = []
    for i, allowed in enumerate(masks):
        low, high = max(0, i - 1) * block, (i + 1) * block
        probs = softmax_down(both_heads(q[i * block : high] * scale), k[low:high], allowed)
        rows.append(merged_heads(mm_rows(probs.astype(bf16), v[low:high])))
    return rows


def attend_pair_back(q, k, v, g, masks, block):
    scale = jnp.asarray(HEAD_DIM**-0.5, bf16)
    dq = []
    dk = [None] * len(masks)
    dv = [None] * len(masks)

    def add(parts, low, high, term):
        for b in range(low, high):
            piece = term[(b - low) * block : (b - low + 1) * block]
            parts[b] = piece if parts[b] is None else parts[b] + piece

    for i, allowed in enumerate(masks):
        first = max(0, i - 1)
        low, high = first * block, (i + 1) * block
        qh, gh = both_heads(q[i * block : high] * scale), both_heads(g[i * block : high])
        probs = softmax_down(qh, k[low:high], allowed)
        dp = mm_t(v[low:high], gh)
        add(dv, first, i + 1, mm(probs.astype(bf16), gh))
        inner = jnp.sum(dp * probs, axis=0, keepdims=True)
        ds = (probs * (dp - inner)).astype(bf16)
        dq.append(merged_heads(mm_rows(ds, k[low:high] * scale)))
        add(dk, first, i + 1, mm(ds, qh))
    return dq, dk, dv


def masks_for(seg_col, seg_row, length, block):
    masks = [
        mask_of(seg_col, seg_row, max(0, i - 1) * block, i * block, (i + 1) * block)
        for i in range(length // block)
    ]
    return [jnp.concatenate([m, m], axis=1) for m in masks]


def attend_kernel(block, pairs, length, qkv_ref, seg_col_ref, seg_row_ref, o_ref):
    for s in range(seg_col_ref.shape[0]):
        masks = masks_for(seg_col_ref[s], seg_row_ref[s], length, block)
        at = slice(s * length, (s + 1) * length)
        for p in range(pairs):
            cut = lambda t: qkv_ref[at, (t * pairs + p) * LANES : (t * pairs + p + 1) * LANES]
            for i, rows in enumerate(attend_pair(cut(0), cut(1), cut(2), masks, block)):
                low = s * length + i * block
                o_ref[low : low + block, p * LANES : (p + 1) * LANES] = rows.astype(bf16)


def attend_out_kernel(block, pairs, length, qkv_ref, sc_ref, sr_ref, w_ref, o_ref, z_ref):
    attend_kernel(block, pairs, length, qkv_ref, sc_ref, sr_ref, o_ref)
    z_ref[...] = mm(o_ref[...], w_ref[...]).astype(bf16)


def attend_back_out_kernel(
    block, pairs, length, qkv_ref, sc_ref, sr_ref, g_ref, x_ref, w_ref, d_ref, z_ref, gain_g
):
    attend_back_kernel(block, pairs, length, qkv_ref, sc_ref, sr_ref, g_ref, d_ref)
    da = mm_t(d_ref[...], w_ref[...])
    z_ref[...] = da.astype(bf16)
    x = x_ref[...].astype(f32)
    grad = jnp.sum(da * (x * inverse_rms(x)), axis=0, keepdims=True)

    @pl.when(pl.program_id(0) == 0)
    def _():
        gain_g[...] = grad

    @pl.when(pl.program_id(0) > 0)
    def _():
        gain_g[...] += grad


def attend_back_kernel(block, pairs, length, qkv_ref, seg_col_ref, seg_row_ref, g_ref, d_ref):
    for s in range(seg_col_ref.shape[0]):
        masks = masks_for(seg_col_ref[s], seg_row_ref[s], length, block)
        at = slice(s * length, (s + 1) * length)
        for p in range(pairs):
            cut = lambda t: qkv_ref[at, (t * pairs + p) * LANES : (t * pairs + p + 1) * LANES]
            g = g_ref[at, p * LANES : (p + 1) * LANES]
            grads = attend_pair_back(cut(0), cut(1), cut(2), g, masks, block)
            for t, parts in enumerate(grads):
                for i, rows in enumerate(parts):
                    low, lane = s * length + i * block, (t * pairs + p) * LANES
                    d_ref[low : low + block, lane : lane + LANES] = rows.astype(bf16)


def attention_call(kernel, seg, arrays, weights, width, sums=0):
    count, length = seg.shape
    pairs = arrays[0].shape[1] // (3 * LANES)
    at = lambda columns: pl.BlockSpec((length, columns), lambda s: (s, 0))
    return pl.pallas_call(
        functools.partial(kernel, LANES, pairs, length),
        grid=(count,),
        out_shape=[
            jax.ShapeDtypeStruct((count * length, width), bf16),
            jax.ShapeDtypeStruct((count * length, D), bf16),
        ]
        + [jax.ShapeDtypeStruct((1, D), f32)] * sums,
        in_specs=[at(arrays[0].shape[1])]
        + [
            pl.BlockSpec((1, length, 1), lambda s: (s, 0, 0)),
            pl.BlockSpec((1, 1, length), lambda s: (s, 0, 0)),
        ]
        + [at(v.shape[1]) for v in arrays[1:]]
        + [pl.BlockSpec(weights.shape, lambda s: (0, 0))],
        out_specs=[at(width), at(D)] + [pl.BlockSpec((1, D), lambda s: (0, 0))] * sums,
        compiler_params=pltpu.CompilerParams(vmem_limit_bytes=16 << 20),
        cost_estimate=light,
    )(arrays[0], seg[:, :, None], seg[:, None, :], *arrays[1:], weights)


def attn_grad_kernel(relative, count, earlier, me_ref, a_ref, d_ref, *refs):
    beside, refs = refs[:count], refs[count + earlier :]
    out = refs[-1] if relative else refs[0]
    product = mm_rows(a_ref[...], d_ref[...]).astype(bf16)
    out[:, :, :, : 3 * HALF] = product.reshape(*out.shape[:3], 3 * HALF)
    low = 3 * HALF
    for ref in beside:
        out[:, :, :, low : low + ref.shape[1]] = ref[...].reshape(*out.shape[:3], ref.shape[1])
        low += ref.shape[1]
    for h in range(2 if relative else 0):

        @pl.when(pl.program_id(0) // 2 == h)
        def _(h=h):
            for j in range(4):
                refs[2 * j + h][...] = out[:, me_ref[0] ^ j]


def attn_grad(me, relative, depth, a, dqkv, *beside, earlier=()):
    tokens, step = a.shape[0], D // 4
    rows = D // (4 * depth)
    deep = step // (4 * rows)
    width = 3 * HALF + sum(v.shape[1] for v in beside)
    if relative:
        half = lambda h: pl.BlockSpec(
            (deep, rows, width), lambda i: (jnp.clip(i - 2 * h, 0, 1), 0, 0)
        )
        outs = [((depth // 2, rows, width), bf16, half(h)) for _ in range(4) for h in range(2)]
    else:
        block = pl.BlockSpec((deep, 4, rows, width), lambda i: (i, 0, 0, 0))
        outs = [((depth, 4, rows, width), bf16, block)]
    found = tiled_call(
        functools.partial(attn_grad_kernel, relative, len(beside), len(earlier)),
        D // step,
        outs,
        [
            (jnp.reshape(me, (1,)), pl.BlockSpec(memory_space=pltpu.SMEM)),
            (a, pl.BlockSpec((tokens, step), lambda i: (0, i))),
            (dqkv, resident(dqkv.shape)),
        ]
        + [(v, pl.BlockSpec((step, v.shape[1]), lambda i: (i, 0))) for v in beside]
        + [(v, pl.BlockSpec((1, *v.shape[1:]), lambda i: (0, 0, 0))) for v in earlier],
        [pltpu.VMEM((deep, 4, rows, width), bf16)] if relative else [],
    )
    return pairs_of(found) if relative else found[0]


def pairs_of(arrays):
    return [tuple(arrays[2 * j : 2 * j + 2]) for j in range(len(arrays) // 2)]


def whole(kernel, outs, scalars, arrays, scratch=(), anywhere=0):
    near = len(arrays) - anywhere
    return pl.pallas_call(
        kernel,
        out_shape=[jax.ShapeDtypeStruct(shape, dtype) for shape, dtype in outs],
        in_specs=[pl.BlockSpec(memory_space=pltpu.SMEM)] * len(scalars)
        + [near_memory] * near
        + [far_memory] * anywhere,
        out_specs=[near_memory] * len(outs),
        scratch_shapes=list(scratch),
        compiler_params=pltpu.CompilerParams(vmem_limit_bytes=16 << 20),
        cost_estimate=light,
    )(*[jnp.reshape(v, (1,)) for v in scalars], *arrays)


def resident(shape):
    return pl.BlockSpec(shape, lambda i: (0, 0), pipeline_mode=pl.Buffered(1))


def tiled_call(kernel, steps, outs, ins, scratch=(), room=56):
    return pl.pallas_call(
        kernel,
        grid=(steps,),
        out_shape=[jax.ShapeDtypeStruct(shape, dtype) for shape, dtype, _ in outs],
        in_specs=[spec for _, spec in ins],
        out_specs=[spec for _, _, spec in outs],
        scratch_shapes=list(scratch),
        compiler_params=pltpu.CompilerParams(vmem_limit_bytes=room << 20),
        cost_estimate=light,
    )(*[v for v, _ in ins])


def shard_kernel(core_ref, qkv_ref, wo_ref, keep_strip, send_strip, keep_ref, send_ref):
    for h, (first_half, second_half) in enumerate(((keep_ref, send_ref), (send_ref, keep_ref))):

        @pl.when(core_ref[0] == h)
        def _(outs=(first_half, second_half)):
            for k, out in enumerate(outs):
                for t in range(3):
                    low = t * D + k * HALF
                    cut = qkv_ref[:, low : low + HALF]
                    out[:, t * HALF : (t + 1) * HALF] = cut.astype(bf16)
                out[:, 3 * HALF : 4 * HALF] = wo_ref[:, k * HALF : (k + 1) * HALF].astype(bf16)

    keep_ref[:, 4 * HALF :] = keep_strip[...]
    send_ref[:, 4 * HALF :] = send_strip[...]


def copy_weights(spans, low, high, me, pieces, w_ref, sems):
    copies = [
        pltpu.make_async_copy(src.at[:, :, low:high], w_ref.at[start:stop, me ^ j], sems.at[p])
        for p, (src, (j, start, stop)) in enumerate(zip(pieces, spans))
    ]
    for copy in copies:
        copy.start()
    return copies


def qkv_kernel(spans, step, me_ref, x_ref, gain_ref, *rest):
    pieces = rest[: len(spans)]
    w_ref, a_ref, qkv_ref, sems = rest[len(spans) :]
    copies = copy_weights(spans, 0, 3 * HALF, me_ref[0], pieces, w_ref, sems)
    for i in range(0, x_ref.shape[0], step):
        x = x_ref[i : i + step].astype(f32)
        a_ref[i : i + step] = (x * inverse_rms(x) * gain_ref[...]).astype(bf16)
    for copy in copies:
        copy.wait()
    weights = w_ref[...].reshape(D, 3 * HALF)
    for i in range(0, x_ref.shape[0], step):
        qkv_ref[i : i + step] = mm(a_ref[i : i + step], weights).astype(bf16)


def hidden_kernel(x_ref, part_ref, recv_ref, gain_ref, h_ref, m_ref):
    h = x_ref[...].astype(f32) + (part_ref[...].astype(f32) + recv_ref[...].astype(f32))
    h_ref[...] = h
    m_ref[...] = (h * inverse_rms(h) * gain_ref[...]).astype(bf16)


def hidden_rows(x, part, recv, gain, step=256):
    tokens = x.shape[0]
    down = pl.BlockSpec((step, D), lambda i: (i, 0))
    row = pl.BlockSpec((1, D), lambda i: (0, 0))
    return tiled_call(
        hidden_kernel,
        tokens // step,
        [((tokens, D), f32, down), ((tokens, D), bf16, down)],
        [(x, down), (part, down), (recv, down), (gain, row)],
    )


def down_kernel(g_ref, w_ref, out_ref, done_ref):
    out_ref[...] = mm(g_ref[...], w_ref[...]).astype(bf16)
    done_ref[...] = jnp.zeros_like(done_ref)


def down_product(g, w, step=256):
    tokens, width = g.shape
    return tiled_call(
        down_kernel,
        tokens // step,
        [
            ((tokens, D), bf16, pl.BlockSpec((step, D), lambda i: (i, 0))),
            (*mark, pl.BlockSpec(mark[0], lambda i: (0, 0))),
        ],
        [(g, pl.BlockSpec((step, width), lambda i: (i, 0))), (w, resident(w.shape))],
        room=20,
    )


def choose_kernel(
    h_ref, part_ref, recv_ref, bias_ref, cot_ref, picked_ref, router_ref, gain_ref, *outs
):
    y_ref, chosen_ref, grad_ref, weight_ref, de_ref, a_ref = outs
    e = part_ref[...].astype(f32) + recv_ref[...].astype(f32) + bias_ref[...]
    y = (h_ref[...] + e).astype(bf16)
    y_ref[...] = y
    picked = picked_ref[0]
    places = lax.broadcasted_iota(jnp.int32, (picked.shape[0], y.shape[0]), 1) == picked
    onehot = places.astype(bf16)
    chosen, grad = mm(onehot, y), mm(onehot, cot_ref[...])
    weight = jax.nn.sigmoid(jnp.sum(chosen * router_ref[...], axis=1, keepdims=True))
    chosen_ref[...] = chosen.astype(bf16)
    grad_ref[...] = grad.astype(bf16)
    weight_ref[...] = weight
    de_ref[...] = (weight * grad).astype(bf16)
    a_ref[...] = (chosen * inverse_rms(chosen) * gain_ref[...]).astype(bf16)


def choose_rows(h, part, recv, bias, cot, picked, router, gain):
    micro, count = picked.shape
    tokens = h.shape[0]
    down = pl.BlockSpec((tokens // micro, D), lambda i: (i, 0))
    row = pl.BlockSpec((1, D), lambda i: (0, 0))
    few = lambda width: pl.BlockSpec((count, width), lambda i: (i, 0))
    rows = micro * count
    return tiled_call(
        choose_kernel,
        micro,
        [
            ((tokens, D), bf16, down),
            ((rows, D), bf16, few(D)),
            ((rows, D), bf16, few(D)),
            ((rows, 1), f32, few(1)),
            ((rows, D), bf16, few(D)),
            ((rows, D), bf16, few(D)),
        ],
        [
            (h, down),
            (part, down),
            (recv, down),
            (bias, row),
            (cot, down),
            (picked[:, :, None], pl.BlockSpec((1, count, 1), lambda i: (i, 0, 0))),
            (router, row),
            (gain, row),
        ],
    )


def last_kernel(part_ref, recv_ref, x_ref, gain_ref, sum_ref, dx_ref):
    da = part_ref[...].astype(f32) + recv_ref[...].astype(f32)
    x = x_ref[...].astype(f32)
    inverse = inverse_rms(x)
    unit = x * inverse
    dx_ref[...] = (sum_ref[...] + norm_back(da, unit, inverse, gain_ref[...])).astype(bf16)


def last_rows(part, recv, x, gain, total, step=256):
    tokens = x.shape[0]
    down = pl.BlockSpec((step, D), lambda i: (i, 0))
    row = pl.BlockSpec((1, D), lambda i: (0, 0))
    return tiled_call(
        last_kernel,
        tokens // step,
        [((tokens, D), bf16, down)],
        [(part, down), (recv, down), (x, down), (gain, row), (total, down)],
    )[0]


def up_kernel(m_ref, w_ref, b_ref, g_ref, slope_ref):
    u = mm(m_ref[...], w_ref[...]) + b_ref[...]
    bell = 0.5 * (1.0 + lax.erf(u * root_half))
    g_ref[...] = (u * bell).astype(bf16)
    slope_ref[...] = (bell + u * jnp.exp(-0.5 * u * u) * inverse_root_two_pi).astype(bf16)


def up_product(m, w, bias, step=512):
    tokens, width = m.shape[0], w.shape[1]
    across = pl.BlockSpec((tokens, step), lambda i: (0, i))
    return tiled_call(
        up_kernel,
        width // step,
        [((tokens, width), bf16, across)] * 2,
        [
            (m, resident(m.shape)),
            (w, pl.BlockSpec((w.shape[0], step), lambda i: (0, i))),
            (bias, pl.BlockSpec((1, step), lambda i: (0, i))),
        ],
    )


def down_grad_kernel(me_ref, g_ref, d_ref, *outs):
    product = mm_rows(g_ref[...], d_ref[...]).astype(bf16)
    for i, out in enumerate(outs):

        @pl.when(pl.program_id(0) == i)
        def _(out=out):
            out[...] = product.reshape(out.shape)


def down_grad(me, depth, chips, g, d):
    tokens, width = g.shape
    units = width // (4 * depth)
    return pl.pallas_call(
        down_grad_kernel,
        grid_spec=pltpu.PrefetchScalarGridSpec(
            num_scalar_prefetch=1,
            grid=(len(chips),),
            in_specs=[
                pl.BlockSpec((tokens, width // 4), lambda i, me: (0, me[0] ^ (i + chips[0]))),
                pl.BlockSpec(d.shape, lambda i, me: (0, 0), pipeline_mode=pl.Buffered(1)),
            ],
            out_specs=[pl.BlockSpec((depth, units, D), lambda i, me: (0, 0, 0))] * len(chips),
        ),
        out_shape=[jax.ShapeDtypeStruct((depth, units, D), bf16)] * len(chips),
        compiler_params=pltpu.CompilerParams(vmem_limit_bytes=56 << 20),
        cost_estimate=light,
    )(jnp.reshape(me, (1,)), g, d)


def norm_back_kernel(
    part_ref, recv_ref, h_ref, gain_ref, gy_ref, w_ref, dz_ref, sum_ref, do_ref, gain_g, bias_g
):
    dm = part_ref[...].astype(f32) + recv_ref[...].astype(f32)
    h, gy = h_ref[...], gy_ref[...].astype(f32)
    inverse = inverse_rms(h)
    unit = h * inverse
    dh = norm_back(dm, unit, inverse, gain_ref[...])
    total = gy + dh
    dz = total.astype(bf16)
    sum_ref[...] = total
    dz_ref[...] = dz
    do_ref[...] = mm_t(dz, w_ref[...]).astype(bf16)
    grads = jnp.sum(dm * unit, axis=0, keepdims=True), jnp.sum(gy, axis=0, keepdims=True)

    @pl.when(pl.program_id(0) == 0)
    def _():
        gain_g[...], bias_g[...] = grads

    @pl.when(pl.program_id(0) > 0)
    def _():
        gain_g[...] += grads[0]
        bias_g[...] += grads[1]


def norm_back_product(part, recv, h, gain, gy, w_out, step=256):
    tokens = part.shape[0]
    down = lambda width: pl.BlockSpec((step, width), lambda i: (i, 0))
    row = pl.BlockSpec((1, D), lambda i: (0, 0))
    return tiled_call(
        norm_back_kernel,
        tokens // step,
        [
            ((tokens, D), bf16, down(D)),
            ((tokens, D), f32, down(D)),
            ((tokens, HALF), bf16, down(HALF)),
            ((1, D), f32, row),
            ((1, D), f32, row),
        ],
        [
            (part, down(D)),
            (recv, down(D)),
            (h, down(D)),
            (gain, row),
            (gy, down(D)),
            (w_out, resident(w_out.shape)),
        ],
    )


def take_rows_kernel(picked_ref, *refs):
    sources, (first_out, second_out, done_ref) = refs[1:3], refs[3:]
    picked = picked_ref[0]
    length = sources[0].shape[0]
    places = lax.broadcasted_iota(jnp.int32, (picked.shape[0], length), 1) == picked
    onehot = places.astype(bf16)
    for source, out in zip(sources, (first_out, second_out)):
        out[...] = mm(onehot, source[...]).astype(bf16)
    done_ref[...] = jnp.zeros_like(done_ref)


def take_rows(picked, earlier, *sources):
    micro, count = picked.shape
    width = sources[0].shape[1]
    length = sources[0].shape[0] // micro
    few = ((micro * count, width), bf16, pl.BlockSpec((count, width), lambda i: (i, 0)))
    corner = pl.BlockSpec((1, 8, LANES), lambda i: (0, 0, 0))
    return tiled_call(
        take_rows_kernel,
        micro,
        [few, few, (*mark, pl.BlockSpec(mark[0], lambda i: (0, 0)))],
        [
            (picked[:, :, None], pl.BlockSpec((1, count, 1), lambda i: (i, 0, 0))),
            (earlier, corner),
        ]
        + [(v, pl.BlockSpec((length, width), lambda i: (i, 0))) for v in sources],
    )


def mlp_pre_kernel(d_ref, wd_ref, slope_ref, wu_ref, du_ref, dm_ref, done_ref, acc):
    du = (mm_t(d_ref[...], wd_ref[...]) * slope_ref[...].astype(f32)).astype(bf16)
    du_ref[...] = du
    part = mm_t(du, wu_ref[...])
    step, last = pl.program_id(0), pl.num_programs(0) - 1

    @pl.when(step == 0)
    def _():
        acc[...] = part

    @pl.when((step > 0) & (step < last))
    def _():
        acc[...] += part

    @pl.when(step == last)
    def _():
        dm_ref[...] = (acc[...] + part).astype(bf16)
        done_ref[...] = jnp.zeros_like(done_ref)


def mlp_pre(d, w_down, slope, w_up, step=512):
    tokens, width = slope.shape
    across = pl.BlockSpec((tokens, step), lambda i: (0, i))
    return tiled_call(
        mlp_pre_kernel,
        width // step,
        [
            ((tokens, width), bf16, across),
            ((tokens, D), bf16, pl.BlockSpec((tokens, D), lambda i: (0, 0))),
            (*mark, pl.BlockSpec(mark[0], lambda i: (0, 0))),
        ],
        [
            (d, resident(d.shape)),
            (w_down, pl.BlockSpec((step, D), lambda i: (i, 0))),
            (slope, across),
            (w_up, pl.BlockSpec((D, step), lambda i: (0, i))),
        ],
        [pltpu.VMEM((tokens, D), f32)],
        room=36,
    )


def down_rest_kernel(me_ref, gy_ref, g_ref, *refs):
    ins, outs = refs[:4], refs[4:]
    more = mm_rows(g_ref[...], gy_ref[...])
    for j in range(4):

        @pl.when(pl.program_id(0) == j)
        def _(j=j):
            total = (ins[j][...].astype(f32) + more.reshape(ins[j].shape)).astype(bf16)
            half = total.shape[0] // 2
            outs[2 * j][...] = total[:half]
            outs[2 * j + 1][...] = total[half:]


def down_rest(me, gy, g, pre):
    rows, width = g.shape
    fixed = lambda shape: pl.BlockSpec(
        shape, lambda i, me: (0,) * len(shape), pipeline_mode=pl.Buffered(1)
    )
    half = (pre[0].shape[0] // 2, *pre[0].shape[1:])
    found = pl.pallas_call(
        down_rest_kernel,
        grid_spec=pltpu.PrefetchScalarGridSpec(
            num_scalar_prefetch=1,
            grid=(4,),
            in_specs=[
                fixed(gy.shape),
                pl.BlockSpec((rows, width // 4), lambda i, me: (0, me[0] ^ i)),
            ]
            + [fixed(v.shape) for v in pre],
            out_specs=[pl.BlockSpec(half, lambda i, me: (0, 0, 0))] * 8,
        ),
        out_shape=[jax.ShapeDtypeStruct(half, bf16)] * 8,
        compiler_params=pltpu.CompilerParams(vmem_limit_bytes=16 << 20),
        cost_estimate=light,
    )(jnp.reshape(me, (1,)), gy, g, *pre)
    return pairs_of(found)


def up_rest_kernel(
    me_ref, picked_ref, gy_ref, wd_ref, slope_ref, du_ref, m_ref, wu_ref, dm_in, _, *refs
):
    outs, (dm_ref, gb_ref, du, acc, gw) = refs[:8], refs[8:]
    half = gw.shape[0] // 2
    micro, count = picked_ref.shape[0], picked_ref.shape[2]
    length = dm_in.shape[0] // micro
    rows = (mm_t(gy_ref[...], wd_ref[...]) * slope_ref[...].astype(f32)).astype(bf16)
    for s in range(micro):
        at = slice(s * length, (s + 1) * length)
        places = lax.broadcasted_iota(jnp.int32, (length, count), 0) == picked_ref[s]
        more = mm(places.astype(bf16), rows[s * count : (s + 1) * count])
        du[at] = du_ref[at] + more.astype(bf16)
    gb_ref[...] = jnp.sum(du[...].astype(f32), axis=0, keepdims=True)
    gw[...] = mm_rows(m_ref[...], du[...]).astype(bf16).reshape(gw.shape)
    for j in range(4):
        outs[2 * j][...] = gw[:half, me_ref[0] ^ j]
        outs[2 * j + 1][...] = gw[half:, me_ref[0] ^ j]
    part = mm_t(rows, wu_ref[...])

    @pl.when(pl.program_id(0) == 0)
    def _():
        acc[...] = part

    @pl.when(pl.program_id(0) > 0)
    def _():
        acc[...] += part

    @pl.when(pl.program_id(0) == pl.num_programs(0) - 1)
    def _():
        for s in range(micro):
            at = slice(s * length, (s + 1) * length)
            cut = acc[s * count : (s + 1) * count]
            dm_ref[at] = put_rows(dm_in[at], cut, picked_ref[s], length).astype(bf16)


def up_rest(me, depth, picked, gy, w_down, slope, du, m, w_up, dm, earlier, step=512):
    tokens, width = du.shape
    rows = D // (4 * depth)
    tall = lambda height: pl.BlockSpec((height, step), lambda i: (0, i))
    once = lambda v: pl.BlockSpec(v.shape, lambda i: (0,) * v.ndim, pipeline_mode=pl.Buffered(1))
    block = pl.BlockSpec((depth // 2, rows, step), lambda i: (0, 0, i))
    return tiled_call(
        up_rest_kernel,
        width // step,
        [((depth // 2, rows, width), bf16, block)] * 8
        + [
            ((tokens, D), bf16, pl.BlockSpec((tokens, D), lambda i: (0, 0))),
            ((1, width), f32, tall(1)),
        ],
        [
            (jnp.reshape(me, (1,)), pl.BlockSpec(memory_space=pltpu.SMEM)),
            (picked, once(picked)),
            (gy, once(gy)),
            (w_down, pl.BlockSpec((step, D), lambda i: (i, 0))),
            (slope, tall(gy.shape[0])),
            (du, tall(tokens)),
            (m, once(m)),
            (w_up, tall(D)),
            (dm, once(dm)),
            (earlier, pl.BlockSpec((1, 1, *earlier.shape[2:]), lambda i: (0, 0, 0, 0))),
        ],
        [
            pltpu.VMEM((tokens, step), bf16),
            pltpu.VMEM((gy.shape[0], D), f32),
            pltpu.VMEM((depth, 4, rows, step), bf16),
        ],
    )


def order_rows_kernel(me_ref, *refs):
    for j, ref in enumerate(refs[:-1]):
        refs[-1][me_ref[0] ^ j] = ref[...]


def halves_kernel(*refs):
    out_ref = refs[-1]
    half = refs[0].shape[0]
    for h in range(2):
        total = sum(ref[...].astype(f32) for ref in refs[3 * h : 3 * h + 3])
        out_ref[h * half : (h + 1) * half] = total.astype(bf16)


def order_mlp_kernel(me_ref, u0, u1, u2, u3, d_ref, out_ref):
    rows, width = u0.shape
    units = d_ref.shape[0]
    for j, ref in enumerate((u0, u1, u2, u3)):
        start = pl.multiple_of((me_ref[0] ^ j) * rows, rows)
        out_ref[pl.ds(start, rows)] = ref[...]
    for k in range(2):
        low = 4 * rows + k * units
        out_ref[low : low + units] = d_ref[:, k * width : (k + 1) * width]


def order_columns_kernel(me_ref, *refs):
    out_ref = refs[-1]
    width = refs[0].shape[1]
    for j, ref in enumerate(refs[:-1]):
        start = pl.multiple_of((me_ref[0] ^ j) * width, width)
        out_ref[:, pl.ds(start, width)] = ref[...]


def routed_attn_kernel(count, a_ref, seg_col_ref, seg_row_ref, w_ref, _, qkv_ref, o_ref):
    weights = w_ref[:, :, :, : 3 * HALF].reshape(D, 3 * HALF)
    qkv_ref[...] = mm(a_ref[...], weights).astype(bf16)
    attend_kernel(count, HALF // LANES, count, qkv_ref, seg_col_ref, seg_row_ref, o_ref)


def routed_hidden_kernel(part_ref, recv_ref, chosen_ref, gain_ref, m_ref):
    z = part_ref[...].astype(f32) + recv_ref[...].astype(f32)
    h = chosen_ref[...].astype(f32) + z
    m_ref[...] = (h * inverse_rms(h) * gain_ref[...]).astype(bf16)


def routed_mlp_kernel(core_ref, m0, m1, m2, m3, d0, d1, d2, d3, w_ref, b_ref, _, *rest):
    g_ref, du_ref, keep_ref, send_ref, gb_ref, m_ref, d_ref = rest
    rows = m0.shape[0]
    for j, (m, d) in enumerate(zip((m0, m1, m2, m3), (d0, d1, d2, d3))):
        m_ref[j * rows : (j + 1) * rows] = m[...]
        d_ref[j * rows : (j + 1) * rows] = d[...]
    hidden = w_ref.shape[2]
    own_rows = D // w_ref.shape[0]
    units = (w_ref.shape[1] - own_rows) // 2
    w_up = w_ref[:, :own_rows].reshape(D, hidden)
    w_down = [
        w_ref[:, own_rows + k * units : own_rows + (k + 1) * units].reshape(hidden, hidden)
        for k in range(2)
    ]
    u = mm(m_ref[...], w_up) + b_ref[...]
    bell = 0.5 * (1.0 + lax.erf(u * root_half))
    g = (u * bell).astype(bf16)
    slope = bell + u * jnp.exp(-0.5 * u * u) * inverse_root_two_pi
    dg = mm_t(d_ref[:, :hidden], w_down[0]) + mm_t(d_ref[:, hidden:], w_down[1])
    du = (dg * slope).astype(bf16)
    g_ref[...] = g
    du_ref[...] = du
    gb_ref[...] = jnp.sum(du.astype(f32), axis=0, keepdims=True)
    e = jnp.concatenate([mm(g, w).astype(bf16) for w in w_down], axis=1).reshape(keep_ref.shape)
    dm = mm_t(du, w_up).astype(bf16).reshape(keep_ref.shape)

    @pl.when(core_ref[0] == 0)
    def _():
        keep_ref[...] = e
        send_ref[...] = dm

    @pl.when(core_ref[0] != 0)
    def _():
        keep_ref[...] = dm
        send_ref[...] = e


def routed_grads_kernel(g_ref, d_ref, m_ref, du_ref, _, out_ref, done_ref):
    depth, all_rows, hidden = out_ref.shape
    rows = D // depth
    units = (all_rows - rows) // 2
    up = mm_rows(m_ref[...], du_ref[...]).astype(bf16)
    out_ref[:, :rows] = up.reshape(depth, rows, hidden)
    for k in range(2):
        down = mm_rows(g_ref[...], d_ref[:, k * hidden : (k + 1) * hidden]).astype(bf16)
        low = rows + k * units
        out_ref[:, low : low + units] = down.reshape(depth, units, hidden)
    done_ref[...] = jnp.zeros_like(done_ref)


def add_parts_kernel(a_ref, b_ref, *outs):
    outs[-1][...] = jnp.zeros_like(outs[-1])
    for j, out in enumerate(outs[:-1]):
        out[...] = (a_ref[j].astype(f32) + b_ref[j].astype(f32)).astype(bf16)


def add_kernel(*refs):
    refs[-1][...] = sum(ref[...].astype(f32) for ref in refs[:4]).astype(bf16)


def routed_back_kernel(count, core_ref, *refs):
    ins, outs = refs[:14], refs[14:]
    total, crossed, bias, z_ref, z_recv, chosen_ref, chosen_g, weight_ref, gain = ins[:9]
    wo_ref, wq_ref, qkv_ref, seg_col_ref, seg_row_ref = ins[9:]
    delta_ref, logit_ref, dh_ref, dz_ref, gain_g, dqkv_ref, da_ref, do_scr = outs
    first = core_ref[0] == 0
    a, b = total[...].astype(f32), crossed[...].astype(f32)
    e = jnp.where(first, a, b) + bias[...]
    dm = jnp.where(first, b, a)
    z = z_ref[...].astype(f32) + z_recv[...].astype(f32)
    delta = z + e
    delta_ref[...] = delta
    weight, grad = weight_ref[...], chosen_g[...].astype(f32)
    logit_ref[...] = jnp.sum(grad * delta, axis=1, keepdims=True) * weight * (1.0 - weight)
    h = chosen_ref[...].astype(f32) + z
    inverse = inverse_rms(h)
    unit = h * inverse
    gain_g[...] = jnp.sum(dm * unit, axis=0, keepdims=True)
    dh = norm_back(dm, unit, inverse, gain[...])
    dh_ref[...] = dh
    dz = (weight * grad + dh).astype(bf16)
    dz_ref[...] = dz
    do_scr[...] = mm_t(dz, wo_ref[...]).astype(bf16)
    attend_back_kernel(
        count, HALF // LANES, count, qkv_ref, seg_col_ref, seg_row_ref, do_scr, dqkv_ref
    )
    weights = wq_ref[:, :, :, : 3 * HALF].reshape(D, 3 * HALF)
    da_ref[...] = mm_t(dqkv_ref[...], weights).astype(bf16)


def put_rows(base, rows, picked, length):
    places = lax.broadcasted_iota(jnp.int32, (length, picked.shape[1]), 0) == picked
    onehot = places.astype(bf16)
    high = rows.astype(bf16)
    low = (rows - high.astype(f32)).astype(bf16)
    return base.astype(f32) + (mm(onehot, high) + mm(onehot, low))


def routed_out_kernel(
    part_ref, recv_ref, chosen_ref, gain, dh_ref, logit_ref, router, picked_ref, cot_ref, *outs
):
    gy_ref, gy_rows, gain_g, router_g = outs
    own = part_ref[...].astype(f32)
    da = own + recv_ref[...].astype(f32)
    chosen, logit = chosen_ref[...].astype(f32), logit_ref[...]
    inverse = inverse_rms(chosen)
    unit = chosen * inverse
    gain_g[...] = jnp.sum(own * unit, axis=0, keepdims=True)
    router_g[...] = jnp.sum(logit * chosen, axis=0, keepdims=True)
    rows = dh_ref[...] + norm_back(da, unit, inverse, gain[...]) + logit * router[...]
    micro, count = picked_ref.shape[0], picked_ref.shape[2]
    length = cot_ref.shape[0] // micro
    for s in range(micro):
        at = slice(s * length, (s + 1) * length)
        cut = rows[s * count : (s + 1) * count]
        gy = put_rows(cot_ref[at], cut, picked_ref[s], length).astype(bf16)
        gy_ref[at] = gy
        places = lax.broadcasted_iota(jnp.int32, (length, count), 0) == picked_ref[s]
        gy_rows[s * count : (s + 1) * count] = mm_rows(places.astype(bf16), gy).astype(bf16)


def routed_sum_kernel(y_ref, delta_ref, weight_ref, picked_ref, out_ref):
    rows = weight_ref[...] * delta_ref[...]
    micro, count = picked_ref.shape[0], picked_ref.shape[2]
    length = y_ref.shape[0] // micro
    for s in range(micro):
        at = slice(s * length, (s + 1) * length)
        cut = rows[s * count : (s + 1) * count]
        out_ref[at] = put_rows(y_ref[at], cut, picked_ref[s], length).astype(bf16)


def finish_kernel(core_ref, keep_ref, recv_ref, qkv_ref, out_ref):
    keep, recv = keep_ref[...].astype(f32), recv_ref[:, : 4 * HALF].astype(f32)
    first = core_ref[0] == 0
    low, high = jnp.where(first, keep, recv), jnp.where(first, recv, keep)
    for t in range(3):
        qkv_ref[:, t * D : t * D + HALF] = low[:, t * HALF : (t + 1) * HALF]
        qkv_ref[:, t * D + HALF : (t + 1) * D] = high[:, t * HALF : (t + 1) * HALF]
    out_ref[:, :HALF] = low[:, 3 * HALF : 4 * HALF]
    out_ref[:, HALF:] = high[:, 3 * HALF : 4 * HALF]


def shards(
    boundary_in,
    segments,
    routed,
    gain_attn,
    w_qkv,
    w_out,
    gain_mlp,
    w_up,
    b_up,
    w_down,
    b_down,
    router,
):
    core = lax.axis_index("section")
    first = core == 0
    me = 2 * lax.axis_index("y") + lax.axis_index("x")
    depth = lax.axis_size("z")
    rows = w_qkv.shape[1]
    dp = 4 * depth
    units = w_up.shape[2] // dp
    half_units = units // 2
    micro, length = boundary_in.shape[1], boundary_in.shape[3]
    tokens = micro * length

    up_halves = w_up[0].astype(bf16).reshape(rows, depth, 4, 2, half_units)
    down_halves = w_down[0].astype(bf16).reshape(2, half_units, D)
    bias_cols = half_units // rows
    bias_halves = b_up[0].astype(bf16).reshape(2, bias_cols, rows)
    column = lambda v: jnp.pad(v.astype(bf16), (0, rows - v.shape[0]))[:, None]
    small = jnp.concatenate(
        [column(gain_attn[0]), column(gain_mlp[0]), column(b_down[0]), column(router)], axis=1
    )

    def half(h):
        pick = lambda v, axis: lax.dynamic_index_in_dim(v, h, axis=axis, keepdims=False)
        strip = jnp.concatenate([small, pick(bias_halves, 0).T], axis=1)
        strip = jnp.pad(strip, ((0, 0), (0, 8 - strip.shape[1])))
        none = jnp.zeros_like(strip)
        strip = jnp.concatenate(
            [jnp.where(first, strip, none), jnp.where(first, none, strip)], axis=1
        )
        strip = jnp.pad(strip, ((0, 0), (0, LANES - 16)))
        up = pick(up_halves, 3).transpose(0, 2, 1, 3).reshape(rows, D * 2)
        return strip, up, pick(down_halves, 0)

    kept, sent = list(half(core)), list(half(1 - core))
    kept[0], sent[0] = whole(
        shard_kernel,
        [((rows, 4 * HALF + LANES), bf16)] * 2,
        [core],
        [w_qkv[0], w_out[0], kept[0], sent[0]],
    )
    came = tuple(swap(v, "section") for v in sent)
    width = 4 * HALF
    shard0 = [jnp.where(first, k, r) for k, r in zip(kept, came)]
    shard1 = [jnp.where(first, r, k) for k, r in zip(kept, came)]
    strip = kept[0][:, width:] + came[0][:, width:]
    shard0[0] = jnp.concatenate([shard0[0][:, :width], strip], axis=1)
    shard1[0] = shard1[0][:, :width]

    mine = boundary_in[0, :, 0].reshape(tokens, D)
    other = swap(mine, "section")
    x_b = jnp.where(first, mine, other)
    cot_b = jnp.where(first, other, mine)
    seg = segments[:, 0]
    picked = routed[:, 0]
    count = picked.shape[1]
    chosen_rows = micro * count

    def whole_out(w_o):
        w_o = w_o.reshape(D, HALF)
        own = lax.dynamic_slice_in_dim(w_o, core * HALF, HALF, axis=0)
        recv = swap(lax.dynamic_slice_in_dim(w_o, (1 - core) * HALF, HALF, axis=0), "section")
        return jnp.concatenate([jnp.where(first, own, recv), jnp.where(first, recv, own)], axis=1)

    halfway = depth // 2

    own_q = over_z(shard0[0])
    rest = [shard1[0]] + [to_plane(shard1[0], j) for j in (1, 2, 3)]
    (rest,) = whole(order_rows_kernel, [((4, rows, width), bf16)], [me], rest)
    hidden = depth * half_units
    pick_up = lambda j: lax.dynamic_slice_in_dim(shard1[1], (me ^ j) * hidden, hidden, axis=1)
    mlp = [pick_up(0)] + [to_plane(pick_up(j), j) for j in (1, 2, 3)]
    mlp_rows = 4 * rows + 2 * half_units
    (mlp,) = whole(order_mlp_kernel, [((mlp_rows, hidden), bf16)], [me], [*mlp, shard1[2]])
    onehot = picked[:, :, None] == lax.broadcasted_iota(jnp.int32, (micro, count, length), 2)
    seg1 = jnp.sum(jnp.where(onehot, seg[:, None, :], 0), axis=2)
    seg1_col, seg1_row = seg1[:, :, None], seg1[:, None, :]
    is_routed = jnp.any(onehot, axis=1).reshape(tokens, 1)
    cot_other = jnp.where(is_routed, jnp.zeros_like(cot_b), cot_b)
    own_q, rest, mlp, shard_u = fence(own_q, rest, mlp, shard0[1])

    px_q, py_q = swap(own_q, "x"), swap(own_q, "y")
    own_u = over_z(shard_u)
    own_q, px_q, py_q, own_u, shard_d, x_b, cot_b, cot_other, seg1_col, seg1_row = fence(
        own_q, px_q, py_q, own_u, shard0[2], x_b, cot_b, cot_other, seg1_col, seg1_row
    )
    pd_q, px_u = swap(px_q, "y"), swap(own_u, "x")
    own_d = over_z(shard_d)
    own_q, px_q, py_q, pd_q, own_u, px_u, own_d, rest = fence(
        own_q, px_q, py_q, pd_q, own_u, px_u, own_d, rest
    )
    py_u = swap(own_u, "y")
    px_d, py_d = swap(own_d, "x"), swap(own_d, "y")
    w_r1 = over_z(rest)

    spans_all = [(j, 0, depth) for j in range(4)]
    w_o0, strip = place(
        me, [own_q, px_q, py_q, pd_q], spans_all, ((3 * HALF, width), (width, width + LANES))
    )
    w_o0 = whole_out(w_o0)
    choose = (
        lax.broadcasted_iota(jnp.int32, (16, LANES), 0)
        == lax.broadcasted_iota(jnp.int32, (16, LANES), 1)
    ).astype(bf16)
    vectors = mm_t(choose, strip.reshape(D, LANES))
    gain_attn0, gain_mlp0, b_down0 = vectors[0:1], vectors[1:2], vectors[2:3]
    gain_attn1, gain_mlp1, b_down1 = vectors[8:9], vectors[9:10], vectors[10:11]
    router_full = jnp.concatenate(
        [vectors[b].reshape(dp, rows)[:, : rows // 2].reshape(1, HALF) for b in (3, 11)], axis=1
    )
    biases = lambda b: (
        vectors[b : b + bias_cols].reshape(bias_cols, depth, 4, rows).transpose(2, 1, 0, 3)
    )
    bias_up0 = biases(4).reshape(1, 2 * D)
    bias_up1 = lax.dynamic_index_in_dim(biases(12), me, axis=0, keepdims=False)
    bias_up1 = bias_up1.reshape(1, hidden)
    w_q0, a0, qkv0 = whole(
        functools.partial(qkv_kernel, spans_all, 256),
        [
            ((depth, 4, rows, 3 * HALF), bf16),
            ((tokens, D), bf16),
            ((tokens, 3 * HALF), bf16),
        ],
        [me],
        [x_b, gain_attn0, own_q, px_q, py_q, pd_q],
        [pltpu.SemaphoreType.DMA((4,))],
        anywhere=4,
    )
    w_q0 = w_q0.reshape(D, 3 * HALF)
    o0, z_part = attention_call(attend_out_kernel, seg, [qkv0], w_o0, HALF)
    o0, z_part, own_u, px_u, py_u, px_d, mlp = fence(o0, z_part, own_u, px_u, py_u, px_d, mlp)
    w_m1 = over_z(mlp)

    pd_u = swap(py_u, "x")
    pd_d0 = swap(px_d[:halfway], "y")
    h0, m0 = hidden_rows(x_b, z_part, swap(z_part, "section"), gain_mlp0)
    m0, pd_u, py_d, bias_up0, bias_up1, router_full = fence(
        m0, pd_u, py_d, bias_up0, bias_up1, router_full
    )

    pd_d1 = swap(py_d[halfway:], "x")
    (w_u0,) = place(me, [own_u, px_u, py_u, pd_u], spans_all, ((0, D * 2),))
    w_u0 = w_u0.reshape(D, D * 2)
    g0, slope0 = up_product(m0, w_u0, bias_up0)
    g0, pd_d0, pd_d1 = fence(g0, pd_d0, pd_d1)

    spans_cut = spans_all[:3] + [(3, 0, halfway), (3, halfway, depth)]
    (w_d0,) = place(
        me, [own_d, px_d, py_d, pd_d0, pd_d1], spans_cut, ((0, D),), plane_first=True
    )
    w_d0 = w_d0.reshape(D * 2, D)
    e_part, down_done = down_product(g0, w_d0)
    w_r1, down_done = fence(w_r1, down_done)
    w_o1 = whole_out(w_r1[..., 3 * HALF :])

    y0_b, chosen, grad_chosen, weight, de1, a1 = choose_rows(
        h0, e_part, swap(e_part, "section"), b_down0, cot_b, picked, router_full, gain_attn1
    )
    de_all = [de1] + [to_plane(de1, j) for j in (1, 2, 3)]
    qkv1, o1 = whole(
        functools.partial(routed_attn_kernel, count),
        [((chosen_rows, 3 * HALF), bf16), ((chosen_rows, HALF), bf16)],
        [],
        [a1, seg1_col, seg1_row, w_r1, down_done],
    )
    z_part = mm(o1, w_o1).astype(bf16)
    z_recv = swap(z_part, "section")
    (m1,) = whole(
        routed_hidden_kernel,
        [((chosen_rows, D), bf16)],
        [],
        [z_part, z_recv, chosen, gain_mlp1],
    )
    m_all = [m1] + [to_plane(m1, j) for j in (1, 2, 3)]
    pre_du, pre_dm, pre_done = mlp_pre(cot_other, w_d0, slope0, w_u0)
    g1, du1, keep, send, gb_u1, m_rows, de_rows = whole(
        routed_mlp_kernel,
        [((4 * chosen_rows, hidden), bf16)] * 2
        + [((4, chosen_rows, D), bf16)] * 2
        + [((1, hidden), f32)]
        + [((4 * chosen_rows, D), bf16)] * 2,
        [core],
        [*m_all, *de_all, w_m1, bias_up1, pre_done],
    )
    plus = lambda *terms: sum(t.astype(f32) for t in terms).astype(bf16)
    others = swap(send, "section")
    *summed, added = whole(
        add_parts_kernel, [((chosen_rows, D), bf16)] * 4 + [mark], [], [keep, others]
    )
    gw_m1, grads_done = whole(
        routed_grads_kernel,
        [((depth, mlp_rows, hidden), bf16), mark],
        [],
        [g1, de_rows, m_rows, du1, added],
    )
    plus = lambda *terms: sum(t.astype(f32) for t in terms).astype(bf16)
    r_m1 = reduce_z(gw_m1)
    terms = [summed[0]] + [to_plane(summed[j], j) for j in (1, 2, 3)]
    pre_d = down_grad(me, depth, (0, 1, 2, 3), g0, cot_other)
    g_rows, slope_rows, rows_done = take_rows(picked, pre_d[0], g0, slope0)
    (total,) = whole(add_kernel, [((chosen_rows, D), bf16)], [], [*terms, rows_done, grads_done])
    crossed = swap(total, "section")

    delta, grad_logit, dh1, dz1, gg_mlp1, dqkv1, da_part = whole(
        functools.partial(routed_back_kernel, count),
        [
            ((chosen_rows, D), f32),
            ((chosen_rows, 1), f32),
            ((chosen_rows, D), f32),
            ((chosen_rows, D), bf16),
            ((1, D), f32),
            ((chosen_rows, 3 * HALF), bf16),
            ((chosen_rows, D), bf16),
        ],
        [core],
        [
            total,
            crossed,
            b_down1,
            z_part,
            z_recv,
            chosen,
            grad_chosen,
            weight,
            gain_mlp1,
            w_o1,
            w_r1,
            qkv1,
            seg1_col,
            seg1_row,
        ],
        [pltpu.VMEM((chosen_rows, HALF), bf16)],
    )

    def out_by_columns(grad):
        own = lax.dynamic_slice_in_dim(grad, core * HALF, HALF, axis=1)
        recv = swap(lax.dynamic_slice_in_dim(grad, (1 - core) * HALF, HALF, axis=1), "section")
        return jnp.concatenate([jnp.where(first, own, recv), jnp.where(first, recv, own)], axis=0)

    gw_o1 = out_by_columns(mm_rows(o1, dz1).astype(bf16))
    gy0_b, gy_rows, gg_attn1, grad_router = whole(
        routed_out_kernel,
        [((tokens, D), bf16), ((chosen_rows, D), bf16), ((1, D), f32), ((1, D), f32)],
        [],
        [
            da_part,
            swap(da_part, "section"),
            chosen,
            gain_attn1,
            dh1,
            grad_logit,
            router_full,
            picked[:, None, :],
            cot_b,
        ],
    )
    send_diagonal = lambda grads: [swap(grads[3][0], "x"), swap(grads[3][1], "y")]
    send_far = lambda grads: [swap(grads[1][0], "x"), swap(grads[2][1], "y")]
    near = lambda grads, diag: [plus(grads[2][0], diag[0]), plus(grads[1][1], diag[1])]
    send_near = lambda sums: [swap(sums[0], "y"), swap(sums[1], "x")]
    parts = lambda grads, near, far: [
        v for h in range(2) for v in (grads[0][h], near[h], far[h])
    ]

    gw_d0 = down_rest(me, gy_rows, g_rows, pre_d)
    gw_d0, gy_rows = fence(gw_d0, gy_rows)
    diag_d, far_d = send_diagonal(gw_d0), send_far(gw_d0)
    attn1 = attn_grad(me, False, depth, a1, dqkv1, gw_o1, earlier=[gw_d0[0][0]])
    *gw_u0, dm_part, gb_u0 = up_rest(
        me,
        depth,
        picked[:, None, :],
        gy_rows,
        w_d0,
        slope_rows,
        pre_du,
        m0,
        w_u0,
        pre_dm,
        attn1,
    )
    r_a1 = reduce_z(attn1)
    diag_d, far_d, gw_u0, dm_part, gy0_b = fence(
        diag_d, far_d, pairs_of(gw_u0), dm_part, gy0_b
    )

    diag_u = send_diagonal(gw_u0)
    near_d = send_near(near(gw_d0, diag_d))
    dz0, gy_dh0, do0, gg_mlp0, g_down0 = norm_back_product(
        dm_part, swap(dm_part, "section"), h0, gain_mlp0, gy0_b, w_o0
    )
    dqkv0, da_part, gg_attn0 = attention_call(
        attend_back_out_kernel, seg, [qkv0, do0, x_b], w_q0, 3 * HALF, sums=1
    )
    diag_u, near_d, dqkv0, da_part, dz0 = fence(diag_u, near_d, dqkv0, da_part, dz0)
    gw_o0 = out_by_columns(mm_rows(o0, dz0).astype(bf16))
    (sum_d,) = whole(
        halves_kernel,
        [((depth, half_units, D), bf16)],
        [],
        parts(gw_d0, near_d, far_d),
    )
    r_d0 = reduce_z(sum_d)

    far_u = send_far(gw_u0)
    near_u = send_near(near(gw_u0, diag_u))
    here = lax.broadcasted_iota(jnp.int32, (depth, 4, bias_cols, rows), 1) == me
    gb_u1 = gb_u1.reshape(depth, 1, bias_cols, rows)
    gb_u1 = jnp.where(here, gb_u1, 0.0).transpose(2, 0, 1, 3).reshape(bias_cols, D)
    gb_u0 = gb_u0.reshape(4, depth, bias_cols, rows).transpose(2, 1, 0, 3).reshape(bias_cols, D)
    router_rows = jnp.pad(
        grad_router.reshape(2, dp, rows // 2), ((0, 0), (0, 0), (0, rows - rows // 2))
    ).reshape(2, D)
    g_down1 = jnp.sum(de1.astype(f32), axis=0, keepdims=True)
    blank = jnp.zeros((4 - bias_cols, D), f32)
    strip = jnp.concatenate(
        [gg_attn0, gg_mlp0, g_down0, router_rows[0:1], gb_u0, blank]
        + [gg_attn1, gg_mlp1, g_down1, router_rows[1:2], gb_u1, blank]
    )
    strip = jnp.pad(strip, ((0, LANES - 16), (0, 0))).T.astype(bf16)
    attn0 = attn_grad(me, True, depth, a0, dqkv0, gw_o0, strip)
    attn0, near_u, far_u, da_part = fence(attn0, near_u, far_u, da_part)

    diag_q, far_q = send_diagonal(attn0), send_far(attn0)
    (sum_u,) = whole(
        halves_kernel,
        [((depth, rows, 2 * D), bf16)],
        [],
        parts(gw_u0, near_u, far_u),
    )
    r_u0 = reduce_z(sum_u)
    dx0_b = last_rows(da_part, swap(da_part, "section"), x_b, gain_attn0, gy_dh0)
    (y1_b,) = whole(
        routed_sum_kernel,
        [((tokens, D), bf16)],
        [],
        [y0_b, delta, weight, picked[:, None, :]],
    )
    boundary_out = jnp.where(first, dx0_b, y1_b).reshape(1, micro, 1, length, D)
    diag_q, r_a1, r_m1 = fence(diag_q, r_a1, r_m1)

    near_q = send_near(near(attn0, diag_q))
    far_q, boundary_out = fence(far_q, boundary_out)
    part = lambda v, j: lax.dynamic_index_in_dim(v, me ^ j, axis=0, keepdims=False)
    def joined(grad0, grad1):
        keep = jnp.where(first, grad0, grad1)
        recv = swap(jnp.where(first, grad1, grad0), "section")
        return jnp.where(first, keep, recv).astype(f32), jnp.where(first, recv, keep).astype(f32)

    low = 4 * rows + half_units
    r_d1 = jnp.concatenate([r_m1[4 * rows : low], r_m1[low:]], axis=1)
    low, high = joined(r_d0, r_d1)
    out_down = jnp.concatenate([low, high], axis=0)[None]
    (sum_q,) = whole(
        halves_kernel,
        [((depth, rows, width + LANES), bf16)],
        [],
        parts(attn0, near_q, far_q),
    )
    sum_q, r_a1, r_m1, out_down = fence(sum_q, r_a1, r_m1, out_down)
    r_a0 = reduce_z(sum_q)
    r_a1 = plus(part(r_a1, 0), *[to_plane(part(r_a1, j), j) for j in (1, 2, 3)])
    up = r_m1[: 4 * rows].reshape(4, rows, hidden)
    up = [part(up, 0)] + [to_plane(part(up, j), j) for j in (1, 2, 3)]
    (r_u1,) = whole(order_columns_kernel, [((rows, 2 * D), bf16)], [me], up)
    low, high = joined(r_u0, r_u1)
    cut = lambda v: v.reshape(rows, 4, depth, half_units).transpose(0, 2, 1, 3)
    out_up = jnp.stack([cut(low), cut(high)], axis=3).reshape(1, rows, FF)
    r_a0, r_a1, out_up, out_down, boundary_out = fence(r_a0, r_a1, out_up, out_down, boundary_out)
    strip = r_a0[:, width:]
    strip_mine = jnp.where(first, strip[:, :8], strip[:, 8:16])
    strip_other = jnp.where(first, strip[:, 8:16], strip[:, :8])
    keep = jnp.where(first, r_a0[:, :width], r_a1)
    send = jnp.where(first, r_a1, r_a0[:, :width])
    pad = lambda v: jnp.pad(v, ((0, 0), (0, LANES - 8)))
    recv = swap(jnp.concatenate([send, pad(strip_other)], axis=1), "section")
    out_qkv, out_out = whole(
        finish_kernel,
        [((rows, 3 * D), f32), ((rows, D), f32)],
        [core],
        [keep, recv],
    )
    small = strip_mine.astype(f32).T
    gain = small[0:1] + recv[:, width : width + 1].astype(f32).T
    bias_half = small[4 : 4 + bias_cols]
    bias_other = recv[:, width + 4 : width + 4 + bias_cols].astype(f32).T
    out_b_up = jnp.concatenate(
        [jnp.where(first, bias_half, bias_other), jnp.where(first, bias_other, bias_half)]
    ).reshape(1, units)
    return (
        boundary_out,
        gain,
        out_qkv[None],
        out_out[None],
        small[1:2],
        out_up,
        out_b_up,
        out_down,
        small[2:3],
        small[3, : rows // 2],
    )


def solution(mesh):
    sections, dp = mesh.shape["section"], mesh.shape["dp"]
    grid = Mesh(mesh.devices.reshape(sections, dp // 4, 2, 2), ("section", "z", "y", "x"))
    chips = ("z", "y", "x")
    in_specs = (
        P("section", None, chips, None, None),
        P(None, chips, None),
        P(None, chips, None),
        P("section", chips),
        P("section", chips, None),
        P("section", chips, None),
        P("section", chips),
        P("section", chips, None),
        P("section", chips),
        P("section", chips, None),
        P("section", chips),
        P(("section",) + chips),
    )
    out_specs = (
        P("section", None, chips, None, None),
        P("section", chips),
        P("section", chips, None),
        P("section", chips, None),
        P("section", chips),
        P("section", chips, None),
        P("section", chips),
        P("section", chips, None),
        P("section", chips),
        P(("section",) + chips),
    )
    return jax.shard_map(shards, mesh=grid, in_specs=in_specs, out_specs=out_specs, check_vma=False)
```
